32 devices in a mesh: stn: 2 (over x), tm: 16 (over z, y, core).
Axes of the slice: x: 2, y: 2, z: 4, core: 2. Of those that a mesh axis runs over, the one named last changes fastest.
Arguments:
- spectra: bfloat16 [16, 8, 64, 2, 4096], P('stn', None, 'tm'), may hold values from -6 to 6
- flags: int32 [16, 8, 64, 32], P('stn', None, 'tm'), may hold values from 0 to 1, as said below
- poly_index: int32 [16, 8, 64], P('stn', None, 'tm'), may hold values from 0 to 63
- delay_model: float32 [64, 3], replicated, may hold values from -48 to 48
- partner_order: int32 [16], replicated, may hold values from 0 to 15, each once
Outputs:
- fringe: float32 [2, 256, 8, 256], P(None, ('stn', 'tm'))
The draws below stay inside these ranges and needn't reach their ends.
Inputs may be any that keep to these rules, and one draw needn't show every extreme that they name: `flags`: 1 marks a flagged block; whole blocks of a station can be flagged for the full window. `partner_order`: each station appears once.
All inputs are finite; a program needn't handle non-finite values.
Results may differ from the reference program's by a relative error of at most 0.003.
Values may be sent and summed in bfloat16 or wider, within the bound.
A program may use at most 128 MiB of HBM per device.

```python
import math
import jax
import jax.numpy as jnp
from jax import lax

S = 16
C = 4096
P_SIZE = 8
LAGS = 256
NPOLY = 64
SPP = 64
CB = 32


def model_rows(key):
    sign_key = jax.random.fold_in(key, 11)
    size_key = jax.random.fold_in(key, 12)
    mixed_key = jax.random.fold_in(key, 13)
    pick_key = jax.random.fold_in(key, 14)
    signs = jnp.where(jax.random.randint(sign_key, (NPOLY, 1), 0, 2) == 0, -1.0, 1.0).astype(jnp.float32)
    aligned = signs * jax.random.uniform(size_key, (NPOLY, 3), jnp.float32, 16.0, 48.0)
    mixed = jax.random.uniform(mixed_key, (NPOLY, 3), jnp.float32, -48.0, 48.0)
    picked = jax.random.randint(pick_key, (NPOLY, 1), 0, 4) == 0
    return jnp.where(picked, mixed, aligned)


def index_rows(key):
    return jax.random.randint(jax.random.fold_in(key, 21), (S, P_SIZE, SPP), 0, NPOLY).astype(jnp.int32)


def draw_delay_model(key, part):
    return model_rows(key)


def draw_poly_index(key, part):
    return index_rows(key)


def draw_spectra(key, part):
    model = model_rows(key)
    index = index_rows(key)
    coeffs = model[index]
    times = (jnp.arange(P_SIZE, dtype=jnp.int32)[:, None] * SPP + jnp.arange(SPP, dtype=jnp.int32)[None, :]).astype(jnp.float32)
    moment = times / float(P_SIZE * SPP)
    delay = coeffs[..., 0] + coeffs[..., 1] * moment + coeffs[..., 2] * moment * moment
    common = jnp.clip(jax.random.normal(jax.random.fold_in(key, 31), (2, P_SIZE, SPP, C), jnp.float32), -4.5, 4.5)
    offsets = jax.random.randint(jax.random.fold_in(key, 41), (S,), -(C // 6), C // 6 + 1).astype(jnp.int32)
    channel = jnp.arange(C, dtype=jnp.int32)
    freq = channel.astype(jnp.float32) * (math.pi / C)
    gains = jnp.ones((S,), jnp.float32)
    strength = 0.5
    noise_base = jax.random.fold_in(key, 51)

    def one_station(items):
        station, station_delay, offset, gain = items
        noise_key = jax.random.fold_in(noise_base, station)
        noise = jnp.clip(jax.random.normal(noise_key, (P_SIZE, SPP, 2, C), jnp.float32), -4.5, 4.5)
        turns = channel * offset % C
        angle = station_delay[..., None] * freq - turns.astype(jnp.float32) * (2.0 * math.pi / C)
        cosine = jnp.cos(angle)
        sine = jnp.sin(angle)
        real = strength * (common[0] * cosine - common[1] * sine)
        imag = strength * (common[0] * sine + common[1] * cosine)
        signal = jnp.stack([real, imag], axis=2)
        return jnp.clip(gain * noise + signal, -6.0, 6.0)
    stations = lax.map(one_station, (jnp.arange(S, dtype=jnp.int32), delay, offsets, gains))
    return stations.astype(jnp.bfloat16)


def draw_flags(key, part):
    sample_key = jax.random.fold_in(key, 101)
    whole_key = jax.random.fold_in(key, 202)
    shared_key = jax.random.fold_in(key, 303)
    sample = jax.random.randint(sample_key, (S, P_SIZE, SPP, CB), 0, 8) == 0
    whole = jax.random.randint(whole_key, (S, 1, 1, CB), 0, 16) == 0
    shared = jax.random.randint(shared_key, (1, P_SIZE, SPP, CB), 0, 3) == 0
    return jnp.logical_or(jnp.logical_or(sample, whole), shared).astype(jnp.int32)


def setup_inputs(seed: int = 0) -> dict:
    key_of = jax.random.split(jax.random.key(seed), 6)
    return {
        "spectra": draw_spectra(jax.random.fold_in(key_of[5], 71), 0),
        "flags": draw_flags(jax.random.fold_in(key_of[5], 71), 0),
        "poly_index": draw_poly_index(jax.random.fold_in(key_of[5], 71), 0),
        "delay_model": draw_delay_model(jax.random.fold_in(key_of[5], 71), 0),
        "partner_order": jax.random.permutation(key_of[4], S).astype(jnp.int32),
    }


def rotate(spectra, flags, coeffs, times, total_time):
    channels = spectra.shape[-1]
    blocks = flags.shape[-1]
    moment = times / total_time
    delay = coeffs[..., 0] + coeffs[..., 1] * moment + coeffs[..., 2] * moment * moment
    freq = jnp.arange(channels, dtype=jnp.int32).astype(jnp.float32) * (math.pi / channels)
    phase = delay[..., None] * freq
    cosine = jnp.cos(phase)
    sine = jnp.sin(phase)
    real = spectra[..., 0, :].astype(jnp.float32)
    imag = spectra[..., 1, :].astype(jnp.float32)
    weight = 1.0 - flags.astype(jnp.float32)
    weight = jnp.broadcast_to(weight[..., None], weight.shape + (channels // blocks,)).reshape(real.shape)
    new_real = weight * (real * cosine + imag * sine)
    new_imag = weight * (imag * cosine - real * sine)
    return jnp.stack([new_real, new_imag], axis=-2).astype(jnp.bfloat16)

def transform(vis, counts, lags):
    rows, periods, _, channels = vis.shape
    blocks = counts.shape[-1]
    scale = 1.0 / jnp.sqrt(jnp.maximum(counts, 1.0))
    normed = vis.reshape(rows, periods, 2, blocks, channels // blocks) * scale[:, :, None, :, None]
    normed = normed.reshape(rows, periods, 2, channels)
    index = jnp.arange(lags, dtype=jnp.int32)
    middle = lags // 2
    delays = jnp.where(index < middle, index - middle, index - middle + 1)
    turns = jnp.arange(channels, dtype=jnp.int32)[:, None] * delays[None, :] % channels
    angle = turns.astype(jnp.float32) * (2.0 * math.pi / channels)
    cosine = jnp.cos(angle)
    sine = jnp.sin(angle)
    highest = lax.Precision.HIGHEST
    real = normed[:, :, 0].reshape(rows * periods, channels)
    imag = normed[:, :, 1].reshape(rows * periods, channels)
    part_real = jnp.dot(real, cosine, precision=highest) + jnp.dot(imag, sine, precision=highest)
    part_imag = jnp.dot(imag, cosine, precision=highest) - jnp.dot(real, sine, precision=highest)
    part_real = part_real.reshape(rows, periods, lags)
    part_imag = part_imag.reshape(rows, periods, lags)
    pidx = jnp.arange(periods, dtype=jnp.int32)
    pturn = pidx[:, None] * pidx[None, :] % periods
    pangle = pturn.astype(jnp.float32) * (2.0 * math.pi / periods)
    pcos = jnp.cos(pangle)
    psin = jnp.sin(pangle)
    out_real = jnp.einsum('rp,npl->nrl', pcos, part_real, precision=highest) + jnp.einsum('rp,npl->nrl', psin, part_imag, precision=highest)
    out_imag = jnp.einsum('rp,npl->nrl', pcos, part_imag, precision=highest) - jnp.einsum('rp,npl->nrl', psin, part_real, precision=highest)
    factor = 1.0 / math.sqrt(periods * channels)
    return jnp.stack([out_real, out_imag]) * factor

def reference(spectra, flags, poly_index, delay_model, partner_order):
    stations, periods, depth, _, channels = spectra.shape
    times = (jnp.arange(periods, dtype=jnp.int32)[:, None] * depth + jnp.arange(depth, dtype=jnp.int32)[None, :]).astype(jnp.float32)
    total_time = float(periods * depth)

    def one_station(items):
        spectrum, flag, index = items
        coeffs = delay_model[index]
        return rotate(spectrum[None], flag[None], coeffs[None], times, total_time)[0]
    rotated = lax.map(one_station, (spectra, flags, poly_index))
    wide = rotated.astype(jnp.float32)

    def one_row(mine):
        product = jnp.einsum('pkxc,bpkyc->bpxyc', mine.astype(jnp.float32), wide)
        real = product[:, :, 0, 0] + product[:, :, 1, 1]
        imag = product[:, :, 1, 0] - product[:, :, 0, 1]
        return jnp.stack([real, imag], axis=2)
    vis = lax.map(one_row, rotated)
    weight = 1.0 - flags.astype(jnp.float32)
    counts = jnp.einsum('apkx,bpkx->abpx', weight, weight, precision=lax.Precision.HIGHEST)
    vis = jnp.take(vis, partner_order, axis=1).reshape(stations * stations, periods, 2, channels)
    counts = jnp.take(counts, partner_order, axis=1).reshape(stations * stations, periods, counts.shape[-1])
    return transform(vis, counts, LAGS)
```

```python
import functools
import math

import jax
import jax.numpy as jnp
import numpy as np
from jax import lax
from jax.experimental import pallas as pl
from jax.experimental.pallas import tpu as pltpu
from jax.sharding import PartitionSpec as P

LAGS = 256
QUARTERS = 4
LANES = 128
SUB = 8
TILE = 4
MESH = pl.DeviceIdType.MESH


def lag_tables(channels):
    lags = np.arange(1, LAGS // 2 + 1)
    j = np.arange(channels // QUARTERS)
    angle = (j[:, None] * lags[None, :] % channels) * (2.0 * np.pi / channels)
    table = np.concatenate([np.cos(angle), np.sin(angle)], axis=1).astype(np.float32)
    high = table.astype(jnp.bfloat16)
    low = (table - high.astype(np.float32)).astype(jnp.bfloat16)
    return high, low


def pair_rows(stations):
    tiles = stations // TILE
    off = [(x * TILE, y * TILE) for x in range(tiles) for y in range(x + 1, tiles)]
    real, imag = {}, {}
    for x, y in off:
        for i in range(TILE):
            for j in range(TILE):
                real[x + i, y + j] = len(real)
    for x in range(tiles):
        for i in range(TILE):
            for j in range(i, TILE):
                real[x * TILE + i, x * TILE + j] = len(real)
    top = len(real)
    for x, y in off:
        for i in range(TILE):
            for j in range(TILE):
                imag[x + i, y + j] = top + len(imag)
    for x in range(tiles):
        for i in range(TILE):
            for j in range(i + 1, TILE):
                imag[x * TILE + i, x * TILE + j] = top + len(imag)
    return off, real, imag


def pick_matrix(stations, groups, owners):
    _, real, imag = pair_rows(stations)
    split = owners // stations
    wide = groups * split
    local = stations // groups
    span = stations // split
    pick = np.zeros((owners, 2, span, stations * stations), np.float32)
    for t in range(owners):
        a = t % wide // split * local + t // wide
        for n in range(span):
            b = t % split * span + n
            key = (min(a, b), max(a, b))
            pick[t, 0, n, real[key]] = 1.0
            if a != b:
                pick[t, 1, n, imag[key]] = 1.0 if a < b else -1.0
    return pick.reshape(owners * 2 * span, stations * stations).astype(jnp.bfloat16)


def period_tables(periods, rows):
    idx = np.arange(periods)
    angle = (idx[:, None] * idx[None, :] % periods) * (2.0 * np.pi / periods)
    eye = np.eye(rows)

    def table(m):
        wide = np.einsum("rp,nm->nrpm", m, eye).reshape(rows * periods, periods * rows)
        return jnp.asarray(wide.astype(np.float32))

    return table(np.cos(angle)), table(np.sin(angle))


def dot(a, b):
    return jnp.dot(a, b, preferred_element_type=jnp.float32)


SIN = [(-1) ** n * math.pi ** (2 * n + 1) / math.factorial(2 * n + 1) for n in range(6)]
COS = [(-1) ** n * math.pi ** (2 * n) / math.factorial(2 * n) for n in range(7)]


def cos_sin_turns(turns):
    frac = turns - jnp.floor(turns + 0.5)
    square = frac * frac
    s = jnp.full_like(square, SIN[-1])
    for coef in SIN[-2::-1]:
        s = s * square + coef
    s = s * frac
    c = jnp.full_like(square, COS[-1])
    for coef in COS[-2::-1]:
        c = c * square + coef
    return 1.0 - 2.0 * (s * s), 2.0 * (s * c)


def kernel(
    sizes,
    x_hbm, w_ref, d_ref, partner_ref, high_hbm, low_hbm, pick_hbm, pcos_ref, psin_ref,
    out_ref,
    xall, wbuf, dbuf, wall, wf, wrow, cnt, scale_t, wide_w, wide_s, dsplat,
    th, tl, pick, wh, wl, ct, st, tmp, yr, yi, v_ref, vh, vl, z_ref,
    zs, rb, red, fs, fr, gf,
    table_sem, own_sem, xs_sem, xr_sem, ws_sem, wr_sem, gs_sem, gr_sem, rs_sem, rr_sem, fs_sem, fr_sem,
):
    groups, owners, stations, periods, depth, blocks = sizes
    local = stations // groups
    mine = periods // groups
    split = owners // stations
    wide = groups * split
    span = stations // split
    own_rows = stations // wide
    rows = stations * stations
    steps = mine * QUARTERS
    lags = LAGS // 2
    me = lax.axis_index("stn")
    t = lax.axis_index("tm")
    home = t // wide
    place = t % wide
    plane = place // split
    part = t % split

    def own_copy(i):
        rows_i = pl.ds(pl.multiple_of((i % QUARTERS) * 2 * SUB, 2 * SUB), 2 * SUB)
        return pltpu.make_async_copy(
            x_hbm.at[:, me * mine + i // QUARTERS, :, rows_i, :],
            xall.at[pl.ds(me * local, local), i // QUARTERS, :, rows_i, :],
            own_sem.at[i],
        )

    tables = [
        pltpu.make_async_copy(high_hbm, th, table_sem.at[0]),
        pltpu.make_async_copy(low_hbm, tl, table_sem.at[1]),
        pltpu.make_async_copy(pick_hbm, pick, table_sem.at[2]),
        pltpu.make_async_copy(w_ref.at[me], wbuf.at[me], table_sem.at[3]),
        pltpu.make_async_copy(d_ref.at[me], dbuf.at[me], table_sem.at[4]),
    ]

    barrier = pltpu.get_barrier_semaphore()
    for shift in range(1, groups):
        for w in range(wide):
            peer = {"stn": lax.rem(me + shift, groups), "tm": home * wide + lax.rem(place + w, wide)}
            pl.semaphore_signal(barrier, inc=1, device_id=peer, device_id_type=MESH)
    for shift in range(1, owners):
        pl.semaphore_signal(barrier, inc=1, device_id={"tm": lax.rem(t + shift, owners)}, device_id_type=MESH)
    for copy in tables:
        copy.start()

    def start_own(i, _):
        own_copy(i).start()
        return 0

    lax.fori_loop(0, steps, start_own, 0)
    pl.semaphore_wait(barrier, (groups - 1) * wide + owners - 1)

    def small_copies(shift, source):
        target = lax.rem(me + shift, groups)
        return [
            pltpu.make_async_remote_copy(
                src_ref=ref.at[target], dst_ref=buf.at[source], send_sem=ws_sem.at[n, shift],
                recv_sem=wr_sem.at[n, source], device_id={"stn": target}, device_id_type=MESH,
            )
            for n, (ref, buf) in enumerate(((w_ref, wbuf), (d_ref, dbuf)))
        ]

    def spectra_copy(shift, source, i):
        target = lax.rem(me + shift, groups)
        rows_i = pl.ds(pl.multiple_of((i % QUARTERS) * 2 * SUB, 2 * SUB), 2 * SUB)
        return pltpu.make_async_remote_copy(
            src_ref=x_hbm.at[:, target * mine + i // QUARTERS, :, rows_i, :],
            dst_ref=xall.at[pl.ds(source * local, local), i // QUARTERS, :, rows_i, :],
            send_sem=xs_sem.at[shift, i], recv_sem=xr_sem.at[source, i],
            device_id={"stn": target}, device_id_type=MESH,
        )

    for shift in range(1, groups):
        for copy in small_copies(shift, me):
            copy.start()

    def start_spectra(i, _):
        for shift in range(1, groups):
            spectra_copy(shift, me, i).start()
        return 0

    lax.fori_loop(0, steps, start_spectra, 0)

    for copy in tables[3:]:
        copy.wait()
    for shift in range(1, groups):
        for copy in small_copies(shift, lax.rem(me + groups - shift, groups)):
            copy.wait_recv()

    def gather_copy(shift, source):
        return pltpu.make_async_remote_copy(
            src_ref=wbuf, dst_ref=wall.at[source], send_sem=gs_sem.at[shift], recv_sem=gr_sem.at[source],
            device_id={"tm": lax.rem(t + shift, owners)}, device_id_type=MESH,
        )

    for shift in range(1, owners):
        gather_copy(shift, t).start()
    wall[t] = wbuf[...]

    for copy in tables[:3]:
        copy.wait()
    lag = lax.broadcasted_iota(jnp.int32, (1, lags), 1) + 1
    for quarter in range(QUARTERS):
        turn = (lag * quarter) % 4
        cq = jnp.where(turn == 0, 1.0, jnp.where(turn == 2, -1.0, 0.0))
        sq = jnp.where(turn == 1, 1.0, jnp.where(turn == 3, -1.0, 0.0))

        def turn_rows(n, _, quarter=quarter, cq=cq, sq=sq):
            r = pl.ds(pl.multiple_of(n * LANES, LANES), LANES)
            for source, target in ((th, wh), (tl, wl)):
                c = source[r, :lags].astype(jnp.float32)
                s = source[r, lags:].astype(jnp.float32)
                target[quarter, r, :lags] = (c * cq - s * sq).astype(jnp.bfloat16)
                target[quarter, r, lags:] = (s * cq + c * sq).astype(jnp.bfloat16)
            return 0

        lax.fori_loop(0, th.shape[0] // LANES, turn_rows, 0)

    for g in range(groups):
        for l in range(local):
            wrow[(g * local + l) * depth : (g * local + l + 1) * depth, :] = wbuf[g, l].astype(jnp.float32)
        d = dbuf[g]
        for p in range(mine):
            dsplat[p, g * local * depth : (g + 1) * local * depth, :] = jnp.broadcast_to(d[:, p : p + 1], d.shape)
    w_t = wrow[...].T
    for r in range(stations * depth):
        wide_w[r] = jnp.broadcast_to(w_t[:, r : r + 1], (w_t.shape[0], LANES))

    for shift in range(1, owners):
        gather_copy(shift, lax.rem(t + owners - shift, owners)).wait_recv()

    def widen(n, _):
        for g in range(groups):
            for l in range(local):
                wf[g * local + l, n] = wall[n, g, l].astype(jnp.float32)
        return 0

    lax.fori_loop(0, owners, widen, 0)
    off, real_row, imag_row = pair_rows(stations)
    for a in range(stations):
        for b0 in range(a // TILE * TILE, stations, TILE):
            b = max(a, b0)
            count = b0 + TILE - b
            product = jnp.sum(wf[a][None] * wf[b : b + count], axis=1)
            cnt[real_row[a, b] : real_row[a, b] + count, :] = jnp.sum(product, axis=1)
    pairs = len(real_row)
    pad = cnt.shape[0]
    scale_t[...] = (1.0 / jnp.sqrt(jnp.maximum(cnt[...], 1.0))).T
    for m in range(pairs):
        wide_s[m] = jnp.broadcast_to(scale_t[:, m : m + 1], (scale_t.shape[0], LANES))

    channel = (
        lax.broadcasted_iota(jnp.int32, (SUB, LANES), 0) * LANES + lax.broadcasted_iota(jnp.int32, (SUB, LANES), 1)
    ).astype(jnp.float32)
    v_flat = v_ref.reshape(rows * SUB, LANES)

    def scatter_copy(p, shift, target, source):
        return pltpu.make_async_remote_copy(
            src_ref=zs.at[p, target], dst_ref=rb.at[p, source], send_sem=rs_sem.at[p, shift],
            recv_sem=rr_sem.at[p, source], device_id={"tm": lax.rem(t + shift, owners)}, device_id_type=MESH,
        )

    def final_copy(p, w, source, piece):
        return pltpu.make_async_remote_copy(
            src_ref=fs.at[p, w], dst_ref=fr.at[source, piece, p], send_sem=fs_sem.at[p, w],
            recv_sem=fr_sem.at[source, piece, p], device_id={"stn": plane, "tm": home * wide + w}, device_id_type=MESH,
        )

    def reduce_period(p):
        total = zs[p, t].astype(jnp.float32)
        for shift in range(1, owners):
            source = lax.rem(t + owners - shift, owners)
            scatter_copy(p, shift, t, source).wait_recv()
        for shift in range(1, owners):
            total = total + rb[p, lax.rem(t + owners - shift, owners)].astype(jnp.float32)
        red[...] = total.reshape(red.shape)
        for w in range(wide):
            for n in range(own_rows):
                b = partner_ref[w * own_rows + n]
                if split > 1:
                    keep = jnp.where(b // span == part, 1.0, 0.0)
                    b = b % span
                for ri in range(2):
                    row = red[ri, pl.ds(b, 1), :]
                    fs[p, w, ri, n : n + 1, :] = row * keep if split > 1 else row
        for w in range(wide):
            to_self = (plane == me) & (w == place)

            @pl.when(to_self)
            def _():
                fr[me, part, p] = fs[p, w]

            @pl.when(jnp.logical_not(to_self))
            def _():
                final_copy(p, w, me, part).start()

    def step(i, _):
        p = i // QUARTERS
        quarter = i % QUARTERS
        at = pl.ds(pl.multiple_of(p * blocks + quarter * SUB, SUB), SUB)
        index = channel + (quarter * (SUB * LANES)).astype(jnp.float32)

        def turn_tables(r, _):
            c, s = cos_sin_turns(dsplat[p, pl.ds(r, 1), :] * index)
            w = wide_w[r, at, :]
            ct[r] = c * w
            st[r] = s * w
            return 0

        lax.fori_loop(0, stations * depth, turn_tables, 0, unroll=4)

        own_copy(i).wait()
        for shift in range(1, groups):
            spectra_copy(shift, lax.rem(me + groups - shift, groups), i).wait_recv()

        rows_i = pl.ds(pl.multiple_of(quarter * 2 * SUB, 2 * SUB), 2 * SUB)

        def rotate(s, _):
            for k in range(depth):
                tmp[k] = xall[s, p, k, rows_i, :].astype(jnp.float32)
                real = tmp[k, pl.ds(0, SUB, stride=2), :]
                imag = tmp[k, pl.ds(1, SUB, stride=2), :]
                c = ct[s * depth + k]
                sn = st[s * depth + k]
                yr[k, s] = (real * c + imag * sn).astype(jnp.bfloat16).astype(jnp.float32)
                yi[k, s] = (imag * c - real * sn).astype(jnp.bfloat16).astype(jnp.float32)
            return 0

        lax.fori_loop(0, stations, rotate, 0)

        for x, y in off:
            real = None
            for k in range(depth):
                ar, ai = yr[k, x : x + TILE][:, None], yi[k, x : x + TILE][:, None]
                br, bi = yr[k, y : y + TILE][None], yi[k, y : y + TILE][None]
                re = ar * br + ai * bi
                im = ai * br - ar * bi
                real = re if real is None else real + re
                imag = im if k == 0 else imag + im
            n = TILE * TILE
            m = real_row[x, y]
            q = imag_row[x, y]
            scale = wide_s[m : m + n, at, :]
            v_ref[m : m + n] = real.reshape(n, SUB, LANES) * scale
            v_ref[q : q + n] = imag.reshape(n, SUB, LANES) * scale
        for x in range(0, stations, TILE):
            for i0 in range(TILE):
                n = TILE - i0
                a = x + i0
                for k in range(depth):
                    ar, ai = yr[k, a : a + 1], yi[k, a : a + 1]
                    br, bi = yr[k, a : a + n], yi[k, a : a + n]
                    re = ar * br + ai * bi
                    real = re if k == 0 else real + re
                    if n > 1:
                        im = ai * br[1:] - ar * bi[1:]
                        imag = im if k == 0 else imag + im
                m = real_row[a, a]
                scale = wide_s[m : m + n, at, :]
                v_ref[m : m + n] = real * scale
                if n > 1:
                    q = imag_row[a, a + 1]
                    v_ref[q : q + n - 1] = imag * scale[1:]

        for b in range(SUB):
            v = v_flat[pl.ds(b, rows, stride=SUB), :]
            high = v.astype(jnp.bfloat16)
            cols = slice(b * LANES, (b + 1) * LANES)
            vh[:, cols] = high
            vl[:, cols] = (v - high.astype(jnp.float32)).astype(jnp.bfloat16)
        values = dot(vh[...], wh[quarter]) + dot(vh[...], wl[quarter]) + dot(vl[...], wh[quarter])

        @pl.when(quarter == 0)
        def _():
            z_ref[...] = values

        @pl.when(quarter > 0)
        def _():
            z_ref[...] += values

        @pl.when(quarter == QUARTERS - 1)
        def _():
            picked = dot(pick[...], z_ref[...].astype(jnp.bfloat16)).astype(jnp.bfloat16)
            zs[p] = picked.reshape(zs.shape[1:])
            for shift in range(1, owners):
                scatter_copy(p, shift, lax.rem(t + shift, owners), t).start()

        @pl.when((quarter == QUARTERS - 1) & (p > 0))
        def _():
            reduce_period(p - 1)

        return 0

    lax.fori_loop(0, steps, step, 0)
    reduce_period(mine - 1)

    for p in range(mine):
        for g in range(groups):
            for h in range(split):
                from_self = (me == g) & (place == me * split + h)

                @pl.when(jnp.logical_not(from_self))
                def _():
                    final_copy(p, 0, g, h).wait_recv()

    for g in range(groups):
        for p in range(mine):
            value = fr[g, 0, p]
            for h in range(1, split):
                value = value + fr[g, h, p]
            r = (g * mine + p) * own_rows
            gf[:, r : r + own_rows, :] = value

    highest = lax.Precision.HIGHEST
    rc, rs = gf[0, :, :lags], gf[0, :, lags:]
    ic, im_s = gf[1, :, :lags], gf[1, :, lags:]
    flip = (
        lax.broadcasted_iota(jnp.int32, (lags, lags), 0) + lax.broadcasted_iota(jnp.int32, (lags, lags), 1) == lags - 1
    ).astype(jnp.float32)
    pcos = pcos_ref[...]
    psin = psin_ref[...]
    factor = 1.0 / math.sqrt(periods * blocks * LANES)

    def mix(m, v):
        return jnp.dot(m, v, precision=highest, preferred_element_type=jnp.float32)

    for side in range(2):
        if side == 0:
            real, imag = mix(rc - im_s, flip), mix(ic + rs, flip)
        else:
            real, imag = rc + im_s, ic - rs
        cols = slice(side * lags, (side + 1) * lags)
        out_ref[0, :, cols] = (mix(pcos, real) + mix(psin, imag)) * factor
        out_ref[1, :, cols] = (mix(pcos, imag) - mix(psin, real)) * factor

    for shift in range(1, groups):
        for copy in small_copies(shift, me):
            copy.wait_send()
    for shift in range(1, owners):
        gather_copy(shift, t).wait_send()

    def sent(i, _):
        for shift in range(1, groups):
            spectra_copy(shift, me, i).wait_send()
        return 0

    lax.fori_loop(0, steps, sent, 0)

    def scattered(p, _):
        for shift in range(1, owners):
            scatter_copy(p, shift, lax.rem(t + shift, owners), t).wait_send()
        for w in range(wide):
            @pl.when(jnp.logical_not((plane == me) & (w == place)))
            def _():
                final_copy(p, w, me, part).wait_send()
        return 0

    lax.fori_loop(0, mine, scattered, 0)


def per_device(spectra, flags, poly_index, delay_model, partner_order):
    local, periods, depth, _, channels = spectra.shape
    groups = lax.axis_size("stn")
    owners = lax.axis_size("tm")
    me = lax.axis_index("stn")
    stations = local * groups
    mine = periods // groups
    blocks = flags.shape[-1]
    split = owners // stations
    wide = groups * split
    own_rows = stations // wide
    span = stations // split
    rows = stations * stations
    steps = mine * QUARTERS
    width = channels // QUARTERS
    assert channels == blocks * LANES and width == SUB * LANES and stations % TILE == 0

    x = spectra.reshape(local, periods, depth, 2, blocks, LANES).transpose(0, 1, 2, 4, 3, 5)
    x = x.reshape(local, periods, depth, 2 * blocks, LANES)

    lanes = -(-mine * blocks // LANES) * LANES
    w = (1.0 - flags.astype(jnp.float32)).astype(jnp.bfloat16)
    w = w.reshape(local, groups, mine, depth, blocks).transpose(1, 0, 3, 2, 4).reshape(groups, local, depth, mine * blocks)
    w = jnp.pad(w, ((0, 0), (0, 0), (0, 0), (0, lanes - mine * blocks)))

    total = depth * owners
    times = (
        jnp.arange(periods, dtype=jnp.int32)[:, None] * total
        + lax.axis_index("tm") * depth
        + jnp.arange(depth, dtype=jnp.int32)[None, :]
    ).astype(jnp.float32)
    moment = times / float(periods * total)
    table_rows = delay_model.shape[0]
    onehot = poly_index[..., None] == jnp.arange(table_rows, dtype=jnp.int32)
    coef = [jnp.sum(jnp.where(onehot, delay_model[:, n], 0.0), axis=-1) for n in range(3)]
    delay = (coef[0] + coef[1] * moment + coef[2] * moment * moment) * (0.5 / channels)
    d = delay.reshape(local, groups, mine, depth).transpose(1, 0, 3, 2).reshape(groups, local * depth, mine)
    d = jnp.pad(d, ((0, 0), (0, 0), (0, LANES - mine)))

    high, low = lag_tables(channels)
    pick = pick_matrix(stations, groups, owners)
    pcos, psin = period_tables(periods, own_rows)
    any_spec = pl.BlockSpec(memory_space=pl.ANY)
    vmem = pl.BlockSpec(memory_space=pltpu.VMEM)
    f32, bf16 = jnp.float32, jnp.bfloat16
    pad = -(-rows // LANES) * LANES
    dma = pltpu.SemaphoreType.DMA
    out = pl.pallas_call(
        functools.partial(kernel, (groups, owners, stations, periods, depth, blocks)),
        out_shape=jax.ShapeDtypeStruct((2, own_rows * periods, LAGS), f32),
        in_specs=[any_spec, vmem, vmem, pl.BlockSpec(memory_space=pltpu.SMEM), any_spec, any_spec, any_spec, vmem, vmem],
        out_specs=vmem,
        scratch_shapes=[
            pltpu.VMEM((stations, mine, depth, 2 * blocks, LANES), bf16),
            pltpu.VMEM((groups, local, depth, lanes), bf16),
            pltpu.VMEM((groups, local * depth, LANES), f32),
            pltpu.VMEM((owners, groups, local, depth, lanes), bf16),
            pltpu.VMEM((stations, owners, depth, lanes), f32),
            pltpu.VMEM((stations * depth, lanes), f32),
            pltpu.VMEM((pad, lanes), f32),
            pltpu.VMEM((lanes, pad), f32),
            pltpu.VMEM((stations * depth, lanes, LANES), f32),
            pltpu.VMEM((stations * (stations + 1) // 2, lanes, LANES), f32),
            pltpu.VMEM((mine, stations * depth, LANES), f32),
            pltpu.VMEM(high.shape, bf16),
            pltpu.VMEM(low.shape, bf16),
            pltpu.VMEM(pick.shape, bf16),
            pltpu.VMEM((QUARTERS,) + high.shape, bf16),
            pltpu.VMEM((QUARTERS,) + low.shape, bf16),
            pltpu.VMEM((stations * depth, SUB, LANES), f32),
            pltpu.VMEM((stations * depth, SUB, LANES), f32),
            pltpu.VMEM((depth, 2 * SUB, LANES), f32),
            pltpu.VMEM((depth, stations, SUB, LANES), f32),
            pltpu.VMEM((depth, stations, SUB, LANES), f32),
            pltpu.VMEM((rows, SUB, LANES), f32),
            pltpu.VMEM((rows, width), bf16),
            pltpu.VMEM((rows, width), bf16),
            pltpu.VMEM((rows, LAGS), f32),
            pltpu.VMEM((mine, owners, 2 * span, LAGS), bf16),
            pltpu.VMEM((mine, owners, 2 * span, LAGS), bf16),
            pltpu.VMEM((2, span, LAGS), f32),
            pltpu.VMEM((mine, wide, 2, own_rows, LAGS), f32),
            pltpu.VMEM((groups, split, mine, 2, own_rows, LAGS), f32),
            pltpu.VMEM((2, periods * own_rows, LAGS), f32),
            dma((5,)),
            dma((steps,)),
            dma((groups, steps)),
            dma((groups, steps)),
            dma((2, groups)),
            dma((2, groups)),
            dma((owners,)),
            dma((owners,)),
            dma((mine, owners)),
            dma((mine, owners)),
            dma((mine, wide)),
            dma((groups, split, mine)),
        ],
        compiler_params=pltpu.CompilerParams(collective_id=0, has_side_effects=True, vmem_limit_bytes=60 << 20),
        name="correlate",
    )(x, w, d, partner_order, jnp.asarray(high), jnp.asarray(low), jnp.asarray(pick), pcos, psin)
    return out.reshape(2, own_rows, periods, LAGS)


def solution(mesh):
    return jax.shard_map(
        per_device,
        mesh=mesh,
        in_specs=(
            P("stn", None, "tm", None, None),
            P("stn", None, "tm", None),
            P("stn", None, "tm"),
            P(),
            P(),
        ),
        out_specs=P(None, ("stn", "tm"), None, None),
        check_vma=False,
    )
```

```python
import functools
import math

import jax
import jax.numpy as jnp
import numpy as np
from jax import lax
from jax.experimental import pallas as pl
from jax.experimental.pallas import tpu as pltpu
from jax.sharding import PartitionSpec as P

LAGS = 256
QUARTERS = 4
LANES = 128
SUB = 8
TILE = 4
MESH = pl.DeviceIdType.MESH


def lag_tables(channels):
    lags = np.arange(1, LAGS // 2 + 1)
    j = np.arange(channels // QUARTERS)
    angle = (j[:, None] * lags[None, :] % channels) * (2.0 * np.pi / channels)
    table = np.concatenate([np.cos(angle), np.sin(angle)], axis=1).astype(np.float32)
    high = table.astype(jnp.bfloat16)
    low = (table - high.astype(np.float32)).astype(jnp.bfloat16)
    return high, low


def pair_rows(stations):
    tiles = stations // TILE
    off = [(x * TILE, y * TILE) for x in range(tiles) for y in range(x + 1, tiles)]
    real, imag = {}, {}
    for x, y in off:
        for i in range(TILE):
            for j in range(TILE):
                real[x + i, y + j] = len(real)
    for x in range(tiles):
        for i in range(TILE):
            for j in range(i, TILE):
                real[x * TILE + i, x * TILE + j] = len(real)
    top = len(real)
    for x, y in off:
        for i in range(TILE):
            for j in range(TILE):
                imag[x + i, y + j] = top + len(imag)
    for x in range(tiles):
        for i in range(TILE):
            for j in range(i + 1, TILE):
                imag[x * TILE + i, x * TILE + j] = top + len(imag)
    return off, real, imag


def pick_matrix(stations, groups, owners):
    _, real, imag = pair_rows(stations)
    split = owners // stations
    wide = groups * split
    local = stations // groups
    span = stations // split
    pick = np.zeros((groups, owners, 2, span, stations * stations), np.float32)
    for g in range(groups):
        for t in range(owners):
            a = (t % wide // split * local + t // wide - g * local) % stations
            for n in range(span):
                b = (t % split * span + n - g * local) % stations
                key = (min(a, b), max(a, b))
                pick[g, t, 0, n, real[key]] = 1.0
                if a != b:
                    pick[g, t, 1, n, imag[key]] = 1.0 if a < b else -1.0
    return pick.reshape(groups, owners * 2 * span, stations * stations).astype(jnp.bfloat16)


def period_tables(periods, rows):
    idx = np.arange(periods)
    angle = (idx[:, None] * idx[None, :] % periods) * (2.0 * np.pi / periods)
    eye = np.eye(rows)

    def table(m):
        wide = np.einsum("rp,nm->nrpm", m, eye).reshape(rows * periods, periods * rows)
        return jnp.asarray(wide.astype(np.float32))

    return table(np.cos(angle)), table(np.sin(angle))


def dot(a, b):
    return jnp.dot(a, b, preferred_element_type=jnp.float32)


SIN = [(-1) ** n * math.pi ** (2 * n + 1) / math.factorial(2 * n + 1) for n in range(6)]
COS = [(-1) ** n * math.pi ** (2 * n) / math.factorial(2 * n) for n in range(7)]


def cos_sin_turns(turns):
    frac = turns - jnp.floor(turns + 0.5)
    square = frac * frac
    s = jnp.full_like(square, SIN[-1])
    for coef in SIN[-2::-1]:
        s = s * square + coef
    s = s * frac
    c = jnp.full_like(square, COS[-1])
    for coef in COS[-2::-1]:
        c = c * square + coef
    return 1.0 - 2.0 * (s * s), 2.0 * (s * c)


def kernel(
    sizes,
    x_hbm, flags_hbm, index_hbm, model_ref, partner_ref, high_hbm, low_hbm, pick_hbm, pcos_hbm, psin_hbm,
    out_ref,
    xall, flags, index_ref, pcos_ref, psin_ref, wsend, dsend, wbuf, dbuf, wall, wf, wrow, acc, scale_ref, turned,
    wide_w, dsplat, step_c, step_s, base_c, base_s, th, tl, pick, wh, wl, tmp, yr, yi, ys, yd, v_ref, vh, z_ref,
    zs, rb, red, fs, fr, gf,
    table_sem, own_sem, xs_sem, xr_sem, ws_sem, wr_sem, gs_sem, gr_sem, rs_sem, rr_sem, fs_sem, fr_sem,
):
    groups, owners, stations, periods, depth, blocks = sizes
    local = stations // groups
    mine = periods // groups
    split = owners // stations
    wide = groups * split
    span = stations // split
    own_rows = stations // wide
    rows = stations * stations
    steps = mine * QUARTERS
    lags = LAGS // 2
    me = lax.axis_index("stn")
    t = lax.axis_index("tm")
    home = t // wide
    place = t % wide
    plane = place // split
    part = t % split

    def band(i):
        return pl.ds(pl.multiple_of((i % QUARTERS) * 2 * SUB, 2 * SUB), 2 * SUB)

    def own_copy(i):
        return pltpu.make_async_copy(
            x_hbm.at[:, me * mine + i // QUARTERS, :, band(i), :],
            xall.at[pl.ds(0, local), i // QUARTERS, :, band(i), :],
            own_sem.at[i],
        )

    tables = [
        pltpu.make_async_copy(source, target, table_sem.at[n])
        for n, (source, target) in enumerate((
            (flags_hbm, flags), (index_hbm, index_ref), (high_hbm, th), (low_hbm, tl), (pick_hbm.at[me], pick),
            (pcos_hbm, pcos_ref), (psin_hbm, psin_ref),
        ))
    ]
    barrier = pltpu.get_barrier_semaphore()
    for shift in range(1, groups):
        for w in range(wide):
            peer = {"stn": lax.rem(me + shift, groups), "tm": home * wide + lax.rem(place + w, wide)}
            pl.semaphore_signal(barrier, inc=1, device_id=peer, device_id_type=MESH)
    for shift in range(1, owners):
        pl.semaphore_signal(barrier, inc=1, device_id={"tm": lax.rem(t + shift, owners)}, device_id_type=MESH)
    for copy in tables:
        copy.start()

    def start_own(i, _):
        own_copy(i).start()
        return 0

    lax.fori_loop(0, steps, start_own, 0)

    tables[1].wait()
    index = index_ref[...]

    def look_up(n, coef):
        here = index == n
        return tuple(jnp.where(here, model_ref[c, n], coef[c]) for c in range(3))

    none = jnp.zeros(index.shape, jnp.float32)
    coef = lax.fori_loop(0, model_ref.shape[1], look_up, (none, none, none), unroll=4)
    total = depth * owners
    times = (
        lax.broadcasted_iota(jnp.int32, index.shape, 2) * total + t * depth + lax.broadcasted_iota(jnp.int32, index.shape, 1)
    ).astype(jnp.float32)
    moment = times / float(periods * total)
    delay = (coef[0] + coef[1] * moment + coef[2] * moment * moment) * (0.5 / (blocks * LANES))
    dsend[...] = jnp.zeros_like(dsend)
    for g in range(groups):
        dsend[g, :, :, :mine] = delay[:, :, g * mine : (g + 1) * mine]
    tables[0].wait()
    for g in range(groups):
        pieces = [flags[:, g * mine + p].astype(jnp.float32) for p in range(mine)]
        gap = wsend.shape[-1] - mine * blocks
        if gap:
            pieces.append(jnp.ones(pieces[0].shape[:-1] + (gap,), jnp.float32))
        both = jnp.concatenate(pieces, axis=-1) if len(pieces) > 1 else pieces[0]
        wsend[g] = (1.0 - both).astype(jnp.bfloat16)
    wbuf[0] = wsend[me]
    dbuf[0] = dsend[me]
    pl.semaphore_wait(barrier, (groups - 1) * wide + owners - 1)

    def small_copies(shift):
        target = lax.rem(me + shift, groups)
        return [
            pltpu.make_async_remote_copy(
                src_ref=ref.at[target], dst_ref=buf.at[groups - shift], send_sem=ws_sem.at[n, shift],
                recv_sem=wr_sem.at[n, shift], device_id={"stn": target}, device_id_type=MESH,
            )
            for n, (ref, buf) in enumerate(((wsend, wbuf), (dsend, dbuf)))
        ]

    def spectra_copy(shift, i):
        target = lax.rem(me + shift, groups)
        return pltpu.make_async_remote_copy(
            src_ref=x_hbm.at[:, target * mine + i // QUARTERS, :, band(i), :],
            dst_ref=xall.at[pl.ds((groups - shift) * local, local), i // QUARTERS, :, band(i), :],
            send_sem=xs_sem.at[shift, i], recv_sem=xr_sem.at[shift, i],
            device_id={"stn": target}, device_id_type=MESH,
        )

    for shift in range(1, groups):
        for copy in small_copies(shift):
            copy.start()

    def start_spectra(i, _):
        for shift in range(1, groups):
            spectra_copy(shift, i).start()
        return 0

    lax.fori_loop(0, steps, start_spectra, 0)

    for copy in tables[2:]:
        copy.wait()
    lag = lax.broadcasted_iota(jnp.int32, (1, lags), 1) + 1
    for quarter in range(QUARTERS):
        turn = (lag * quarter) % 4
        cq = jnp.where(turn == 0, 1.0, jnp.where(turn == 2, -1.0, 0.0))
        sq = jnp.where(turn == 1, 1.0, jnp.where(turn == 3, -1.0, 0.0))

        def turn_rows(n, _, quarter=quarter, cq=cq, sq=sq):
            r = pl.ds(pl.multiple_of(n * LANES, LANES), LANES)
            for source, target in ((th, wh), (tl, wl)):
                c = source[r, :lags].astype(jnp.float32)
                s = source[r, lags:].astype(jnp.float32)
                target[quarter, r, :lags] = (c * cq - s * sq).astype(jnp.bfloat16)
                target[quarter, r, lags:] = (s * cq + c * sq).astype(jnp.bfloat16)
            return 0

        lax.fori_loop(0, th.shape[0] // LANES, turn_rows, 0)

    for shift in range(1, groups):
        for copy in small_copies(shift):
            copy.wait_recv()

    def gather_copy(shift, source):
        return pltpu.make_async_remote_copy(
            src_ref=wbuf, dst_ref=wall.at[source], send_sem=gs_sem.at[shift], recv_sem=gr_sem.at[source],
            device_id={"tm": lax.rem(t + shift, owners)}, device_id_type=MESH,
        )

    for shift in range(1, owners):
        gather_copy(shift, t).start()
    wall[t] = wbuf[...]

    for g in range(groups):
        for l in range(local):
            r = (g * local + l) * depth
            wrow[r : r + depth, :] = wbuf[g, l].astype(jnp.float32)
            d = dbuf[g, l]
            for p in range(mine):
                dsplat[p, r : r + depth, :] = jnp.broadcast_to(d[:, p : p + 1], d.shape)
    c, s = cos_sin_turns(dsplat[...] * float(SUB * LANES))
    step_c[...] = c
    step_s[...] = s
    channel = (
        lax.broadcasted_iota(jnp.int32, (SUB, LANES), 0) * LANES + lax.broadcasted_iota(jnp.int32, (SUB, LANES), 1)
    ).astype(jnp.float32)
    spectra = stations * depth

    def start_phase(n, _):
        p = n // spectra
        r = n % spectra
        c, s = cos_sin_turns(dsplat[p, pl.ds(r, 1), :] * channel)
        base_c[p, r] = c
        base_s[p, r] = s
        return 0

    lax.fori_loop(0, mine * spectra, start_phase, 0, unroll=8)
    w_t = wrow[...].T
    for r in range(spectra):
        wide_w[r] = jnp.broadcast_to(w_t[:, r : r + 1], (w_t.shape[0], LANES))

    off, real_row, imag_row = pair_rows(stations)
    pairs = len(real_row)
    acc_flat = acc.reshape(pairs * SUB, LANES)
    v_flat = v_ref.reshape(rows * SUB, LANES)

    def make_scale():
        for shift in range(1, owners):
            gather_copy(shift, lax.rem(t + owners - shift, owners)).wait_recv()
        for n in range(owners):
            wf[:, n * depth : (n + 1) * depth, :] = wall[n].astype(jnp.float32).reshape(stations, depth, LANES)
        for a in range(stations):
            for b0 in range(a // TILE * TILE, stations, TILE):
                b = max(a, b0)
                count = b0 + TILE - b
                product = wf[a][None] * wf[b : b + count]
                m = real_row[a, b]
                acc[m : m + count] = jnp.sum(product.reshape(count, owners * depth // SUB, SUB, LANES), axis=1)
        count = acc_flat[pl.ds(0, pairs, stride=SUB), :]
        for b in range(1, SUB):
            count = count + acc_flat[pl.ds(b, pairs, stride=SUB), :]
        scale_ref[:pairs, :] = 1.0 / jnp.sqrt(jnp.maximum(count, 1.0))
        n = len(off) * TILE * TILE
        if n:
            scale_ref[pairs : pairs + n, :] = scale_ref[:n, :]
        for x in range(0, stations, TILE):
            for i in range(TILE - 1):
                m, q, n = real_row[x + i, x + i + 1], imag_row[x + i, x + i + 1], TILE - 1 - i
                scale_ref[q : q + n, :] = scale_ref[m : m + n, :]

    def scatter_copy(p, shift, target, source):
        return pltpu.make_async_remote_copy(
            src_ref=zs.at[p, target], dst_ref=rb.at[p, source], send_sem=rs_sem.at[p, shift],
            recv_sem=rr_sem.at[p, source], device_id={"tm": lax.rem(t + shift, owners)}, device_id_type=MESH,
        )

    def final_copy(p, w, source, piece):
        return pltpu.make_async_remote_copy(
            src_ref=fs.at[p, w], dst_ref=fr.at[source, piece, p], send_sem=fs_sem.at[p, w],
            recv_sem=fr_sem.at[source, piece, p], device_id={"stn": plane, "tm": home * wide + w}, device_id_type=MESH,
        )

    def reduce_period(p):
        total = zs[p, t].astype(jnp.float32)
        for shift in range(1, owners):
            source = lax.rem(t + owners - shift, owners)
            scatter_copy(p, shift, t, source).wait_recv()
        for shift in range(1, owners):
            total = total + rb[p, lax.rem(t + owners - shift, owners)].astype(jnp.float32)
        red[...] = total.reshape(red.shape)
        for w in range(wide):
            for n in range(own_rows):
                b = partner_ref[w * own_rows + n]
                if split > 1:
                    keep = jnp.where(b // span == part, 1.0, 0.0)
                    b = b % span
                for ri in range(2):
                    row = red[ri, pl.ds(b, 1), :]
                    fs[p, w, ri, n : n + 1, :] = row * keep if split > 1 else row
        for w in range(wide):
            to_self = (plane == me) & (w == place)

            @pl.when(to_self)
            def _():
                fr[me, part, p] = fs[p, w]

            @pl.when(jnp.logical_not(to_self))
            def _():
                final_copy(p, w, me, part).start()

    def step(i, _):
        p = i // QUARTERS
        quarter = i % QUARTERS
        at = pl.ds(pl.multiple_of(p * blocks + quarter * SUB, SUB), SUB)

        own_copy(i).wait()
        for shift in range(1, groups):
            spectra_copy(shift, i).wait_recv()

        def rotate(n, _):
            for j in range(2):
                s = n * 2 + j
                for k in range(depth):
                    r = s * depth + k
                    tmp[j * depth + k] = xall[s, p, k, band(i), :].astype(jnp.float32)
                    real = tmp[j * depth + k, pl.ds(0, SUB, stride=2), :]
                    imag = tmp[j * depth + k, pl.ds(1, SUB, stride=2), :]
                    c = base_c[p, r]
                    sn = base_s[p, r]
                    w = wide_w[r, at, :]
                    new_real = (w * (real * c + imag * sn)).astype(jnp.bfloat16).astype(jnp.float32)
                    new_imag = (w * (imag * c - real * sn)).astype(jnp.bfloat16).astype(jnp.float32)
                    yr[k, s] = new_real
                    yi[k, s] = new_imag
                    ys[k, s] = new_real + new_imag
                    yd[k, s] = new_real - new_imag
                    pc = step_c[p, pl.ds(r, 1), :]
                    ps = step_s[p, pl.ds(r, 1), :]
                    base_c[p, r] = c * pc - sn * ps
                    base_s[p, r] = sn * pc + c * ps
            return 0

        lax.fori_loop(0, stations // 2, rotate, 0)

        half = TILE // 2
        for x, y0 in off:
            for y in (y0, y0 + half):
                for k in range(depth):
                    ar, ai, asum = (ref[k, x : x + TILE][:, None] for ref in (yr, yi, ys))
                    br, bi, bdiff = (ref[k, y : y + half][None] for ref in (yr, yi, yd))
                    first = ar * br if k == 0 else first + ar * br
                    second = ai * bi if k == 0 else second + ai * bi
                    third = asum * bdiff if k == 0 else third + asum * bdiff
                real = first + second
                imag = third - (first - second)
                for n in range(TILE):
                    m = real_row[x + n, y]
                    q = imag_row[x + n, y]
                    v_ref[m : m + half] = real[n]
                    v_ref[q : q + half] = imag[n]
        for x in range(0, stations, TILE):
            for a in range(x, x + TILE):
                n = x + TILE - a
                for k in range(depth):
                    ar, ai = yr[k, a], yi[k, a]
                    term = ar * ar + ai * ai
                    auto = term if k == 0 else auto + term
                    if n > 1:
                        br, bi, bdiff = yr[k, a + 1 : a + n], yi[k, a + 1 : a + n], yd[k, a + 1 : a + n]
                        asum = ys[k, a]
                        first = ar * br if k == 0 else first + ar * br
                        second = ai * bi if k == 0 else second + ai * bi
                        third = asum * bdiff if k == 0 else third + asum * bdiff
                m = real_row[a, a]
                v_ref[m] = auto
                if n > 1:
                    q = imag_row[a, a + 1]
                    v_ref[m + 1 : m + n] = first + second
                    v_ref[q : q + n - 1] = third - (first - second)

        pl.when(i == 0)(make_scale)
        turned[...] = pltpu.roll(scale_ref[...], LANES - (p * blocks + quarter * SUB), 1)
        for b in range(SUB):
            v = v_flat[pl.ds(b, rows, stride=SUB), :] * turned[:, b : b + 1]
            vh[:, b * LANES : (b + 1) * LANES] = v.astype(jnp.bfloat16)
        values = dot(vh[...], wh[quarter]) + dot(vh[...], wl[quarter])

        @pl.when(quarter == 0)
        def _():
            z_ref[...] = values

        @pl.when(quarter > 0)
        def _():
            z_ref[...] += values

        @pl.when(quarter == QUARTERS - 1)
        def _():
            picked = dot(pick[...], z_ref[...].astype(jnp.bfloat16)).astype(jnp.bfloat16)
            zs[p] = picked.reshape(zs.shape[1:])
            for shift in range(1, owners):
                scatter_copy(p, shift, lax.rem(t + shift, owners), t).start()

        @pl.when((quarter == QUARTERS - 1) & (p > 0))
        def _():
            reduce_period(p - 1)

        return 0

    lax.fori_loop(0, steps, step, 0)
    reduce_period(mine - 1)

    for p in range(mine):
        for g in range(groups):
            for h in range(split):
                from_self = (me == g) & (place == me * split + h)

                @pl.when(jnp.logical_not(from_self))
                def _():
                    final_copy(p, 0, g, h).wait_recv()

    for g in range(groups):
        for p in range(mine):
            value = fr[g, 0, p]
            for h in range(1, split):
                value = value + fr[g, h, p]
            r = (g * mine + p) * own_rows
            gf[:, r : r + own_rows, :] = value

    highest = lax.Precision.HIGHEST
    rc, rs = gf[0, :, :lags], gf[0, :, lags:]
    ic, im_s = gf[1, :, :lags], gf[1, :, lags:]
    flip = (
        lax.broadcasted_iota(jnp.int32, (lags, lags), 0) + lax.broadcasted_iota(jnp.int32, (lags, lags), 1) == lags - 1
    ).astype(jnp.float32)
    pcos = pcos_ref[...]
    psin = psin_ref[...]
    factor = 1.0 / math.sqrt(periods * blocks * LANES)

    def mix(m, v):
        return jnp.dot(m, v, precision=highest, preferred_element_type=jnp.float32)

    for side in range(2):
        if side == 0:
            real, imag = mix(rc - im_s, flip), mix(ic + rs, flip)
        else:
            real, imag = rc + im_s, ic - rs
        cols = slice(side * lags, (side + 1) * lags)
        out_ref[0, :, cols] = (mix(pcos, real) + mix(psin, imag)) * factor
        out_ref[1, :, cols] = (mix(pcos, imag) - mix(psin, real)) * factor

    for shift in range(1, groups):
        for copy in small_copies(shift):
            copy.wait_send()
    for shift in range(1, owners):
        gather_copy(shift, t).wait_send()

    def sent(i, _):
        for shift in range(1, groups):
            spectra_copy(shift, i).wait_send()
        return 0

    lax.fori_loop(0, steps, sent, 0)

    def scattered(p, _):
        for shift in range(1, owners):
            scatter_copy(p, shift, lax.rem(t + shift, owners), t).wait_send()
        for w in range(wide):
            @pl.when(jnp.logical_not((plane == me) & (w == place)))
            def _():
                final_copy(p, w, me, part).wait_send()
        return 0

    lax.fori_loop(0, mine, scattered, 0)


def per_device(spectra, flags, poly_index, delay_model, partner_order):
    local, periods, depth, _, channels = spectra.shape
    groups = lax.axis_size("stn")
    owners = lax.axis_size("tm")
    stations = local * groups
    mine = periods // groups
    blocks = flags.shape[-1]
    split = owners // stations
    wide = groups * split
    own_rows = stations // wide
    span = stations // split
    rows = stations * stations
    pairs = stations * (stations + 1) // 2
    steps = mine * QUARTERS
    width = channels // QUARTERS
    lanes = LANES
    assert channels == blocks * LANES and width == SUB * LANES and stations % TILE == 0 and mine * blocks <= lanes

    x = spectra.reshape(local, periods, depth, 2, blocks, LANES).transpose(0, 1, 2, 4, 3, 5)
    x = x.reshape(local, periods, depth, 2 * blocks, LANES)
    high, low = lag_tables(channels)
    pick = pick_matrix(stations, groups, owners)
    pcos, psin = period_tables(periods, own_rows)
    any_spec = pl.BlockSpec(memory_space=pl.ANY)
    smem = pl.BlockSpec(memory_space=pltpu.SMEM)
    f32, bf16, i32 = jnp.float32, jnp.bfloat16, jnp.int32
    spectra_rows = stations * depth
    dma = pltpu.SemaphoreType.DMA
    out = pl.pallas_call(
        functools.partial(kernel, (groups, owners, stations, periods, depth, blocks)),
        out_shape=jax.ShapeDtypeStruct((2, own_rows * periods, LAGS), f32),
        in_specs=[any_spec, any_spec, any_spec, smem, smem] + [any_spec] * 5,
        out_specs=pl.BlockSpec(memory_space=pltpu.VMEM),
        scratch_shapes=[
            pltpu.VMEM((stations, mine, depth, 2 * blocks, LANES), bf16),
            pltpu.VMEM(flags.shape, i32),
            pltpu.VMEM((local, depth, periods), i32),
            pltpu.VMEM(pcos.shape, f32),
            pltpu.VMEM(psin.shape, f32),
            pltpu.VMEM((groups, local, depth, lanes), bf16),
            pltpu.VMEM((groups, local, depth, LANES), f32),
            pltpu.VMEM((groups, local, depth, lanes), bf16),
            pltpu.VMEM((groups, local, depth, LANES), f32),
            pltpu.VMEM((owners, groups, local, depth, lanes), bf16),
            pltpu.VMEM((stations, owners * depth, lanes), f32),
            pltpu.VMEM((spectra_rows, lanes), f32),
            pltpu.VMEM((pairs, SUB, lanes), f32),
            pltpu.VMEM((rows, lanes), f32),
            pltpu.VMEM((rows, lanes), f32),
            pltpu.VMEM((spectra_rows, lanes, LANES), f32),
            pltpu.VMEM((mine, spectra_rows, LANES), f32),
            pltpu.VMEM((mine, spectra_rows, LANES), f32),
            pltpu.VMEM((mine, spectra_rows, LANES), f32),
            pltpu.VMEM((mine, spectra_rows, SUB, LANES), f32),
            pltpu.VMEM((mine, spectra_rows, SUB, LANES), f32),
            pltpu.VMEM(high.shape, bf16),
            pltpu.VMEM(low.shape, bf16),
            pltpu.VMEM(pick.shape[1:], bf16),
            pltpu.VMEM((QUARTERS,) + high.shape, bf16),
            pltpu.VMEM((QUARTERS,) + low.shape, bf16),
            pltpu.VMEM((2 * depth, 2 * SUB, LANES), f32),
            pltpu.VMEM((depth, stations, SUB, LANES), f32),
            pltpu.VMEM((depth, stations, SUB, LANES), f32),
            pltpu.VMEM((depth, stations, SUB, LANES), f32),
            pltpu.VMEM((depth, stations, SUB, LANES), f32),
            pltpu.VMEM((rows, SUB, LANES), f32),
            pltpu.VMEM((rows, width), bf16),
            pltpu.VMEM((rows, LAGS), f32),
            pltpu.VMEM((mine, owners, 2 * span, LAGS), bf16),
            pltpu.VMEM((mine, owners, 2 * span, LAGS), bf16),
            pltpu.VMEM((2, span, LAGS), f32),
            pltpu.VMEM((mine, wide, 2, own_rows, LAGS), f32),
            pltpu.VMEM((groups, split, mine, 2, own_rows, LAGS), f32),
            pltpu.VMEM((2, periods * own_rows, LAGS), f32),
            dma((7,)),
            dma((steps,)),
            dma((groups, steps)),
            dma((groups, steps)),
            dma((2, groups)),
            dma((2, groups)),
            dma((owners,)),
            dma((owners,)),
            dma((mine, owners)),
            dma((mine, owners)),
            dma((mine, wide)),
            dma((groups, split, mine)),
        ],
        compiler_params=pltpu.CompilerParams(collective_id=0, has_side_effects=True, vmem_limit_bytes=60 << 20),
        name="correlate",
    )(
        x, flags, poly_index.transpose(0, 2, 1), delay_model.T, partner_order,
        jnp.asarray(high), jnp.asarray(low), jnp.asarray(pick), pcos, psin,
    )
    return out.reshape(2, own_rows, periods, LAGS)


def solution(mesh):
    return jax.shard_map(
        per_device,
        mesh=mesh,
        in_specs=(
            P("stn", None, "tm", None, None),
            P("stn", None, "tm", None),
            P("stn", None, "tm"),
            P(),
            P(),
        ),
        out_specs=P(None, ("stn", "tm"), None, None),
        check_vma=False,
    )
```

```python
import functools
import math

import jax
import jax.numpy as jnp
import numpy as np
from jax import lax
from jax.experimental import pallas as pl
from jax.experimental.pallas import tpu as pltpu
from jax.sharding import PartitionSpec as P

LAGS = 256
QUARTERS = 4
LANES = 128
SUB = 8
TILE = 4
MESH = pl.DeviceIdType.MESH


def lag_tables(channels):
    lags = np.arange(1, LAGS // 2 + 1)
    j = np.arange(channels // QUARTERS)
    angle = (j[:, None] * lags[None, :] % channels) * (2.0 * np.pi / channels)
    table = np.concatenate([np.cos(angle), np.sin(angle)], axis=1).astype(np.float32)
    high = table.astype(jnp.bfloat16)
    low = (table - high.astype(np.float32)).astype(jnp.bfloat16)
    return high, low


def pair_rows(stations):
    last = stations - TILE
    kinds = []
    real, imag, order = {}, {}, {}
    row = 0
    for late in (False, True):
        off = [(x, y) for x in range(0, stations, TILE) for y in range(x + TILE, stations, TILE) if (y == last) == late]
        same = [last] if late else list(range(0, last, TILE))
        for part in (real, imag):
            skip = 0 if part is real else 1
            start = row
            keys = [(x + i, y + j) for x, y in off for i in range(TILE) for j in range(TILE)]
            keys += [(x + i, x + j) for x in same for i in range(TILE) for j in range(i + skip, TILE)]
            for key in keys:
                part[key] = row
                row += 1
                if part is real:
                    order[key] = len(order)
        kinds.append((off, same))
    return kinds, real, imag, order


def late_first(local):
    return local // 4 if local >= 2 * TILE else 0


def relative(station, plane, groups, local):
    slot = (station // local - plane) % groups
    place = station % local
    return slot * local + (place if slot == 0 else (place + late_first(local)) % local)


def pick_matrices(stations, groups, owners):
    _, real, imag, _ = pair_rows(stations)
    split = owners // stations
    wide = groups * split
    local = stations // groups
    units = stations // split // TILE
    rows = stations * stations
    early = (stations - TILE) ** 2
    pick_a = np.zeros((groups, owners, units - 1, 2, TILE, rows), np.float32)
    pick_b = np.zeros((groups, owners, 2, TILE, rows), np.float32)
    pick_c = np.zeros((groups, TILE * split, units - 1, 2, TILE, rows), np.float32)
    for g in range(groups):
        for t in range(owners):
            a = relative(t % wide // split * local + t // wide, g, groups, local)
            late = a >= stations - TILE
            for u in range(units):
                for n in range(TILE):
                    b = (t % split * units + u) * TILE + n
                    key = (min(a, b), max(a, b))
                    if u == units - 1:
                        target = pick_b[g, t]
                    elif late:
                        target = pick_c[g, (a - stations + TILE) * split + t % split, u]
                    else:
                        target = pick_a[g, t, u]
                    target[0, n, real[key]] = 1.0
                    if a != b:
                        target[1, n, imag[key]] = 1.0 if a < b else -1.0
    pick_a = pick_a.reshape(groups, -1, rows)
    assert not pick_a[:, :, early:].any()
    pick_b = np.concatenate([pick_b.reshape(groups, -1, rows), pick_c.reshape(groups, -1, rows)], axis=1)
    return pick_a[:, :, :early].astype(jnp.bfloat16), pick_b.astype(jnp.bfloat16)


def arrivals(stations, groups):
    local = stations // groups
    runs = []
    for shift in range(1, groups):
        slot = groups - shift
        turn = late_first(local)
        places = [((i - turn) % local, slot * local + i) for i in range(local)]
        for source, here in places:
            late = here >= stations - TILE
            if runs and runs[-1][:2] == (late, shift) and source == runs[-1][2] + runs[-1][3]:
                runs[-1] = (late, shift, runs[-1][2], runs[-1][3] + 1, runs[-1][4])
            else:
                runs.append((late, shift, source, 1, here))
    return runs


def period_tables(periods, rows):
    idx = np.arange(periods)
    angle = (idx[:, None] * idx[None, :] % periods) * (2.0 * np.pi / periods)
    eye = np.eye(rows)

    def table(m):
        wide = np.einsum("rp,nm->nrpm", m, eye).reshape(rows * periods, periods * rows)
        return jnp.asarray(wide.astype(np.float32))

    return table(np.cos(angle)), table(np.sin(angle))


def dot(a, b):
    return jnp.dot(a, b, preferred_element_type=jnp.float32)


SIN = [(-1) ** n * math.pi ** (2 * n + 1) / math.factorial(2 * n + 1) for n in range(6)]
COS = [(-1) ** n * math.pi ** (2 * n) / math.factorial(2 * n) for n in range(7)]


def cos_sin_turns(turns):
    frac = turns - jnp.floor(turns + 0.5)
    square = frac * frac
    s = jnp.full_like(square, SIN[-1])
    for coef in SIN[-2::-1]:
        s = s * square + coef
    s = s * frac
    c = jnp.full_like(square, COS[-1])
    for coef in COS[-2::-1]:
        c = c * square + coef
    return 1.0 - 2.0 * (s * s), 2.0 * (s * c)


def kernel(
    sizes,
    x_hbm, flags_hbm, index_hbm, model_ref, partner_ref, high_hbm, low_hbm, pick_a_hbm, pick_b_hbm, pcos_hbm, psin_hbm,
    out_ref,
    xall, flags, index_ref, pcos_ref, psin_ref, wsend, dsend, wbuf, dbuf, wall, wf, wrow, acc, counts, scale_ref, turned,
    wide_w, dsplat, step_c, step_s, base_c, base_s, th, tl, pick_a, pick_b, wh, wl, tmp, yr, yi, ys, yd, v_ref, vh, z_ref,
    zs_a, zs_b, zs_c, rb, red, fs, fr, gf,
    table_sem, own_sem, xs_sem, xr_sem, ws_sem, wr_sem, gs_sem, gr_sem, rs_sem, rr_sem, fs_sem, fr_sem,
):
    groups, owners, stations, periods, depth, blocks = sizes
    local = stations // groups
    mine = periods // groups
    split = owners // stations
    wide = groups * split
    span = stations // split
    own_rows = stations // wide
    rows = stations * stations
    steps = mine * QUARTERS
    lags = LAGS // 2
    me = lax.axis_index("stn")
    t = lax.axis_index("tm")
    home = t // wide
    place = t % wide
    plane = place // split
    part = t % split
    units = span // TILE
    early = (stations - TILE) ** 2
    turn_by = late_first(local)
    runs = arrivals(stations, groups)
    kinds, real_row, imag_row, pair_order = pair_rows(stations)
    pairs = len(real_row)

    def relative_here(station):
        slot = (station // local - me + groups) % groups
        return slot * local + (station % local + (slot + groups - 1) // groups * turn_by) % local

    mine_a = relative_here(plane * local + home)
    total_steps = 2 * steps
    full = 2 * (mine - 1) * QUARTERS

    def sub_step(n):
        last = n // full if full else 1
        i = (1 - last) * (n // 2) + last * ((mine - 1) * QUARTERS + (n + QUARTERS * 2 - full % (QUARTERS * 2)) % QUARTERS)
        kind = (1 - last) * (n % 2) + last * ((n + total_steps - full) // QUARTERS - total_steps // QUARTERS)
        return i, kind

    def band(i):
        return pl.ds(pl.multiple_of((i % QUARTERS) * 2 * SUB, 2 * SUB), 2 * SUB)

    def own_copy(i):
        return pltpu.make_async_copy(
            x_hbm.at[:, me * mine + i // QUARTERS, :, band(i), :],
            xall.at[pl.ds(0, local), i // QUARTERS, :, band(i), :],
            own_sem.at[i],
        )

    tables = [
        pltpu.make_async_copy(source, target, table_sem.at[n])
        for n, (source, target) in enumerate((
            (flags_hbm, flags), (index_hbm, index_ref), (high_hbm, th), (low_hbm, tl),
            (pick_a_hbm.at[me], pick_a), (pick_b_hbm.at[me], pick_b), (pcos_hbm, pcos_ref), (psin_hbm, psin_ref),
        ))
    ]
    barrier = pltpu.get_barrier_semaphore()
    for shift in range(1, groups):
        for w in range(wide):
            peer = {"stn": lax.rem(me + shift, groups), "tm": home * wide + lax.rem(place + w, wide)}
            pl.semaphore_signal(barrier, inc=1, device_id=peer, device_id_type=MESH)
    for shift in range(1, owners):
        pl.semaphore_signal(barrier, inc=1, device_id={"tm": lax.rem(t + shift, owners)}, device_id_type=MESH)
    for copy in tables:
        copy.start()

    def start_own(i, _):
        own_copy(i).start()
        return 0

    lax.fori_loop(0, steps, start_own, 0)

    tables[1].wait()
    index = index_ref[...]

    def look_up(n, coef):
        here = index == n
        return tuple(jnp.where(here, model_ref[c, n], coef[c]) for c in range(3))

    none = jnp.zeros(index.shape, jnp.float32)
    coef = lax.fori_loop(0, model_ref.shape[1], look_up, (none, none, none), unroll=4)
    total = depth * owners
    times = (
        lax.broadcasted_iota(jnp.int32, index.shape, 2) * total + t * depth + lax.broadcasted_iota(jnp.int32, index.shape, 1)
    ).astype(jnp.float32)
    moment = times / float(periods * total)
    delay = (coef[0] + coef[1] * moment + coef[2] * moment * moment) * (0.5 / (blocks * LANES))
    dsend[...] = jnp.zeros_like(dsend)
    for g in range(groups):
        dsend[g, :, :, :mine] = delay[:, :, g * mine : (g + 1) * mine]
    tables[0].wait()
    for g in range(groups):
        pieces = [flags[:, g * mine + p].astype(jnp.float32) for p in range(mine)]
        gap = wsend.shape[-1] - mine * blocks
        if gap:
            pieces.append(jnp.ones(pieces[0].shape[:-1] + (gap,), jnp.float32))
        both = jnp.concatenate(pieces, axis=-1) if len(pieces) > 1 else pieces[0]
        wsend[g] = (1.0 - both).astype(jnp.bfloat16)
    wbuf[0] = wsend[me]
    dbuf[0] = dsend[me]
    pl.semaphore_wait(barrier, (groups - 1) * wide + owners - 1)

    def small_copies(shift):
        target = lax.rem(me + shift, groups)
        return [
            pltpu.make_async_remote_copy(
                src_ref=ref.at[target], dst_ref=buf.at[groups - shift], send_sem=ws_sem.at[n, shift],
                recv_sem=wr_sem.at[n, shift], device_id={"stn": target}, device_id_type=MESH,
            )
            for n, (ref, buf) in enumerate(((wsend, wbuf), (dsend, dbuf)))
        ]

    def spectra_copy(n, i):
        _, shift, source, count, here = runs[n]
        target = lax.rem(me + shift, groups)
        return pltpu.make_async_remote_copy(
            src_ref=x_hbm.at[pl.ds(source, count), target * mine + i // QUARTERS, :, band(i), :],
            dst_ref=xall.at[pl.ds(here, count), i // QUARTERS, :, band(i), :],
            send_sem=xs_sem.at[n, i], recv_sem=xr_sem.at[n, i],
            device_id={"stn": target}, device_id_type=MESH,
        )

    for shift in range(1, groups):
        for copy in small_copies(shift):
            copy.start()

    def start_spectra(n, _):
        i, kind = sub_step(n)
        for late in (False, True):

            @pl.when(kind == int(late))
            def _():
                for r in range(len(runs)):
                    if runs[r][0] == late:
                        spectra_copy(r, i).start()

        return 0

    lax.fori_loop(0, total_steps, start_spectra, 0)

    for copy in tables[2:]:
        copy.wait()
    lag = lax.broadcasted_iota(jnp.int32, (1, lags), 1) + 1
    for quarter in range(QUARTERS):
        turn = (lag * quarter) % 4
        cq = jnp.where(turn == 0, 1.0, jnp.where(turn == 2, -1.0, 0.0))
        sq = jnp.where(turn == 1, 1.0, jnp.where(turn == 3, -1.0, 0.0))

        def turn_rows(n, _, quarter=quarter, cq=cq, sq=sq):
            r = pl.ds(pl.multiple_of(n * LANES, LANES), LANES)
            for source, target in ((th, wh), (tl, wl)):
                c = source[r, :lags].astype(jnp.float32)
                s = source[r, lags:].astype(jnp.float32)
                target[quarter, r, :lags] = (c * cq - s * sq).astype(jnp.bfloat16)
                target[quarter, r, lags:] = (s * cq + c * sq).astype(jnp.bfloat16)
            return 0

        lax.fori_loop(0, th.shape[0] // LANES, turn_rows, 0)

    for shift in range(1, groups):
        for copy in small_copies(shift):
            copy.wait_recv()

    def gather_copy(shift, source):
        return pltpu.make_async_remote_copy(
            src_ref=wbuf, dst_ref=wall.at[source], send_sem=gs_sem.at[shift], recv_sem=gr_sem.at[source],
            device_id={"tm": lax.rem(t + shift, owners)}, device_id_type=MESH,
        )

    for shift in range(1, owners):
        gather_copy(shift, t).start()
    wall[t] = wbuf[...]

    for g in range(groups):
        for l in range(local):
            r = (g * local + (l + turn_by * min(g, 1)) % local) * depth
            wrow[r : r + depth, :] = wbuf[g, l].astype(jnp.float32)
            d = dbuf[g, l]
            for p in range(mine):
                dsplat[p, r : r + depth, :] = jnp.broadcast_to(d[:, p : p + 1], d.shape)
    c, s = cos_sin_turns(dsplat[...] * float(SUB * LANES))
    step_c[...] = c
    step_s[...] = s
    channel = (
        lax.broadcasted_iota(jnp.int32, (SUB, LANES), 0) * LANES + lax.broadcasted_iota(jnp.int32, (SUB, LANES), 1)
    ).astype(jnp.float32)
    spectra = stations * depth

    def start_phase(n, _):
        p = n // spectra
        r = n % spectra
        c, s = cos_sin_turns(dsplat[p, pl.ds(r, 1), :] * channel)
        base_c[p, r] = c
        base_s[p, r] = s
        return 0

    lax.fori_loop(0, mine * spectra, start_phase, 0, unroll=8)
    w_t = wrow[...].T
    for r in range(spectra):
        wide_w[r] = jnp.broadcast_to(w_t[:, r : r + 1], (w_t.shape[0], LANES))

    acc_flat = acc.reshape(pairs * SUB, LANES)
    v_flat = v_ref.reshape(rows * SUB, LANES)

    def make_scale():
        for shift in range(1, owners):
            gather_copy(shift, lax.rem(t + owners - shift, owners)).wait_recv()
        for n in range(owners):
            for g in range(groups):
                turn = turn_by * min(g, 1)
                value = wall[n, g].astype(jnp.float32)
                at = slice(n * depth, (n + 1) * depth)
                wf[g * local + turn : (g + 1) * local, at, :] = value[: local - turn]
                if turn:
                    wf[g * local : g * local + turn, at, :] = value[local - turn :]
        for a in range(stations):
            for b0 in range(a // TILE * TILE, stations, TILE):
                b = max(a, b0)
                count = b0 + TILE - b
                product = wf[a][None] * wf[b : b + count]
                m = pair_order[a, b]
                acc[m : m + count] = jnp.sum(product.reshape(count, owners * depth // SUB, SUB, LANES), axis=1)
        count = acc_flat[pl.ds(0, pairs, stride=SUB), :]
        for b in range(1, SUB):
            count = count + acc_flat[pl.ds(b, pairs, stride=SUB), :]
        counts[...] = 1.0 / jnp.sqrt(jnp.maximum(count, 1.0))
        for off, same in kinds:
            pieces = []
            if off:
                x, y = off[0]
                n = len(off) * TILE * TILE
                pieces += [(real_row[x, y], pair_order[x, y], n), (imag_row[x, y], pair_order[x, y], n)]
            for x in same:
                if x == same[0]:
                    n = len(same) * TILE * (TILE + 1) // 2
                    pieces.append((real_row[x, x], pair_order[x, x], n))
                for i in range(TILE - 1):
                    pieces.append((imag_row[x + i, x + i + 1], pair_order[x + i, x + i + 1], TILE - 1 - i))
            for row, source, n in pieces:
                scale_ref[row : row + n, :] = counts[source : source + n, :]

    def station_of(target):
        return relative_here(target % wide // split * local + target // wide)

    def scatter_copy(p, shift, what, target, source):
        if what == "last":
            src, dst = zs_b.at[p, target], rb.at[p, source, units - 1]
        elif what == "early":
            src, dst = zs_a.at[p, target], rb.at[p, source, pl.ds(0, units - 1)]
        else:
            late = (station_of(target) + TILE) % stations * split + target % split
            src, dst = zs_c.at[p, late], rb.at[p, source, pl.ds(0, units - 1)]
        n = int(what == "last")
        return pltpu.make_async_remote_copy(
            src_ref=src, dst_ref=dst, send_sem=rs_sem.at[n, p, shift],
            recv_sem=rr_sem.at[n, p, source], device_id={"tm": lax.rem(t + shift, owners)}, device_id_type=MESH,
        )

    def is_late(target):
        return station_of(target) >= stations - TILE

    def final_copy(p, w, source, piece):
        return pltpu.make_async_remote_copy(
            src_ref=fs.at[p, w], dst_ref=fr.at[source, piece, p], send_sem=fs_sem.at[p, w],
            recv_sem=fr_sem.at[source, piece, p], device_id={"stn": plane, "tm": home * wide + w}, device_id_type=MESH,
        )

    def reduce_period(p):
        for shift in range(1, owners):
            source = lax.rem(t + owners - shift, owners)
            scatter_copy(p, shift, "early", t, source).wait_recv()
            scatter_copy(p, shift, "last", t, source).wait_recv()
        late = jnp.where(is_late(t), 1.0, 0.0)
        first = zs_a[p, t].astype(jnp.float32)
        first += late * zs_c[p, (mine_a % TILE) * split + part].astype(jnp.float32)
        last = zs_b[p, t].astype(jnp.float32)
        for shift in range(1, owners):
            source = lax.rem(t + owners - shift, owners)
            first += rb[p, source, : units - 1].astype(jnp.float32)
            last += rb[p, source, units - 1].astype(jnp.float32)
        red[: units - 1] = first
        red[units - 1] = last
        for w in range(wide):
            for n in range(own_rows):
                b = relative_here(partner_ref[w * own_rows + n])
                if split > 1:
                    keep = jnp.where(b // span == part, 1.0, 0.0)
                    b = b % span
                for ri in range(2):
                    row = red[b // TILE, pl.ds(ri * TILE + b % TILE, 1), :]
                    fs[p, w, ri, n : n + 1, :] = row * keep if split > 1 else row
        for w in range(wide):
            to_self = (plane == me) & (w == place)

            @pl.when(to_self)
            def _():
                fr[me, part, p] = fs[p, w]

            @pl.when(jnp.logical_not(to_self))
            def _():
                final_copy(p, w, me, part).start()

    half = TILE // 2

    def work(i, late):
        p = i // QUARTERS
        quarter = i % QUARTERS
        at = pl.ds(pl.multiple_of(p * blocks + quarter * SUB, SUB), SUB)
        first_station = stations - TILE if late else 0
        off, same = kinds[late]
        top, size = (early, rows - early) if late else (0, early)

        if not late:
            own_copy(i).wait()
        for n in range(len(runs)):
            if runs[n][0] == late:
                spectra_copy(n, i).wait_recv()

        def rotate(n, _):
            for j in range(2):
                s = first_station + n * 2 + j
                for k in range(depth):
                    r = s * depth + k
                    tmp[j * depth + k] = xall[s, p, k, band(i), :].astype(jnp.float32)
                    real = tmp[j * depth + k, pl.ds(0, SUB, stride=2), :]
                    imag = tmp[j * depth + k, pl.ds(1, SUB, stride=2), :]
                    c = base_c[p, r]
                    sn = base_s[p, r]
                    w = wide_w[r, at, :]
                    new_real = (w * (real * c + imag * sn)).astype(jnp.bfloat16).astype(jnp.float32)
                    new_imag = (w * (imag * c - real * sn)).astype(jnp.bfloat16).astype(jnp.float32)
                    yr[quarter, k, s] = new_real
                    yi[quarter, k, s] = new_imag
                    ys[quarter, k, s] = new_real + new_imag
                    yd[quarter, k, s] = new_real - new_imag
                    pc = step_c[p, pl.ds(r, 1), :]
                    ps = step_s[p, pl.ds(r, 1), :]
                    base_c[p, r] = c * pc - sn * ps
                    base_s[p, r] = sn * pc + c * ps
            return 0

        lax.fori_loop(0, (TILE if late else stations - TILE) // 2, rotate, 0)

        for x, y0 in off:
            for y in (y0, y0 + half):
                for k in range(depth):
                    ar, ai, asum = (ref[quarter, k, x : x + TILE][:, None] for ref in (yr, yi, ys))
                    br, bi, bdiff = (ref[quarter, k, y : y + half][None] for ref in (yr, yi, yd))
                    first = ar * br if k == 0 else first + ar * br
                    second = ai * bi if k == 0 else second + ai * bi
                    third = asum * bdiff if k == 0 else third + asum * bdiff
                real = first + second
                imag = third - (first - second)
                for n in range(TILE):
                    m = real_row[x + n, y]
                    q = imag_row[x + n, y]
                    v_ref[m : m + half] = real[n]
                    v_ref[q : q + half] = imag[n]
        for x in same:
            for a in range(x, x + TILE):
                n = x + TILE - a
                for k in range(depth):
                    ar, ai = yr[quarter, k, a], yi[quarter, k, a]
                    term = ar * ar + ai * ai
                    auto = term if k == 0 else auto + term
                    if n > 1:
                        br, bi, bdiff = (ref[quarter, k, a + 1 : a + n] for ref in (yr, yi, yd))
                        asum = ys[quarter, k, a]
                        first = ar * br if k == 0 else first + ar * br
                        second = ai * bi if k == 0 else second + ai * bi
                        third = asum * bdiff if k == 0 else third + asum * bdiff
                m = real_row[a, a]
                v_ref[m] = auto
                if n > 1:
                    q = imag_row[a, a + 1]
                    v_ref[m + 1 : m + n] = first + second
                    v_ref[q : q + n - 1] = third - (first - second)

        if not late:
            pl.when(i == 0)(make_scale)
        here = slice(top, top + size)
        turned[here] = pltpu.roll(scale_ref[here], LANES - (p * blocks + quarter * SUB), 1)
        for b in range(SUB):
            v = v_flat[pl.ds(top * SUB + b, size, stride=SUB), :] * turned[here, b : b + 1]
            vh[here, b * LANES : (b + 1) * LANES] = v.astype(jnp.bfloat16)
        values = dot(vh[here], wh[quarter]) + dot(vh[here], wl[quarter])

        @pl.when(quarter == 0)
        def _():
            z_ref[here] = values

        @pl.when(quarter > 0)
        def _():
            z_ref[here] += values

        @pl.when(quarter == QUARTERS - 1)
        def _():
            if late:
                picked = dot(pick_b[...], z_ref[...].astype(jnp.bfloat16)).reshape(-1, 2 * TILE, LAGS)
                zs_b[p] = picked[:owners].astype(jnp.bfloat16)
                zs_c[p] = picked[owners:].reshape(zs_c.shape[1:]).astype(jnp.bfloat16)
            else:
                picked = dot(pick_a[...], z_ref[here].astype(jnp.bfloat16))
                zs_a[p] = picked.reshape(zs_a.shape[1:]).astype(jnp.bfloat16)
            for shift in range(1, owners):
                target = lax.rem(t + shift, owners)
                if late:
                    scatter_copy(p, shift, "last", target, t).start()

                @pl.when(is_late(target) == late)
                def _():
                    scatter_copy(p, shift, "late" if late else "early", target, t).start()

        if late:
            @pl.when((quarter == QUARTERS - 1) & (p > 0))
            def _():
                reduce_period(p - 1)

    def step(n, _):
        i, kind = sub_step(n)

        @pl.when(kind == 0)
        def _():
            work(i, False)

        @pl.when(kind == 1)
        def _():
            work(i, True)

        return 0

    lax.fori_loop(0, total_steps, step, 0)
    reduce_period(mine - 1)

    for p in range(mine):
        for g in range(groups):
            for h in range(split):
                from_self = (me == g) & (place == me * split + h)

                @pl.when(jnp.logical_not(from_self))
                def _():
                    final_copy(p, 0, g, h).wait_recv()

    for g in range(groups):
        for p in range(mine):
            value = fr[g, 0, p]
            for h in range(1, split):
                value = value + fr[g, h, p]
            r = (g * mine + p) * own_rows
            gf[:, r : r + own_rows, :] = value

    highest = lax.Precision.HIGHEST
    rc, rs = gf[0, :, :lags], gf[0, :, lags:]
    ic, im_s = gf[1, :, :lags], gf[1, :, lags:]
    flip = (
        lax.broadcasted_iota(jnp.int32, (lags, lags), 0) + lax.broadcasted_iota(jnp.int32, (lags, lags), 1) == lags - 1
    ).astype(jnp.float32)
    pcos = pcos_ref[...]
    psin = psin_ref[...]
    factor = 1.0 / math.sqrt(periods * blocks * LANES)

    def mix(m, v):
        return jnp.dot(m, v, precision=highest, preferred_element_type=jnp.float32)

    for side in range(2):
        if side == 0:
            real, imag = mix(rc - im_s, flip), mix(ic + rs, flip)
        else:
            real, imag = rc + im_s, ic - rs
        cols = slice(side * lags, (side + 1) * lags)
        out_ref[0, :, cols] = (mix(pcos, real) + mix(psin, imag)) * factor
        out_ref[1, :, cols] = (mix(pcos, imag) - mix(psin, real)) * factor

    for shift in range(1, groups):
        for copy in small_copies(shift):
            copy.wait_send()
    for shift in range(1, owners):
        gather_copy(shift, t).wait_send()

    def sent(i, _):
        for n in range(len(runs)):
            spectra_copy(n, i).wait_send()
        return 0

    lax.fori_loop(0, steps, sent, 0)

    def scattered(p, _):
        for shift in range(1, owners):
            scatter_copy(p, shift, "last", lax.rem(t + shift, owners), t).wait_send()
            scatter_copy(p, shift, "early", lax.rem(t + shift, owners), t).wait_send()
        for w in range(wide):
            @pl.when(jnp.logical_not((plane == me) & (w == place)))
            def _():
                final_copy(p, w, me, part).wait_send()
        return 0

    lax.fori_loop(0, mine, scattered, 0)


def per_device(spectra, flags, poly_index, delay_model, partner_order):
    local, periods, depth, _, channels = spectra.shape
    groups = lax.axis_size("stn")
    owners = lax.axis_size("tm")
    stations = local * groups
    mine = periods // groups
    blocks = flags.shape[-1]
    split = owners // stations
    wide = groups * split
    own_rows = stations // wide
    span = stations // split
    rows = stations * stations
    pairs = stations * (stations + 1) // 2
    steps = mine * QUARTERS
    width = channels // QUARTERS
    lanes = LANES
    assert channels == blocks * LANES and width == SUB * LANES and stations % TILE == 0 and mine * blocks <= lanes

    x = spectra.reshape(local, periods, depth, 2, blocks, LANES).transpose(0, 1, 2, 4, 3, 5)
    x = x.reshape(local, periods, depth, 2 * blocks, LANES)
    high, low = lag_tables(channels)
    pick_a, pick_b = pick_matrices(stations, groups, owners)
    units = span // TILE
    runs = arrivals(stations, groups)
    pcos, psin = period_tables(periods, own_rows)
    any_spec = pl.BlockSpec(memory_space=pl.ANY)
    smem = pl.BlockSpec(memory_space=pltpu.SMEM)
    f32, bf16, i32 = jnp.float32, jnp.bfloat16, jnp.int32
    spectra_rows = stations * depth
    dma = pltpu.SemaphoreType.DMA
    out = pl.pallas_call(
        functools.partial(kernel, (groups, owners, stations, periods, depth, blocks)),
        out_shape=jax.ShapeDtypeStruct((2, own_rows * periods, LAGS), f32),
        in_specs=[any_spec, any_spec, any_spec, smem, smem] + [any_spec] * 6,
        out_specs=pl.BlockSpec(memory_space=pltpu.VMEM),
        scratch_shapes=[
            pltpu.VMEM((stations, mine, depth, 2 * blocks, LANES), bf16),
            pltpu.VMEM(flags.shape, i32),
            pltpu.VMEM((local, depth, periods), i32),
            pltpu.VMEM(pcos.shape, f32),
            pltpu.VMEM(psin.shape, f32),
            pltpu.VMEM((groups, local, depth, lanes), bf16),
            pltpu.VMEM((groups, local, depth, LANES), f32),
            pltpu.VMEM((groups, local, depth, lanes), bf16),
            pltpu.VMEM((groups, local, depth, LANES), f32),
            pltpu.VMEM((owners, groups, local, depth, lanes), bf16),
            pltpu.VMEM((stations, owners * depth, lanes), f32),
            pltpu.VMEM((spectra_rows, lanes), f32),
            pltpu.VMEM((pairs, SUB, lanes), f32),
            pltpu.VMEM((pairs, lanes), f32),
            pltpu.VMEM((rows, lanes), f32),
            pltpu.VMEM((rows, lanes), f32),
            pltpu.VMEM((spectra_rows, lanes, LANES), f32),
            pltpu.VMEM((mine, spectra_rows, LANES), f32),
            pltpu.VMEM((mine, spectra_rows, LANES), f32),
            pltpu.VMEM((mine, spectra_rows, LANES), f32),
            pltpu.VMEM((mine, spectra_rows, SUB, LANES), f32),
            pltpu.VMEM((mine, spectra_rows, SUB, LANES), f32),
            pltpu.VMEM(high.shape, bf16),
            pltpu.VMEM(low.shape, bf16),
            pltpu.VMEM(pick_a.shape[1:], bf16),
            pltpu.VMEM(pick_b.shape[1:], bf16),
            pltpu.VMEM((QUARTERS,) + high.shape, bf16),
            pltpu.VMEM((QUARTERS,) + low.shape, bf16),
            pltpu.VMEM((2 * depth, 2 * SUB, LANES), f32),
            pltpu.VMEM((QUARTERS, depth, stations, SUB, LANES), f32),
            pltpu.VMEM((QUARTERS, depth, stations, SUB, LANES), f32),
            pltpu.VMEM((QUARTERS, depth, stations, SUB, LANES), f32),
            pltpu.VMEM((QUARTERS, depth, stations, SUB, LANES), f32),
            pltpu.VMEM((rows, SUB, LANES), f32),
            pltpu.VMEM((rows, width), bf16),
            pltpu.VMEM((rows, LAGS), f32),
            pltpu.VMEM((mine, owners, units - 1, 2 * TILE, LAGS), bf16),
            pltpu.VMEM((mine, owners, 2 * TILE, LAGS), bf16),
            pltpu.VMEM((mine, TILE * split, units - 1, 2 * TILE, LAGS), bf16),
            pltpu.VMEM((mine, owners, units, 2 * TILE, LAGS), bf16),
            pltpu.VMEM((units, 2 * TILE, LAGS), f32),
            pltpu.VMEM((mine, wide, 2, own_rows, LAGS), f32),
            pltpu.VMEM((groups, split, mine, 2, own_rows, LAGS), f32),
            pltpu.VMEM((2, periods * own_rows, LAGS), f32),
            dma((8,)),
            dma((steps,)),
            dma((len(runs), steps)),
            dma((len(runs), steps)),
            dma((2, groups)),
            dma((2, groups)),
            dma((owners,)),
            dma((owners,)),
            dma((2, mine, owners)),
            dma((2, mine, owners)),
            dma((mine, wide)),
            dma((groups, split, mine)),
        ],
        compiler_params=pltpu.CompilerParams(collective_id=0, has_side_effects=True, vmem_limit_bytes=60 << 20),
        name="correlate",
    )(
        x, flags, poly_index.transpose(0, 2, 1), delay_model.T, partner_order,
        jnp.asarray(high), jnp.asarray(low), jnp.asarray(pick_a), jnp.asarray(pick_b), pcos, psin,
    )
    return out.reshape(2, own_rows, periods, LAGS)


def solution(mesh):
    return jax.shard_map(
        per_device,
        mesh=mesh,
        in_specs=(
            P("stn", None, "tm", None, None),
            P("stn", None, "tm", None),
            P("stn", None, "tm"),
            P(),
            P(),
        ),
        out_specs=P(None, ("stn", "tm"), None, None),
        check_vma=False,
    )
```

```python
import functools
import math

import jax
import jax.numpy as jnp
import numpy as np
from jax import lax
from jax.experimental import pallas as pl
from jax.experimental.pallas import tpu as pltpu
from jax.sharding import PartitionSpec as P

LAGS = 256
QUARTERS = 4
LANES = 128
SUB = 8
TILE = 4
MESH = pl.DeviceIdType.MESH


def lag_tables(channels):
    lags = np.arange(1, LAGS // 2 + 1)
    j = np.arange(channels // QUARTERS)
    angle = (j[:, None] * lags[None, :] % channels) * (2.0 * np.pi / channels)
    table = np.concatenate([np.cos(angle), np.sin(angle)], axis=1).astype(np.float32)
    high = table.astype(jnp.bfloat16)
    low = (table - high.astype(np.float32)).astype(jnp.bfloat16)
    return high, low


def pair_rows(stations):
    last = stations - TILE
    kinds = []
    real, imag, order = {}, {}, {}
    row = 0
    for late in (False, True):
        off = [(x, y) for x in range(0, stations, TILE) for y in range(x + TILE, stations, TILE) if (y == last) == late]
        same = [last] if late else list(range(0, last, TILE))
        for part in (real, imag):
            skip = 0 if part is real else 1
            start = row
            keys = [(x + i, y + j) for x, y in off for i in range(TILE) for j in range(TILE)]
            keys += [(x + i, x + j) for x in same for i in range(TILE) for j in range(i + skip, TILE)]
            for key in keys:
                part[key] = row
                row += 1
                if part is real:
                    order[key] = len(order)
        kinds.append((off, same))
    return kinds, real, imag, order


def late_first(local):
    return local // 4 if local >= 2 * TILE else 0


def relative(station, plane, groups, local):
    slot = (station // local - plane) % groups
    place = station % local
    return slot * local + (place if slot == 0 else (place + late_first(local)) % local)


def pick_matrices(stations, groups, owners):
    _, real, imag, _ = pair_rows(stations)
    split = owners // stations
    wide = groups * split
    local = stations // groups
    units = stations // split // TILE
    rows = stations * stations
    early = (stations - TILE) ** 2
    pick_a = np.zeros((groups, owners, units - 1, 2, TILE, rows), np.float32)
    pick_b = np.zeros((groups, owners, 2, TILE, rows), np.float32)
    pick_c = np.zeros((groups, TILE * split, units - 1, 2, TILE, rows), np.float32)
    for g in range(groups):
        for t in range(owners):
            a = relative(t % wide // split * local + t // wide, g, groups, local)
            late = a >= stations - TILE
            for u in range(units):
                for n in range(TILE):
                    b = (t % split * units + u) * TILE + n
                    key = (min(a, b), max(a, b))
                    if u == units - 1:
                        target = pick_b[g, t]
                    elif late:
                        target = pick_c[g, (a - stations + TILE) * split + t % split, u]
                    else:
                        target = pick_a[g, t, u]
                    target[0, n, real[key]] = 1.0
                    if a != b:
                        target[1, n, imag[key]] = 1.0 if a < b else -1.0
    pick_a = pick_a.reshape(groups, -1, rows)
    assert not pick_a[:, :, early:].any()
    pick_b = np.concatenate([pick_b.reshape(groups, -1, rows), pick_c.reshape(groups, -1, rows)], axis=1)
    return pick_a[:, :, :early].astype(jnp.bfloat16), pick_b.astype(jnp.bfloat16)


def arrivals(stations, groups):
    local = stations // groups
    runs = []
    for shift in range(1, groups):
        slot = groups - shift
        turn = late_first(local)
        places = [((i - turn) % local, slot * local + i) for i in range(local)]
        for source, here in places:
            late = here >= stations - TILE
            if runs and runs[-1][:2] == (late, shift) and source == runs[-1][2] + runs[-1][3]:
                runs[-1] = (late, shift, runs[-1][2], runs[-1][3] + 1, runs[-1][4])
            else:
                runs.append((late, shift, source, 1, here))
    return runs


def period_tables(periods, rows):
    idx = np.arange(periods)
    angle = (idx[:, None] * idx[None, :] % periods) * (2.0 * np.pi / periods)
    eye = np.eye(rows)

    def table(m):
        wide = np.einsum("rp,nm->nrpm", m, eye).reshape(rows * periods, periods * rows)
        return jnp.asarray(wide.astype(np.float32))

    return table(np.cos(angle)), table(np.sin(angle))


def dot(a, b):
    return jnp.dot(a, b, preferred_element_type=jnp.float32)


SIN = [(-1) ** n * math.pi ** (2 * n + 1) / math.factorial(2 * n + 1) for n in range(6)]
COS = [(-1) ** n * math.pi ** (2 * n) / math.factorial(2 * n) for n in range(7)]


def cos_sin_turns(turns):
    frac = turns - jnp.floor(turns + 0.5)
    square = frac * frac
    s = jnp.full_like(square, SIN[-1])
    for coef in SIN[-2::-1]:
        s = s * square + coef
    s = s * frac
    c = jnp.full_like(square, COS[-1])
    for coef in COS[-2::-1]:
        c = c * square + coef
    return 1.0 - 2.0 * (s * s), 2.0 * (s * c)


def kernel(
    sizes,
    x_hbm, flags_hbm, index_hbm, model_ref, partner_ref, high_hbm, low_hbm, pick_a_hbm, pick_b_hbm, pcos_hbm, psin_hbm,
    out_ref,
    xall, flags, index_ref, pcos_ref, psin_ref, wsend, dsend, wbuf, dbuf, wall, wf, wrow, acc, counts, scale_ref, turned,
    wide_w, dsplat, step_c, step_s, base_c, base_s, th, tl, pick_a, pick_b, wh, wl, tmp, yr, yi, ys, yd, v_ref, vh, z_ref,
    zs_a, zs_b, zs_c, rb, red, fs, fr, gf,
    table_sem, own_sem, xs_sem, xr_sem, ws_sem, wr_sem, gs_sem, gr_sem, rs_sem, rr_sem, fs_sem, fr_sem, up_sem, down_sem,
):
    groups, owners, stations, periods, depth, blocks = sizes
    local = stations // groups
    mine = periods // groups
    split = owners // stations
    wide = groups * split
    span = stations // split
    own_rows = stations // wide
    rows = stations * stations
    steps = mine * QUARTERS
    lags = LAGS // 2
    me = lax.axis_index("stn")
    t = lax.axis_index("tm")
    home = t // wide
    place = t % wide
    plane = place // split
    part = t % split
    units = span // TILE
    early = (stations - TILE) ** 2
    turn_by = late_first(local)
    runs = arrivals(stations, groups)
    kinds, real_row, imag_row, pair_order = pair_rows(stations)
    pairs = len(real_row)

    def relative_here(station):
        slot = (station // local - me + groups) % groups
        return slot * local + (station % local + (slot + groups - 1) // groups * turn_by) % local

    mine_a = relative_here(plane * local + home)
    total_steps = 2 * steps
    full = 2 * (mine - 1) * QUARTERS

    def sub_step(n):
        last = n // full if full else 1
        i = (1 - last) * (n // 2) + last * ((mine - 1) * QUARTERS + (n + QUARTERS * 2 - full % (QUARTERS * 2)) % QUARTERS)
        kind = (1 - last) * (n % 2) + last * ((n + total_steps - full) // QUARTERS - total_steps // QUARTERS)
        return i, kind

    def band(i):
        return pl.ds(pl.multiple_of((i % QUARTERS) * 2 * SUB, 2 * SUB), 2 * SUB)

    own_copy = pltpu.make_async_copy(x_hbm.at[:, pl.ds(me * mine, mine)], xall.at[pl.ds(0, local)], own_sem)

    def all_of(ref, sem):
        return pltpu.make_async_copy(ref, ref, sem)

    tables = [
        pltpu.make_async_copy(source, target, table_sem.at[n])
        for n, (source, target) in enumerate((
            (flags_hbm, flags), (index_hbm, index_ref), (high_hbm, th), (low_hbm, tl),
            (pick_a_hbm.at[me], pick_a), (pick_b_hbm.at[me], pick_b), (pcos_hbm, pcos_ref), (psin_hbm, psin_ref),
        ))
    ]
    barrier = pltpu.get_barrier_semaphore()
    is_root = (me == 0) & (t == 0)
    others = groups * owners - 1

    def tell(sem, peer):
        pl.semaphore_signal(sem, inc=1, device_id=peer, device_id_type=MESH)

    def tell_all(sem):
        def one(n, _):
            tell(sem, {"stn": (n + 1) // owners, "tm": (n + 1) % owners})
            return 0

        lax.fori_loop(0, others, one, 0)

    for shift in range(1, groups):
        tell(barrier, {"stn": lax.rem(me + shift, groups)})

    @pl.when(is_root)
    def _():
        tell_all(barrier)

    for copy in tables:
        copy.start()

    own_copy.start()

    @pl.when(is_root)
    def _():
        pl.semaphore_wait(barrier, groups - 1)

    @pl.when(jnp.logical_not(is_root))
    def _():
        pl.semaphore_wait(barrier, groups)
        tell(up_sem, {"stn": 0, "tm": 0})


    def small_copies(shift):
        target = lax.rem(me + shift, groups)
        return [
            pltpu.make_async_remote_copy(
                src_ref=ref.at[target], dst_ref=buf.at[groups - shift], send_sem=ws_sem.at[n, shift - 1],
                recv_sem=wr_sem.at[n, shift - 1], device_id={"stn": target}, device_id_type=MESH,
            )
            for n, (ref, buf) in enumerate(((wsend, wbuf), (dsend, dbuf)))
        ]

    def arrival(i, late):
        last = i // ((mine - 1) * QUARTERS) if mine > 1 else 1
        return i + last * QUARTERS * int(late)

    def spectra_copy(n, i):
        late, shift, source, count, here = runs[n]
        target = lax.rem(me + shift, groups)
        return pltpu.make_async_remote_copy(
            src_ref=x_hbm.at[pl.ds(source, count), target * mine + i // QUARTERS, :, band(i), :],
            dst_ref=xall.at[pl.ds(here, count), i // QUARTERS, :, band(i), :],
            send_sem=xs_sem, recv_sem=xr_sem.at[arrival(i, late)],
            device_id={"stn": target}, device_id_type=MESH,
        )

    def start_spectra(n, _):
        i, kind = sub_step(n)
        for late in (False, True):

            @pl.when(kind == int(late))
            def _():
                for r in range(len(runs)):
                    if runs[r][0] == late:
                        spectra_copy(r, i).start()

        return 0

    lax.fori_loop(0, 2, start_spectra, 0)

    tables[1].wait()
    index = index_ref[...]

    def look_up(n, coef):
        here = index == n
        return tuple(jnp.where(here, model_ref[c, n], coef[c]) for c in range(3))

    none = jnp.zeros(index.shape, jnp.float32)
    coef = lax.fori_loop(0, model_ref.shape[1], look_up, (none, none, none), unroll=4)
    total = depth * owners
    times = (
        lax.broadcasted_iota(jnp.int32, index.shape, 2) * total + t * depth + lax.broadcasted_iota(jnp.int32, index.shape, 1)
    ).astype(jnp.float32)
    moment = times / float(periods * total)
    delay = (coef[0] + coef[1] * moment + coef[2] * moment * moment) * (0.5 / (blocks * LANES))
    dsend[...] = jnp.zeros_like(dsend)
    for g in range(groups):
        dsend[g, :, :, :mine] = delay[:, :, g * mine : (g + 1) * mine]
    tables[0].wait()
    for g in range(groups):
        pieces = [flags[:, g * mine + p].astype(jnp.float32) for p in range(mine)]
        gap = wsend.shape[-1] - mine * blocks
        if gap:
            pieces.append(jnp.ones(pieces[0].shape[:-1] + (gap,), jnp.float32))
        both = jnp.concatenate(pieces, axis=-1) if len(pieces) > 1 else pieces[0]
        wsend[g] = (1.0 - both).astype(jnp.bfloat16)
    wbuf[0] = wsend[me]
    dbuf[0] = dsend[me]
    for shift in range(1, groups):
        for copy in small_copies(shift):
            copy.start()
    lax.fori_loop(2, total_steps, start_spectra, 0)

    for copy in tables[2:]:
        copy.wait()
    lag = lax.broadcasted_iota(jnp.int32, (1, lags), 1) + 1
    for quarter in range(QUARTERS):
        turn = (lag * quarter) % 4
        cq = jnp.where(turn == 0, 1.0, jnp.where(turn == 2, -1.0, 0.0))
        sq = jnp.where(turn == 1, 1.0, jnp.where(turn == 3, -1.0, 0.0))

        def turn_rows(n, _, quarter=quarter, cq=cq, sq=sq):
            r = pl.ds(pl.multiple_of(n * LANES, LANES), LANES)
            for source, target in ((th, wh), (tl, wl)):
                c = source[r, :lags].astype(jnp.float32)
                s = source[r, lags:].astype(jnp.float32)
                target[quarter, r, :lags] = (c * cq - s * sq).astype(jnp.bfloat16)
                target[quarter, r, lags:] = (s * cq + c * sq).astype(jnp.bfloat16)
            return 0

        lax.fori_loop(0, th.shape[0] // LANES, turn_rows, 0)

    for shift in range(1, groups):
        for copy in small_copies(shift):
            copy.wait_recv()

    @pl.when(is_root)
    def _():
        pl.semaphore_wait(up_sem, others)
        tell_all(down_sem)

    @pl.when(jnp.logical_not(is_root))
    def _():
        pl.semaphore_wait(down_sem, 1)

    def gather_copy(shift, source):
        return pltpu.make_async_remote_copy(
            src_ref=wbuf, dst_ref=wall.at[source], send_sem=gs_sem, recv_sem=gr_sem,
            device_id={"tm": lax.rem(t + shift, owners)}, device_id_type=MESH,
        )

    for shift in range(1, owners):
        gather_copy(shift, t).start()
    wall[t] = wbuf[...]

    for g in range(groups):
        for l in range(local):
            r = (g * local + (l + turn_by * min(g, 1)) % local) * depth
            wrow[r : r + depth, :] = wbuf[g, l].astype(jnp.float32)
            d = dbuf[g, l]
            for p in range(mine):
                dsplat[p, r : r + depth, :] = jnp.broadcast_to(d[:, p : p + 1], d.shape)
    c, s = cos_sin_turns(dsplat[...] * float(SUB * LANES))
    step_c[...] = c
    step_s[...] = s
    channel = (
        lax.broadcasted_iota(jnp.int32, (SUB, LANES), 0) * LANES + lax.broadcasted_iota(jnp.int32, (SUB, LANES), 1)
    ).astype(jnp.float32)
    spectra = stations * depth

    def start_phases(p):
        def one(r, _):
            c, s = cos_sin_turns(dsplat[p, pl.ds(r, 1), :] * channel)
            base_c[r] = c
            base_s[r] = s
            return 0

        lax.fori_loop(0, spectra, one, 0, unroll=8)

    w_t = wrow[...].T
    for r in range(spectra):
        wide_w[r] = jnp.broadcast_to(w_t[:, r : r + 1], (w_t.shape[0], LANES))

    acc_flat = acc.reshape(pairs * SUB, LANES)
    v_flat = v_ref.reshape(rows * SUB, LANES)

    def make_scale():
        all_of(wall.at[pl.ds(0, owners - 1)], gr_sem).wait()
        for n in range(owners):
            for g in range(groups):
                turn = turn_by * min(g, 1)
                value = wall[n, g].astype(jnp.float32)
                at = slice(n * depth, (n + 1) * depth)
                wf[g * local + turn : (g + 1) * local, at, :] = value[: local - turn]
                if turn:
                    wf[g * local : g * local + turn, at, :] = value[local - turn :]
        for a in range(stations):
            for b0 in range(a // TILE * TILE, stations, TILE):
                b = max(a, b0)
                count = b0 + TILE - b
                product = wf[a][None] * wf[b : b + count]
                m = pair_order[a, b]
                acc[m : m + count] = jnp.sum(product.reshape(count, owners * depth // SUB, SUB, LANES), axis=1)
        count = acc_flat[pl.ds(0, pairs, stride=SUB), :]
        for b in range(1, SUB):
            count = count + acc_flat[pl.ds(b, pairs, stride=SUB), :]
        counts[...] = 1.0 / jnp.sqrt(jnp.maximum(count, 1.0))
        for off, same in kinds:
            pieces = []
            if off:
                x, y = off[0]
                n = len(off) * TILE * TILE
                pieces += [(real_row[x, y], pair_order[x, y], n), (imag_row[x, y], pair_order[x, y], n)]
            for x in same:
                if x == same[0]:
                    n = len(same) * TILE * (TILE + 1) // 2
                    pieces.append((real_row[x, x], pair_order[x, x], n))
                for i in range(TILE - 1):
                    pieces.append((imag_row[x + i, x + i + 1], pair_order[x + i, x + i + 1], TILE - 1 - i))
            for row, source, n in pieces:
                scale_ref[row : row + n, :] = counts[source : source + n, :]

    def station_of(target):
        return relative_here(target % wide // split * local + target // wide)

    def scatter_copy(p, shift, what, target, source):
        if what == "last":
            src, dst = zs_b.at[p, target], rb.at[p, source, units - 1]
        elif what == "early":
            src, dst = zs_a.at[p, target], rb.at[p, source, pl.ds(0, units - 1)]
        else:
            late = (station_of(target) + TILE) % stations * split + target % split
            src, dst = zs_c.at[p, late], rb.at[p, source, pl.ds(0, units - 1)]
        return pltpu.make_async_remote_copy(
            src_ref=src, dst_ref=dst, send_sem=rs_sem,
            recv_sem=rr_sem.at[p], device_id={"tm": lax.rem(t + shift, owners)}, device_id_type=MESH,
        )

    def is_late(target):
        return station_of(target) >= stations - TILE

    def final_copy(p, w, source, piece):
        return pltpu.make_async_remote_copy(
            src_ref=fs.at[w, p], dst_ref=fr.at[source * split + piece, p], send_sem=fs_sem,
            recv_sem=fr_sem, device_id={"stn": plane, "tm": home * wide + w}, device_id_type=MESH,
        )

    def reduce_period(p):
        all_of(rb.at[p, pl.ds(0, owners - 1)], rr_sem.at[p]).wait()
        late = jnp.where(is_late(t), 1.0, 0.0)
        first = zs_a[p, t].astype(jnp.float32)
        first += late * zs_c[p, (mine_a % TILE) * split + part].astype(jnp.float32)
        last = zs_b[p, t].astype(jnp.float32)
        for shift in range(1, owners):
            source = lax.rem(t + owners - shift, owners)
            first += rb[p, source, : units - 1].astype(jnp.float32)
            last += rb[p, source, units - 1].astype(jnp.float32)
        red[: units - 1] = first
        red[units - 1] = last
        for w in range(wide):
            for n in range(own_rows):
                b = relative_here(partner_ref[w * own_rows + n])
                if split > 1:
                    keep = jnp.where(b // span == part, 1.0, 0.0)
                    b = b % span
                for ri in range(2):
                    row = red[b // TILE, pl.ds(ri * TILE + b % TILE, 1), :]
                    fs[w, p, ri, n : n + 1, :] = row * keep if split > 1 else row
        for w in range(wide):
            to_self = (plane == me) & (w == place)

            @pl.when(to_self)
            def _():
                fr[me * split + part, p] = fs[w, p]

            @pl.when(jnp.logical_not(to_self))
            def _():
                final_copy(p, w, me, part).start()

    half = TILE // 2

    def work(i, late):
        p = i // QUARTERS
        quarter = i % QUARTERS
        at = pl.ds(pl.multiple_of(p * blocks + quarter * SUB, SUB), SUB)
        first_station = stations - TILE if late else 0
        off, same = kinds[late]
        top, size = (early, rows - early) if late else (0, early)

        def wait_spectra(low, high):
            piece = xall.at[pl.ds(low, high - low), p, :, band(i), :]
            all_of(piece, xr_sem.at[arrival(i, late)]).wait()

        if late:
            @pl.when(i >= steps - QUARTERS)
            def _():
                wait_spectra(stations - TILE, stations)
        else:
            @pl.when(i < steps - QUARTERS)
            def _():
                wait_spectra(local, stations)

            @pl.when(i >= steps - QUARTERS)
            def _():
                wait_spectra(local, stations - TILE)

            @pl.when(quarter == 0)
            def _():
                start_phases(p)

        def rotate(n, _):
            for j in range(2):
                s = first_station + n * 2 + j
                for k in range(depth):
                    r = s * depth + k
                    tmp[j * depth + k] = xall[s, p, k, band(i), :].astype(jnp.float32)
                    real = tmp[j * depth + k, pl.ds(0, SUB, stride=2), :]
                    imag = tmp[j * depth + k, pl.ds(1, SUB, stride=2), :]
                    c = base_c[r]
                    sn = base_s[r]
                    w = wide_w[r, at, :]
                    new_real = (w * (real * c + imag * sn)).astype(jnp.bfloat16).astype(jnp.float32)
                    new_imag = (w * (imag * c - real * sn)).astype(jnp.bfloat16).astype(jnp.float32)
                    yr[quarter, k, s] = new_real
                    yi[quarter, k, s] = new_imag
                    ys[quarter, k, s] = new_real + new_imag
                    yd[quarter, k, s] = new_real - new_imag
                    pc = step_c[p, pl.ds(r, 1), :]
                    ps = step_s[p, pl.ds(r, 1), :]
                    base_c[r] = c * pc - sn * ps
                    base_s[r] = sn * pc + c * ps
            return 0

        lax.fori_loop(0, (TILE if late else stations - TILE) // 2, rotate, 0)

        for x, y0 in off:
            for y in (y0, y0 + half):
                for k in range(depth):
                    ar, ai, asum = (ref[quarter, k, x : x + TILE][:, None] for ref in (yr, yi, ys))
                    br, bi, bdiff = (ref[quarter, k, y : y + half][None] for ref in (yr, yi, yd))
                    first = ar * br if k == 0 else first + ar * br
                    second = ai * bi if k == 0 else second + ai * bi
                    third = asum * bdiff if k == 0 else third + asum * bdiff
                real = first + second
                imag = third - (first - second)
                for n in range(TILE):
                    m = real_row[x + n, y]
                    q = imag_row[x + n, y]
                    v_ref[m : m + half] = real[n]
                    v_ref[q : q + half] = imag[n]
        for x in same:
            for a in range(x, x + TILE):
                n = x + TILE - a
                for k in range(depth):
                    ar, ai = yr[quarter, k, a], yi[quarter, k, a]
                    term = ar * ar + ai * ai
                    auto = term if k == 0 else auto + term
                    if n > 1:
                        br, bi, bdiff = (ref[quarter, k, a + 1 : a + n] for ref in (yr, yi, yd))
                        asum = ys[quarter, k, a]
                        first = ar * br if k == 0 else first + ar * br
                        second = ai * bi if k == 0 else second + ai * bi
                        third = asum * bdiff if k == 0 else third + asum * bdiff
                m = real_row[a, a]
                v_ref[m] = auto
                if n > 1:
                    q = imag_row[a, a + 1]
                    v_ref[m + 1 : m + n] = first + second
                    v_ref[q : q + n - 1] = third - (first - second)

        if not late:
            pl.when(i == 0)(make_scale)
        here = slice(top, top + size)
        turned[here] = pltpu.roll(scale_ref[here], LANES - (p * blocks + quarter * SUB), 1)
        for b in range(SUB):
            v = v_flat[pl.ds(top * SUB + b, size, stride=SUB), :] * turned[here, b : b + 1]
            vh[here, b * LANES : (b + 1) * LANES] = v.astype(jnp.bfloat16)
        values = dot(vh[here], wh[quarter]) + dot(vh[here], wl[quarter])

        @pl.when(quarter == 0)
        def _():
            z_ref[here] = values

        @pl.when(quarter > 0)
        def _():
            z_ref[here] += values

        @pl.when(quarter == QUARTERS - 1)
        def _():
            if late:
                picked = dot(pick_b[...], z_ref[...].astype(jnp.bfloat16)).reshape(-1, 2 * TILE, LAGS)
                zs_b[p] = picked[:owners].astype(jnp.bfloat16)
                zs_c[p] = picked[owners:].reshape(zs_c.shape[1:]).astype(jnp.bfloat16)
            else:
                picked = dot(pick_a[...], z_ref[here].astype(jnp.bfloat16))
                zs_a[p] = picked.reshape(zs_a.shape[1:]).astype(jnp.bfloat16)
            for shift in range(1, owners):
                target = lax.rem(t + shift, owners)
                if late:
                    scatter_copy(p, shift, "last", target, t).start()

                @pl.when(is_late(target) == late)
                def _():
                    scatter_copy(p, shift, "late" if late else "early", target, t).start()

        if late:
            @pl.when((quarter == QUARTERS - 1) & (p > 0))
            def _():
                reduce_period(p - 1)

    def step(n, _):
        i, kind = sub_step(n)

        @pl.when(kind == 0)
        def _():
            work(i, False)

        @pl.when(kind == 1)
        def _():
            work(i, True)

        return 0

    own_copy.wait()
    lax.fori_loop(0, total_steps, step, 0)
    for shift in range(1, groups):
        for copy in small_copies(shift):
            copy.wait_send()
    all_of(wall.at[pl.ds(0, owners - 1)], gs_sem).wait()
    all_of(xall.at[pl.ds(local, stations - local)], xs_sem).wait()
    reduce_period(mine - 1)
    all_of(rb.at[:, pl.ds(0, owners - 1)], rs_sem).wait()

    @pl.when(plane == me)
    def _():
        all_of(fr.at[pl.ds(0, wide - 1)], fr_sem).wait()
        all_of(fs.at[pl.ds(0, wide - 1)], fs_sem).wait()

    @pl.when(plane != me)
    def _():
        all_of(fr, fr_sem).wait()
        all_of(fs, fs_sem).wait()

    for g in range(groups):
        for p in range(mine):
            value = fr[g * split, p]
            for h in range(1, split):
                value = value + fr[g * split + h, p]
            r = (g * mine + p) * own_rows
            gf[:, r : r + own_rows, :] = value

    highest = lax.Precision.HIGHEST
    rc, rs = gf[0, :, :lags], gf[0, :, lags:]
    ic, im_s = gf[1, :, :lags], gf[1, :, lags:]
    flip = (
        lax.broadcasted_iota(jnp.int32, (lags, lags), 0) + lax.broadcasted_iota(jnp.int32, (lags, lags), 1) == lags - 1
    ).astype(jnp.float32)
    pcos = pcos_ref[...]
    psin = psin_ref[...]
    factor = 1.0 / math.sqrt(periods * blocks * LANES)

    def mix(m, v):
        return jnp.dot(m, v, precision=highest, preferred_element_type=jnp.float32)

    for side in range(2):
        if side == 0:
            real, imag = mix(rc - im_s, flip), mix(ic + rs, flip)
        else:
            real, imag = rc + im_s, ic - rs
        cols = slice(side * lags, (side + 1) * lags)
        out_ref[0, :, cols] = (mix(pcos, real) + mix(psin, imag)) * factor
        out_ref[1, :, cols] = (mix(pcos, imag) - mix(psin, real)) * factor


def per_device(spectra, flags, poly_index, delay_model, partner_order):
    local, periods, depth, _, channels = spectra.shape
    groups = lax.axis_size("stn")
    owners = lax.axis_size("tm")
    stations = local * groups
    mine = periods // groups
    blocks = flags.shape[-1]
    split = owners // stations
    wide = groups * split
    own_rows = stations // wide
    span = stations // split
    rows = stations * stations
    pairs = stations * (stations + 1) // 2
    steps = mine * QUARTERS
    width = channels // QUARTERS
    lanes = LANES
    assert channels == blocks * LANES and width == SUB * LANES and stations % TILE == 0 and mine * blocks <= lanes

    x = spectra.reshape(local, periods, depth, 2, blocks, LANES).transpose(0, 1, 2, 4, 3, 5)
    x = x.reshape(local, periods, depth, 2 * blocks, LANES)
    high, low = lag_tables(channels)
    pick_a, pick_b = pick_matrices(stations, groups, owners)
    units = span // TILE
    runs = arrivals(stations, groups)
    pcos, psin = period_tables(periods, own_rows)
    any_spec = pl.BlockSpec(memory_space=pl.ANY)
    smem = pl.BlockSpec(memory_space=pltpu.SMEM)
    f32, bf16, i32 = jnp.float32, jnp.bfloat16, jnp.int32
    spectra_rows = stations * depth
    dma = pltpu.SemaphoreType.DMA
    out = pl.pallas_call(
        functools.partial(kernel, (groups, owners, stations, periods, depth, blocks)),
        out_shape=jax.ShapeDtypeStruct((2, own_rows * periods, LAGS), f32),
        in_specs=[any_spec, any_spec, any_spec, smem, smem] + [any_spec] * 6,
        out_specs=pl.BlockSpec(memory_space=pltpu.VMEM),
        scratch_shapes=[
            pltpu.VMEM((stations, mine, depth, 2 * blocks, LANES), bf16),
            pltpu.VMEM(flags.shape, i32),
            pltpu.VMEM((local, depth, periods), i32),
            pltpu.VMEM(pcos.shape, f32),
            pltpu.VMEM(psin.shape, f32),
            pltpu.VMEM((groups, local, depth, lanes), bf16),
            pltpu.VMEM((groups, local, depth, LANES), f32),
            pltpu.VMEM((groups, local, depth, lanes), bf16),
            pltpu.VMEM((groups, local, depth, LANES), f32),
            pltpu.VMEM((owners, groups, local, depth, lanes), bf16),
            pltpu.VMEM((stations, owners * depth, lanes), f32),
            pltpu.VMEM((spectra_rows, lanes), f32),
            pltpu.VMEM((pairs, SUB, lanes), f32),
            pltpu.VMEM((pairs, lanes), f32),
            pltpu.VMEM((rows, lanes), f32),
            pltpu.VMEM((rows, lanes), f32),
            pltpu.VMEM((spectra_rows, lanes, LANES), f32),
            pltpu.VMEM((mine, spectra_rows, LANES), f32),
            pltpu.VMEM((mine, spectra_rows, LANES), f32),
            pltpu.VMEM((mine, spectra_rows, LANES), f32),
            pltpu.VMEM((spectra_rows, SUB, LANES), f32),
            pltpu.VMEM((spectra_rows, SUB, LANES), f32),
            pltpu.VMEM(high.shape, bf16),
            pltpu.VMEM(low.shape, bf16),
            pltpu.VMEM(pick_a.shape[1:], bf16),
            pltpu.VMEM(pick_b.shape[1:], bf16),
            pltpu.VMEM((QUARTERS,) + high.shape, bf16),
            pltpu.VMEM((QUARTERS,) + low.shape, bf16),
            pltpu.VMEM((2 * depth, 2 * SUB, LANES), f32),
            pltpu.VMEM((QUARTERS, depth, stations, SUB, LANES), f32),
            pltpu.VMEM((QUARTERS, depth, stations, SUB, LANES), f32),
            pltpu.VMEM((QUARTERS, depth, stations, SUB, LANES), f32),
            pltpu.VMEM((QUARTERS, depth, stations, SUB, LANES), f32),
            pltpu.VMEM((rows, SUB, LANES), f32),
            pltpu.VMEM((rows, width), bf16),
            pltpu.VMEM((rows, LAGS), f32),
            pltpu.VMEM((mine, owners, units - 1, 2 * TILE, LAGS), bf16),
            pltpu.VMEM((mine, owners, 2 * TILE, LAGS), bf16),
            pltpu.VMEM((mine, TILE * split, units - 1, 2 * TILE, LAGS), bf16),
            pltpu.VMEM((mine, owners, units, 2 * TILE, LAGS), bf16),
            pltpu.VMEM((units, 2 * TILE, LAGS), f32),
            pltpu.VMEM((wide, mine, 2, own_rows, LAGS), f32),
            pltpu.VMEM((wide, mine, 2, own_rows, LAGS), f32),
            pltpu.VMEM((2, periods * own_rows, LAGS), f32),
            dma((8,)),
            dma,
            dma,
            dma((steps + QUARTERS,)),
            dma((2, groups - 1)),
            dma((2, groups - 1)),
            dma,
            dma,
            dma,
            dma((mine,)),
            dma,
            dma,
            pltpu.SemaphoreType.REGULAR,
            pltpu.SemaphoreType.REGULAR,
        ],
        compiler_params=pltpu.CompilerParams(collective_id=0, has_side_effects=True, vmem_limit_bytes=60 << 20),
        name="correlate",
    )(
        x, flags, poly_index.transpose(0, 2, 1), delay_model.T, partner_order,
        jnp.asarray(high), jnp.asarray(low), jnp.asarray(pick_a), jnp.asarray(pick_b), pcos, psin,
    )
    return out.reshape(2, own_rows, periods, LAGS)


def solution(mesh):
    return jax.shard_map(
        per_device,
        mesh=mesh,
        in_specs=(
            P("stn", None, "tm", None, None),
            P("stn", None, "tm", None),
            P("stn", None, "tm"),
            P(),
            P(),
        ),
        out_specs=P(None, ("stn", "tm"), None, None),
        check_vma=False,
    )
```

```python
import functools
import math

import jax
import jax.numpy as jnp
import numpy as np
from jax import lax
from jax.experimental import pallas as pl
from jax.experimental.pallas import tpu as pltpu
from jax.sharding import PartitionSpec as P

LAGS = 256
QUARTERS = 4
LANES = 128
SUB = 8
TILE = 4
MESH = pl.DeviceIdType.MESH


def lag_tables(channels):
    lags = np.arange(1, LAGS // 2 + 1)
    j = np.arange(channels // QUARTERS)
    angle = (j[:, None] * lags[None, :] % channels) * (2.0 * np.pi / channels)
    table = np.concatenate([np.cos(angle), np.sin(angle)], axis=1).astype(np.float32)
    high = table.astype(jnp.bfloat16)
    low = (table - high.astype(np.float32)).astype(jnp.bfloat16)
    return high, low


def pair_rows(stations):
    last = stations - TILE
    kinds = []
    real, imag, order = {}, {}, {}
    row = 0
    for late in (False, True):
        off = [(x, y) for x in range(0, stations, TILE) for y in range(x + TILE, stations, TILE) if (y == last) == late]
        same = [last] if late else list(range(0, last, TILE))
        for part in (real, imag):
            skip = 0 if part is real else 1
            start = row
            keys = [(x + i, y + j) for x, y in off for i in range(TILE) for j in range(TILE)]
            keys += [(x + i, x + j) for x in same for i in range(TILE) for j in range(i + skip, TILE)]
            for key in keys:
                part[key] = row
                row += 1
                if part is real:
                    order[key] = len(order)
        kinds.append((off, same))
    return kinds, real, imag, order


def late_first(local):
    return local // 4 if local >= 2 * TILE else 0


def relative(station, plane, groups, local):
    slot = (station // local - plane) % groups
    place = station % local
    return slot * local + (place if slot == 0 else (place + late_first(local)) % local)


def pick_matrices(stations, groups, owners):
    _, real, imag, _ = pair_rows(stations)
    split = owners // stations
    wide = groups * split
    local = stations // groups
    units = stations // split // TILE
    rows = stations * stations
    early = (stations - TILE) ** 2
    pick_a = np.zeros((groups, owners, units - 1, 2, TILE, rows), np.float32)
    pick_b = np.zeros((groups, owners, 2, TILE, rows), np.float32)
    pick_c = np.zeros((groups, TILE * split, units - 1, 2, TILE, rows), np.float32)
    for g in range(groups):
        for t in range(owners):
            a = relative(t % wide // split * local + t // wide, g, groups, local)
            late = a >= stations - TILE
            for u in range(units):
                for n in range(TILE):
                    b = (t % split * units + u) * TILE + n
                    key = (min(a, b), max(a, b))
                    if u == units - 1:
                        target = pick_b[g, t]
                    elif late:
                        target = pick_c[g, (a - stations + TILE) * split + t % split, u]
                    else:
                        target = pick_a[g, t, u]
                    target[0, n, real[key]] = 1.0
                    if a != b:
                        target[1, n, imag[key]] = 1.0 if a < b else -1.0
    pick_a = pick_a.reshape(groups, -1, rows)
    assert not pick_a[:, :, early:].any()
    pick_b = np.concatenate([pick_b.reshape(groups, -1, rows), pick_c.reshape(groups, -1, rows)], axis=1)
    return pick_a[:, :, :early].astype(jnp.bfloat16), pick_b.astype(jnp.bfloat16)


def arrivals(stations, groups):
    local = stations // groups
    runs = []
    for shift in range(1, groups):
        slot = groups - shift
        turn = late_first(local)
        places = [((i - turn) % local, slot * local + i) for i in range(local)]
        for source, here in places:
            late = here >= stations - TILE
            if runs and runs[-1][:2] == (late, shift) and source == runs[-1][2] + runs[-1][3]:
                runs[-1] = (late, shift, runs[-1][2], runs[-1][3] + 1, runs[-1][4])
            else:
                runs.append((late, shift, source, 1, here))
    return runs


def dot(a, b):
    return jnp.dot(a, b, preferred_element_type=jnp.float32)


SIN = [(-1) ** n * math.pi ** (2 * n + 1) / math.factorial(2 * n + 1) for n in range(6)]
COS = [(-1) ** n * math.pi ** (2 * n) / math.factorial(2 * n) for n in range(7)]


def cos_sin_turns(turns):
    frac = turns - jnp.floor(turns + 0.5)
    square = frac * frac
    s = jnp.full_like(square, SIN[-1])
    for coef in SIN[-2::-1]:
        s = s * square + coef
    s = s * frac
    c = jnp.full_like(square, COS[-1])
    for coef in COS[-2::-1]:
        c = c * square + coef
    return 1.0 - 2.0 * (s * s), 2.0 * (s * c)


def kernel(
    sizes,
    x_hbm, flags_hbm, index_hbm, model_hbm, partner_hbm, high_hbm, low_hbm, pick_a_hbm, pick_b_hbm,
    out_ref,
    xall, flags, index_ref, model_ref, partner_ref, wsend, dsend, wbuf, dbuf, wall, wf, wrow, acc, counts, scale_ref, turned,
    wide_w, dsplat, step_c, step_s, base_c, base_s, th, tl, pick_a, pick_b, wh, wl, tmp, yr, yi, ys, yd, v_ref, vh, z_ref,
    zs_a, zs_b, zs_c, rb, red, fs, fr, gf,
    table_sem, own_sem, xs_sem, xr_sem, ws_sem, wr_sem, gs_sem, gr_sem, rs_sem, rr_sem, fs_sem, fr_sem, up_sem, down_sem,
):
    groups, owners, stations, periods, depth, blocks = sizes
    local = stations // groups
    mine = periods // groups
    split = owners // stations
    wide = groups * split
    span = stations // split
    own_rows = stations // wide
    rows = stations * stations
    steps = mine * QUARTERS
    lags = LAGS // 2
    me = lax.axis_index("stn")
    t = lax.axis_index("tm")
    home = t // wide
    place = t % wide
    plane = place // split
    part = t % split
    units = span // TILE
    early = (stations - TILE) ** 2
    turn_by = late_first(local)
    runs = arrivals(stations, groups)
    kinds, real_row, imag_row, pair_order = pair_rows(stations)
    pairs = len(real_row)

    def relative_here(station):
        slot = (station // local - me + groups) % groups
        return slot * local + (station % local + (slot + groups - 1) // groups * turn_by) % local

    mine_a = relative_here(plane * local + home)
    total_steps = 2 * steps
    full = 2 * (mine - 1) * QUARTERS

    def sub_step(n):
        last = n // full if full else 1
        i = (1 - last) * (n // 2) + last * ((mine - 1) * QUARTERS + (n + QUARTERS * 2 - full % (QUARTERS * 2)) % QUARTERS)
        kind = (1 - last) * (n % 2) + last * ((n + total_steps - full) // QUARTERS - total_steps // QUARTERS)
        return i, kind

    def band(i):
        return pl.ds(pl.multiple_of((i % QUARTERS) * 2 * SUB, 2 * SUB), 2 * SUB)

    own_copy = pltpu.make_async_copy(x_hbm.at[:, pl.ds(me * mine, mine)], xall.at[pl.ds(0, local)], own_sem)

    def all_of(ref, sem):
        return pltpu.make_async_copy(ref, ref, sem)

    tables = [
        pltpu.make_async_copy(source, target, table_sem.at[n])
        for n, (source, target) in enumerate((
            (flags_hbm, flags), (index_hbm, index_ref), (high_hbm, th), (low_hbm, tl),
            (pick_a_hbm.at[me], pick_a), (pick_b_hbm.at[me], pick_b), (partner_hbm, partner_ref),
            (model_hbm, model_ref),
        ))
    ]
    barrier = pltpu.get_barrier_semaphore()
    is_root = (me == 0) & (t == 0)
    others = groups * owners - 1

    def tell(sem, peer):
        pl.semaphore_signal(sem, inc=1, device_id=peer, device_id_type=MESH)

    def tell_all(sem):
        def one(n, _):
            tell(sem, {"stn": (n + 1) // owners, "tm": (n + 1) % owners})
            return 0

        lax.fori_loop(0, others, one, 0)

    for shift in range(1, groups):
        tell(barrier, {"stn": lax.rem(me + shift, groups)})

    @pl.when(is_root)
    def _():
        tell_all(barrier)

    for copy in tables:
        copy.start()

    own_copy.start()

    @pl.when(is_root)
    def _():
        pl.semaphore_wait(barrier, groups - 1)

    @pl.when(jnp.logical_not(is_root))
    def _():
        pl.semaphore_wait(barrier, groups)
        tell(up_sem, {"stn": 0, "tm": 0})


    def small_copies(shift):
        target = lax.rem(me + shift, groups)
        return [
            pltpu.make_async_remote_copy(
                src_ref=ref.at[target], dst_ref=buf.at[groups - shift], send_sem=ws_sem.at[n, shift - 1],
                recv_sem=wr_sem.at[n, shift - 1], device_id={"stn": target}, device_id_type=MESH,
            )
            for n, (ref, buf) in enumerate(((wsend, wbuf), (dsend, dbuf)))
        ]

    def arrival(i, late):
        last = i // ((mine - 1) * QUARTERS) if mine > 1 else 1
        return i + last * QUARTERS * int(late)

    def spectra_copy(n, i):
        late, shift, source, count, here = runs[n]
        target = lax.rem(me + shift, groups)
        return pltpu.make_async_remote_copy(
            src_ref=x_hbm.at[pl.ds(source, count), target * mine + i // QUARTERS, :, band(i), :],
            dst_ref=xall.at[pl.ds(here, count), i // QUARTERS, :, band(i), :],
            send_sem=xs_sem, recv_sem=xr_sem.at[arrival(i, late)],
            device_id={"stn": target}, device_id_type=MESH,
        )

    def start_spectra(n, _):
        i, kind = sub_step(n)
        for late in (False, True):

            @pl.when(kind == int(late))
            def _():
                for r in range(len(runs)):
                    if runs[r][0] == late:
                        spectra_copy(r, i).start()

        return 0

    lax.fori_loop(0, 2, start_spectra, 0)

    tables[1].wait()
    tables[7].wait()
    index = index_ref[...]

    def look_up(n, coef):
        here = index == n
        return tuple(jnp.where(here, model_ref[c, n], coef[c]) for c in range(3))

    none = jnp.zeros(index.shape, jnp.float32)
    coef = lax.fori_loop(0, model_ref.shape[1], look_up, (none, none, none), unroll=4)
    total = depth * owners
    times = (
        lax.broadcasted_iota(jnp.int32, index.shape, 2) * total + t * depth + lax.broadcasted_iota(jnp.int32, index.shape, 1)
    ).astype(jnp.float32)
    moment = times / float(periods * total)
    delay = (coef[0] + coef[1] * moment + coef[2] * moment * moment) * (0.5 / (blocks * LANES))
    dsend[...] = jnp.zeros_like(dsend)
    for g in range(groups):
        dsend[g, :, :, :mine] = delay[:, :, g * mine : (g + 1) * mine]
    tables[0].wait()
    for g in range(groups):
        pieces = [flags[:, g * mine + p].astype(jnp.float32) for p in range(mine)]
        gap = wsend.shape[-1] - mine * blocks
        if gap:
            pieces.append(jnp.ones(pieces[0].shape[:-1] + (gap,), jnp.float32))
        both = jnp.concatenate(pieces, axis=-1) if len(pieces) > 1 else pieces[0]
        wsend[g] = (1.0 - both).astype(jnp.bfloat16)
    wbuf[0] = wsend[me]
    dbuf[0] = dsend[me]
    for shift in range(1, groups):
        for copy in small_copies(shift):
            copy.start()
    lax.fori_loop(2, total_steps, start_spectra, 0)

    for copy in tables[2:7]:
        copy.wait()
    lag = lax.broadcasted_iota(jnp.int32, (1, lags), 1) + 1
    for quarter in range(QUARTERS):
        turn = (lag * quarter) % 4
        cq = jnp.where(turn == 0, 1.0, jnp.where(turn == 2, -1.0, 0.0))
        sq = jnp.where(turn == 1, 1.0, jnp.where(turn == 3, -1.0, 0.0))

        def turn_rows(n, _, quarter=quarter, cq=cq, sq=sq):
            r = pl.ds(pl.multiple_of(n * LANES, LANES), LANES)
            for source, target in ((th, wh), (tl, wl)):
                c = source[r, :lags].astype(jnp.float32)
                s = source[r, lags:].astype(jnp.float32)
                target[quarter, r, :lags] = (c * cq - s * sq).astype(jnp.bfloat16)
                target[quarter, r, lags:] = (s * cq + c * sq).astype(jnp.bfloat16)
            return 0

        lax.fori_loop(0, th.shape[0] // LANES, turn_rows, 0)

    for shift in range(1, groups):
        for copy in small_copies(shift):
            copy.wait_recv()

    @pl.when(is_root)
    def _():
        pl.semaphore_wait(up_sem, others)
        tell_all(down_sem)

    @pl.when(jnp.logical_not(is_root))
    def _():
        pl.semaphore_wait(down_sem, 1)

    def gather_copy(shift, source):
        return pltpu.make_async_remote_copy(
            src_ref=wbuf, dst_ref=wall.at[source], send_sem=gs_sem, recv_sem=gr_sem,
            device_id={"tm": lax.rem(t + shift, owners)}, device_id_type=MESH,
        )

    for shift in range(1, owners):
        gather_copy(shift, t).start()
    wall[t] = wbuf[...]

    for g in range(groups):
        for l in range(local):
            r = (g * local + (l + turn_by * min(g, 1)) % local) * depth
            wrow[r : r + depth, :] = wbuf[g, l].astype(jnp.float32)
            d = dbuf[g, l]
            for p in range(mine):
                dsplat[p, r : r + depth, :] = jnp.broadcast_to(d[:, p : p + 1], d.shape)
    c, s = cos_sin_turns(dsplat[...] * float(SUB * LANES))
    step_c[...] = c
    step_s[...] = s
    channel = (
        lax.broadcasted_iota(jnp.int32, (SUB, LANES), 0) * LANES + lax.broadcasted_iota(jnp.int32, (SUB, LANES), 1)
    ).astype(jnp.float32)
    spectra = stations * depth

    def start_phases(p):
        def one(r, _):
            c, s = cos_sin_turns(dsplat[p, pl.ds(r, 1), :] * channel)
            base_c[r] = c
            base_s[r] = s
            return 0

        lax.fori_loop(0, spectra, one, 0, unroll=8)

    w_t = wrow[...].T
    for r in range(spectra):
        wide_w[r] = jnp.broadcast_to(w_t[:, r : r + 1], (w_t.shape[0], LANES))

    acc_flat = acc.reshape(pairs * SUB, LANES)
    v_flat = v_ref.reshape(rows * SUB, LANES)

    def make_scale():
        all_of(wall.at[pl.ds(0, owners - 1)], gr_sem).wait()
        for n in range(owners):
            for g in range(groups):
                turn = turn_by * min(g, 1)
                value = wall[n, g].astype(jnp.float32)
                at = slice(n * depth, (n + 1) * depth)
                wf[g * local + turn : (g + 1) * local, at, :] = value[: local - turn]
                if turn:
                    wf[g * local : g * local + turn, at, :] = value[local - turn :]
        for a in range(stations):
            for b0 in range(a // TILE * TILE, stations, TILE):
                b = max(a, b0)
                count = b0 + TILE - b
                product = wf[a][None] * wf[b : b + count]
                m = pair_order[a, b]
                acc[m : m + count] = jnp.sum(product.reshape(count, owners * depth // SUB, SUB, LANES), axis=1)
        count = acc_flat[pl.ds(0, pairs, stride=SUB), :]
        for b in range(1, SUB):
            count = count + acc_flat[pl.ds(b, pairs, stride=SUB), :]
        counts[...] = 1.0 / jnp.sqrt(jnp.maximum(count, 1.0))
        for off, same in kinds:
            pieces = []
            if off:
                x, y = off[0]
                n = len(off) * TILE * TILE
                pieces += [(real_row[x, y], pair_order[x, y], n), (imag_row[x, y], pair_order[x, y], n)]
            for x in same:
                if x == same[0]:
                    n = len(same) * TILE * (TILE + 1) // 2
                    pieces.append((real_row[x, x], pair_order[x, x], n))
                for i in range(TILE - 1):
                    pieces.append((imag_row[x + i, x + i + 1], pair_order[x + i, x + i + 1], TILE - 1 - i))
            for row, source, n in pieces:
                scale_ref[row : row + n, :] = counts[source : source + n, :]

    def station_of(target):
        return relative_here(target % wide // split * local + target // wide)

    def scatter_copy(p, shift, what, target, source):
        if what == "last":
            src, dst = zs_b.at[p, target], rb.at[p, source, units - 1]
        elif what == "early":
            src, dst = zs_a.at[p, target], rb.at[p, source, pl.ds(0, units - 1)]
        else:
            late = (station_of(target) + TILE) % stations * split + target % split
            src, dst = zs_c.at[p, late], rb.at[p, source, pl.ds(0, units - 1)]
        return pltpu.make_async_remote_copy(
            src_ref=src, dst_ref=dst, send_sem=rs_sem,
            recv_sem=rr_sem.at[p], device_id={"tm": lax.rem(t + shift, owners)}, device_id_type=MESH,
        )

    def is_late(target):
        return station_of(target) >= stations - TILE

    def final_copy(p, w, source, piece):
        return pltpu.make_async_remote_copy(
            src_ref=fs.at[w, p], dst_ref=fr.at[source * split + piece, p], send_sem=fs_sem,
            recv_sem=fr_sem.at[p // (mine - 1) if mine > 1 else 1], device_id={"stn": plane, "tm": home * wide + w}, device_id_type=MESH,
        )

    def reduce_period(p):
        all_of(rb.at[p, pl.ds(0, owners - 1)], rr_sem.at[p]).wait()
        late = jnp.where(is_late(t), 1.0, 0.0)
        first = zs_a[p, t].astype(jnp.float32)
        first += late * zs_c[p, (mine_a % TILE) * split + part].astype(jnp.float32)
        last = zs_b[p, t].astype(jnp.float32)
        for shift in range(1, owners):
            source = lax.rem(t + owners - shift, owners)
            first += rb[p, source, : units - 1].astype(jnp.float32)
            last += rb[p, source, units - 1].astype(jnp.float32)
        red[: units - 1] = first
        red[units - 1] = last
        for w in range(wide):
            for n in range(own_rows):
                b = relative_here(partner_ref[w * own_rows + n])
                if split > 1:
                    keep = jnp.where(b // span == part, 1.0, 0.0)
                    b = b % span
                for ri in range(2):
                    row = red[b // TILE, pl.ds(ri * TILE + b % TILE, 1), :]
                    fs[w, p, ri, n : n + 1, :] = row * keep if split > 1 else row
        for w in range(wide):
            @pl.when((plane == me) & (w == place))
            def _():
                fr[me * split + part, p] = fs[w, p]

    def start_final(p):
        for w in range(wide):
            @pl.when(jnp.logical_not((plane == me) & (w == place)))
            def _():
                final_copy(p, w, me, part).start()

    half = TILE // 2

    def work(i, late):
        p = i // QUARTERS
        quarter = i % QUARTERS
        at = pl.ds(pl.multiple_of(p * blocks + quarter * SUB, SUB), SUB)
        first_station = stations - TILE if late else 0
        off, same = kinds[late]
        top, size = (early, rows - early) if late else (0, early)

        def wait_spectra(low, high):
            piece = xall.at[pl.ds(low, high - low), p, :, band(i), :]
            all_of(piece, xr_sem.at[arrival(i, late)]).wait()

        if late:
            @pl.when(i >= steps - QUARTERS)
            def _():
                wait_spectra(stations - TILE, stations)
        else:
            @pl.when(i < steps - QUARTERS)
            def _():
                wait_spectra(local, stations)

            @pl.when(i >= steps - QUARTERS)
            def _():
                wait_spectra(local, stations - TILE)

            @pl.when(quarter == 0)
            def _():
                start_phases(p)

        def rotate(n, _):
            for j in range(2):
                s = first_station + n * 2 + j
                for k in range(depth):
                    r = s * depth + k
                    tmp[j * depth + k] = xall[s, p, k, band(i), :].astype(jnp.float32)
                    real = tmp[j * depth + k, pl.ds(0, SUB, stride=2), :]
                    imag = tmp[j * depth + k, pl.ds(1, SUB, stride=2), :]
                    c = base_c[r]
                    sn = base_s[r]
                    w = wide_w[r, at, :]
                    new_real = (w * (real * c + imag * sn)).astype(jnp.bfloat16).astype(jnp.float32)
                    new_imag = (w * (imag * c - real * sn)).astype(jnp.bfloat16).astype(jnp.float32)
                    yr[quarter, k, s] = new_real
                    yi[quarter, k, s] = new_imag
                    ys[quarter, k, s] = new_real + new_imag
                    yd[quarter, k, s] = new_real - new_imag
                    pc = step_c[p, pl.ds(r, 1), :]
                    ps = step_s[p, pl.ds(r, 1), :]
                    base_c[r] = c * pc - sn * ps
                    base_s[r] = sn * pc + c * ps
            return 0

        lax.fori_loop(0, (TILE if late else stations - TILE) // 2, rotate, 0)

        for x, y0 in off:
            for y in (y0, y0 + half):
                for k in range(depth):
                    ar, ai, asum = (ref[quarter, k, x : x + TILE][:, None] for ref in (yr, yi, ys))
                    br, bi, bdiff = (ref[quarter, k, y : y + half][None] for ref in (yr, yi, yd))
                    first = ar * br if k == 0 else first + ar * br
                    second = ai * bi if k == 0 else second + ai * bi
                    third = asum * bdiff if k == 0 else third + asum * bdiff
                real = first + second
                imag = third - (first - second)
                for n in range(TILE):
                    m = real_row[x + n, y]
                    q = imag_row[x + n, y]
                    v_ref[m : m + half] = real[n]
                    v_ref[q : q + half] = imag[n]
        for x in same:
            for a in range(x, x + TILE):
                n = x + TILE - a
                for k in range(depth):
                    ar, ai = yr[quarter, k, a], yi[quarter, k, a]
                    term = ar * ar + ai * ai
                    auto = term if k == 0 else auto + term
                    if n > 1:
                        br, bi, bdiff = (ref[quarter, k, a + 1 : a + n] for ref in (yr, yi, yd))
                        asum = ys[quarter, k, a]
                        first = ar * br if k == 0 else first + ar * br
                        second = ai * bi if k == 0 else second + ai * bi
                        third = asum * bdiff if k == 0 else third + asum * bdiff
                m = real_row[a, a]
                v_ref[m] = auto
                if n > 1:
                    q = imag_row[a, a + 1]
                    v_ref[m + 1 : m + n] = first + second
                    v_ref[q : q + n - 1] = third - (first - second)

        if not late:
            pl.when(i == 0)(make_scale)
        here = slice(top, top + size)
        turned[here] = pltpu.roll(scale_ref[here], LANES - (p * blocks + quarter * SUB), 1)
        for b in range(SUB):
            v = v_flat[pl.ds(top * SUB + b, size, stride=SUB), :] * turned[here, b : b + 1]
            vh[here, b * LANES : (b + 1) * LANES] = v.astype(jnp.bfloat16)
        values = dot(vh[here], wh[quarter]) + dot(vh[here], wl[quarter])

        @pl.when(quarter == 0)
        def _():
            z_ref[here] = values

        @pl.when(quarter > 0)
        def _():
            z_ref[here] += values

        @pl.when(quarter == QUARTERS - 1)
        def _():
            if late:
                picked = dot(pick_b[...], z_ref[...].astype(jnp.bfloat16)).reshape(-1, 2 * TILE, LAGS)
                zs_b[p] = picked[:owners].astype(jnp.bfloat16)
                zs_c[p] = picked[owners:].reshape(zs_c.shape[1:]).astype(jnp.bfloat16)
            else:
                picked = dot(pick_a[...], z_ref[here].astype(jnp.bfloat16))
                zs_a[p] = picked.reshape(zs_a.shape[1:]).astype(jnp.bfloat16)
            for shift in range(1, owners):
                target = lax.rem(t + shift, owners)
                if late:
                    scatter_copy(p, shift, "last", target, t).start()

                @pl.when(is_late(target) == late)
                def _():
                    scatter_copy(p, shift, "late" if late else "early", target, t).start()

        if late:
            @pl.when((quarter == QUARTERS - 1) & (p > 0))
            def _():
                reduce_period(p - 1)

    def step(n, _):
        i, kind = sub_step(n)

        @pl.when(kind == 0)
        def _():
            work(i, False)

        @pl.when(kind == 1)
        def _():
            work(i, True)

        return 0

    own_copy.wait()
    lax.fori_loop(0, total_steps, step, 0)
    for p in range(mine - 1):
        start_final(p)
    for shift in range(1, groups):
        for copy in small_copies(shift):
            copy.wait_send()
    all_of(wall.at[pl.ds(0, owners - 1)], gs_sem).wait()
    reduce_period(mine - 1)
    start_final(mine - 1)
    all_of(xall.at[pl.ds(local, stations - local)], xs_sem).wait()
    all_of(rb.at[:, pl.ds(0, owners - 1)], rs_sem).wait()

    flip = (
        lax.broadcasted_iota(jnp.int32, (lags, lags), 0) + lax.broadcasted_iota(jnp.int32, (lags, lags), 1) == lags - 1
    ).astype(jnp.bfloat16)
    factor = 1.0 / math.sqrt(periods * blocks * LANES)

    def wait_final(which, count):
        @pl.when(plane == me)
        def _():
            all_of(fr.at[pl.ds(0, wide - 1), pl.ds(0, count)], fr_sem.at[which]).wait()

        @pl.when(plane != me)
        def _():
            all_of(fr.at[:, pl.ds(0, count)], fr_sem.at[which]).wait()

    def transform(first, last):
        values, low = [], []
        for g in range(groups):
            for p in range(first, last):
                value = fr[g * split, p]
                for h in range(1, split):
                    value = value + fr[g * split + h, p]
                rc, rs = value[0, :, :lags], value[0, :, lags:]
                ic, im_s = value[1, :, :lags], value[1, :, lags:]
                values.append((g * mine + p, rc + im_s, ic - rs))
                low += [rc - im_s, ic + rs]
        low = jnp.concatenate(low, axis=0) if len(low) > 1 else low[0]
        high = low.astype(jnp.bfloat16)
        rest = low - high.astype(jnp.float32)
        middle = rest.astype(jnp.bfloat16)
        rest = (rest - middle.astype(jnp.float32)).astype(jnp.bfloat16)
        low = dot(high, flip) + dot(middle, flip) + dot(rest, flip)
        sums = []
        for r in range(periods):
            parts = []
            for side in range(2):
                real = imag = None
                for n, (p, re, im) in enumerate(values):
                    if side == 0:
                        re = low[2 * n * own_rows : (2 * n + 1) * own_rows]
                        im = low[(2 * n + 1) * own_rows : (2 * n + 2) * own_rows]
                    c = math.cos(2.0 * math.pi * (p * r % periods) / periods) * factor
                    s = math.sin(2.0 * math.pi * (p * r % periods) / periods) * factor
                    if abs(c) < 1e-9 * factor:
                        new_re, new_im = s * im, -s * re
                    elif abs(s) < 1e-9 * factor:
                        new_re, new_im = c * re, c * im
                    else:
                        new_re, new_im = c * re + s * im, c * im - s * re
                    real = new_re if real is None else real + new_re
                    imag = new_im if imag is None else imag + new_im
                parts.append((real, imag))
            sums.append(parts)
        return sums

    if mine > 1:
        wait_final(0, mine - 1)
        for r, parts in enumerate(transform(0, mine - 1)):
            for side, (real, imag) in enumerate(parts):
                cols = slice(side * lags, (side + 1) * lags)
                gf[0, r, :, cols] = real
                gf[1, r, :, cols] = imag
    wait_final(1, 1)
    for r, parts in enumerate(transform(mine - 1, mine)):
        for side, pair in enumerate(parts):
            cols = slice(side * lags, (side + 1) * lags)
            for n, value in enumerate(pair):
                if mine > 1:
                    value = value + gf[n, r, :, cols]
                out_ref[n, pl.ds(side * periods + r, own_rows, stride=2 * periods), :] = value

    @pl.when(plane == me)
    def _():
        all_of(fs.at[pl.ds(0, wide - 1)], fs_sem).wait()

    @pl.when(plane != me)
    def _():
        all_of(fs, fs_sem).wait()


def per_device(spectra, flags, poly_index, delay_model, partner_order):
    local, periods, depth, _, channels = spectra.shape
    groups = lax.axis_size("stn")
    owners = lax.axis_size("tm")
    stations = local * groups
    mine = periods // groups
    blocks = flags.shape[-1]
    split = owners // stations
    wide = groups * split
    own_rows = stations // wide
    span = stations // split
    rows = stations * stations
    pairs = stations * (stations + 1) // 2
    steps = mine * QUARTERS
    width = channels // QUARTERS
    lanes = LANES
    assert channels == blocks * LANES and width == SUB * LANES and stations % TILE == 0 and mine * blocks <= lanes

    x = spectra.reshape(local, periods, depth, 2, blocks, LANES).transpose(0, 1, 2, 4, 3, 5)
    x = x.reshape(local, periods, depth, 2 * blocks, LANES)
    high, low = lag_tables(channels)
    pick_a, pick_b = pick_matrices(stations, groups, owners)
    units = span // TILE
    runs = arrivals(stations, groups)
    hbm = pl.BlockSpec(memory_space=pltpu.HBM)
    f32, bf16, i32 = jnp.float32, jnp.bfloat16, jnp.int32
    spectra_rows = stations * depth
    dma = pltpu.SemaphoreType.DMA
    out = pl.pallas_call(
        functools.partial(kernel, (groups, owners, stations, periods, depth, blocks)),
        out_shape=jax.ShapeDtypeStruct((2, own_rows * 2 * periods, LAGS // 2), f32),
        in_specs=[hbm] * 9,
        out_specs=pl.BlockSpec(memory_space=pltpu.VMEM),
        scratch_shapes=[
            pltpu.VMEM((stations, mine, depth, 2 * blocks, LANES), bf16),
            pltpu.VMEM(flags.shape, i32),
            pltpu.VMEM((local, depth, periods), i32),
            pltpu.SMEM(delay_model.shape[::-1], f32),
            pltpu.SMEM(partner_order.shape, i32),
            pltpu.VMEM((groups, local, depth, lanes), bf16),
            pltpu.VMEM((groups, local, depth, LANES), f32),
            pltpu.VMEM((groups, local, depth, lanes), bf16),
            pltpu.VMEM((groups, local, depth, LANES), f32),
            pltpu.VMEM((owners, groups, local, depth, lanes), bf16),
            pltpu.VMEM((stations, owners * depth, lanes), f32),
            pltpu.VMEM((spectra_rows, lanes), f32),
            pltpu.VMEM((pairs, SUB, lanes), f32),
            pltpu.VMEM((pairs, lanes), f32),
            pltpu.VMEM((rows, lanes), f32),
            pltpu.VMEM((rows, lanes), f32),
            pltpu.VMEM((spectra_rows, lanes, LANES), f32),
            pltpu.VMEM((mine, spectra_rows, LANES), f32),
            pltpu.VMEM((mine, spectra_rows, LANES), f32),
            pltpu.VMEM((mine, spectra_rows, LANES), f32),
            pltpu.VMEM((spectra_rows, SUB, LANES), f32),
            pltpu.VMEM((spectra_rows, SUB, LANES), f32),
            pltpu.VMEM(high.shape, bf16),
            pltpu.VMEM(low.shape, bf16),
            pltpu.VMEM(pick_a.shape[1:], bf16),
            pltpu.VMEM(pick_b.shape[1:], bf16),
            pltpu.VMEM((QUARTERS,) + high.shape, bf16),
            pltpu.VMEM((QUARTERS,) + low.shape, bf16),
            pltpu.VMEM((2 * depth, 2 * SUB, LANES), f32),
            pltpu.VMEM((QUARTERS, depth, stations, SUB, LANES), f32),
            pltpu.VMEM((QUARTERS, depth, stations, SUB, LANES), f32),
            pltpu.VMEM((QUARTERS, depth, stations, SUB, LANES), f32),
            pltpu.VMEM((QUARTERS, depth, stations, SUB, LANES), f32),
            pltpu.VMEM((rows, SUB, LANES), f32),
            pltpu.VMEM((rows, width), bf16),
            pltpu.VMEM((rows, LAGS), f32),
            pltpu.VMEM((mine, owners, units - 1, 2 * TILE, LAGS), bf16),
            pltpu.VMEM((mine, owners, 2 * TILE, LAGS), bf16),
            pltpu.VMEM((mine, TILE * split, units - 1, 2 * TILE, LAGS), bf16),
            pltpu.VMEM((mine, owners, units, 2 * TILE, LAGS), bf16),
            pltpu.VMEM((units, 2 * TILE, LAGS), f32),
            pltpu.VMEM((wide, mine, 2, own_rows, LAGS), f32),
            pltpu.VMEM((wide, mine, 2, own_rows, LAGS), f32),
            pltpu.VMEM((2, periods, own_rows, LAGS), f32),
            dma((8,)),
            dma,
            dma,
            dma((steps + QUARTERS,)),
            dma((2, groups - 1)),
            dma((2, groups - 1)),
            dma,
            dma,
            dma,
            dma((mine,)),
            dma,
            dma((2,)),
            pltpu.SemaphoreType.REGULAR,
            pltpu.SemaphoreType.REGULAR,
        ],
        compiler_params=pltpu.CompilerParams(collective_id=0, has_side_effects=True, vmem_limit_bytes=40 << 20),
        name="correlate",
    )(*(
        pltpu.with_memory_space_constraint(value, pltpu.HBM)
        for value in (
            x, flags, poly_index.transpose(0, 2, 1), delay_model.T, partner_order,
            jnp.asarray(high), jnp.asarray(low), jnp.asarray(pick_a), jnp.asarray(pick_b),
        )
    ))
    out = out.reshape(2, own_rows, 2, periods, LAGS // 2).transpose(0, 1, 3, 2, 4)
    return out.reshape(2, own_rows, periods, LAGS)


def solution(mesh):
    return jax.shard_map(
        per_device,
        mesh=mesh,
        in_specs=(
            P("stn", None, "tm", None, None),
            P("stn", None, "tm", None),
            P("stn", None, "tm"),
            P(),
            P(),
        ),
        out_specs=P(None, ("stn", "tm"), None, None),
        check_vma=False,
    )
```

```python
import functools
import math

import jax
import jax.numpy as jnp
import numpy as np
from jax import lax
from jax.experimental import pallas as pl
from jax.experimental.pallas import tpu as pltpu
from jax.sharding import PartitionSpec as P

LAGS = 256
QUARTERS = 4
LANES = 128
SUB = 8
TILE = 4
MESH = pl.DeviceIdType.MESH


def lag_tables(channels):
    lags = np.arange(1, LAGS // 2 + 1)
    j = np.arange(channels // QUARTERS)
    angle = (j[:, None] * lags[None, :] % channels) * (2.0 * np.pi / channels)
    table = np.concatenate([np.cos(angle), np.sin(angle)], axis=1).astype(np.float32)
    high = table.astype(jnp.bfloat16)
    low = (table - high.astype(np.float32)).astype(jnp.bfloat16)
    return high, low


def pair_rows(stations):
    last = stations - TILE
    kinds = []
    real, imag, order = {}, {}, {}
    row = 0
    for late in (False, True):
        off = [(x, y) for x in range(0, stations, TILE) for y in range(x + TILE, stations, TILE) if (y == last) == late]
        same = [last] if late else list(range(0, last, TILE))
        for part in (real, imag):
            skip = 0 if part is real else 1
            start = row
            keys = [(x + i, y + j) for x, y in off for i in range(TILE) for j in range(TILE)]
            keys += [(x + i, x + j) for x in same for i in range(TILE) for j in range(i + skip, TILE)]
            for key in keys:
                part[key] = row
                row += 1
                if part is real:
                    order[key] = len(order)
        kinds.append((off, same))
    return kinds, real, imag, order


def late_first(local):
    return local // 4 if local >= 2 * TILE else 0


def relative(station, plane, groups, local):
    slot = (station // local - plane) % groups
    place = station % local
    return slot * local + (place if slot == 0 else (place + late_first(local)) % local)


def pick_matrices(stations, groups, owners):
    _, real, imag, _ = pair_rows(stations)
    split = owners // stations
    wide = groups * split
    local = stations // groups
    units = stations // split // TILE
    rows = stations * stations
    early = (stations - TILE) ** 2
    pick_a = np.zeros((groups, owners, units - 1, 2, TILE, rows), np.float32)
    pick_b = np.zeros((groups, owners, 2, TILE, rows), np.float32)
    pick_c = np.zeros((groups, TILE * split, units - 1, 2, TILE, rows), np.float32)
    for g in range(groups):
        for t in range(owners):
            a = relative((t % wide // split + g) % groups * local + t // wide, g, groups, local)
            late = a >= stations - TILE
            for u in range(units):
                for n in range(TILE):
                    b = (t % split * units + u) * TILE + n
                    key = (min(a, b), max(a, b))
                    if u == units - 1:
                        target = pick_b[g, t]
                    elif late:
                        target = pick_c[g, (a - stations + TILE) * split + t % split, u]
                    else:
                        target = pick_a[g, t, u]
                    target[0, n, real[key]] = 1.0
                    if a != b:
                        target[1, n, imag[key]] = 1.0 if a < b else -1.0
    pick_a = pick_a.reshape(groups, -1, rows)
    assert not pick_a[:, :, early:].any()
    pick_b = np.concatenate([pick_b.reshape(groups, -1, rows), pick_c.reshape(groups, -1, rows)], axis=1)
    return pick_a[:, :, :early].astype(jnp.bfloat16), pick_b.astype(jnp.bfloat16)


def arrivals(stations, groups):
    local = stations // groups
    runs = []
    for shift in range(1, groups):
        slot = groups - shift
        turn = late_first(local)
        places = [((i - turn) % local, slot * local + i) for i in range(local)]
        for source, here in places:
            late = here >= stations - TILE
            if runs and runs[-1][:2] == (late, shift) and source == runs[-1][2] + runs[-1][3]:
                runs[-1] = (late, shift, runs[-1][2], runs[-1][3] + 1, runs[-1][4])
            else:
                runs.append((late, shift, source, 1, here))
    return runs


def dot(a, b):
    return jnp.dot(a, b, preferred_element_type=jnp.float32)


SIN = [(-1) ** n * math.pi ** (2 * n + 1) / math.factorial(2 * n + 1) for n in range(6)]
COS = [(-1) ** n * math.pi ** (2 * n) / math.factorial(2 * n) for n in range(7)]


def cos_sin_turns(turns):
    frac = turns - jnp.floor(turns + 0.5)
    square = frac * frac
    s = jnp.full_like(square, SIN[-1])
    for coef in SIN[-2::-1]:
        s = s * square + coef
    s = s * frac
    c = jnp.full_like(square, COS[-1])
    for coef in COS[-2::-1]:
        c = c * square + coef
    return 1.0 - 2.0 * (s * s), 2.0 * (s * c)


def kernel(
    sizes,
    x_hbm, flags_hbm, index_hbm, model_hbm, partner_hbm, high_hbm, low_hbm, pick_a_hbm, pick_b_hbm,
    out_ref,
    xall, flags, index_ref, model_ref, partner_ref, wsend, dsend, wbuf, dbuf, wall, wf, wrow, acc, counts, scale_ref, turned,
    wide_w, dsplat, step_c, step_s, base_c, base_s, th, tl, pick_a, pick_b, wh, wl, tmp, yr, yi, ys, yd, v_ref, vh, z_ref,
    zs_a, zs_b, zs_c, rb, red, fs, fr, gf,
    table_sem, own_sem, xs_sem, xr_sem, ws_sem, wr_sem, gs_sem, gr_sem, rs_sem, rr_sem, fs_sem, fr_sem, up_sem, down_sem,
):
    groups, owners, stations, periods, depth, blocks = sizes
    local = stations // groups
    mine = periods // groups
    split = owners // stations
    wide = groups * split
    span = stations // split
    own_rows = stations // wide
    rows = stations * stations
    steps = mine * QUARTERS
    lags = LAGS // 2
    me = lax.axis_index("stn")
    t = lax.axis_index("tm")
    home = t // wide
    place = t % wide
    plane = (place // split + me) % groups
    part = t % split
    units = span // TILE
    early = (stations - TILE) ** 2
    turn_by = late_first(local)
    runs = arrivals(stations, groups)
    kinds, real_row, imag_row, pair_order = pair_rows(stations)
    pairs = len(real_row)

    def relative_here(station):
        slot = (station // local - me + groups) % groups
        return slot * local + (station % local + (slot + groups - 1) // groups * turn_by) % local

    mine_a = relative_here(plane * local + home)
    total_steps = 2 * steps
    full = 2 * (mine - 1) * QUARTERS

    def sub_step(n):
        last = n // full if full else 1
        i = (1 - last) * (n // 2) + last * ((mine - 1) * QUARTERS + (n + QUARTERS * 2 - full % (QUARTERS * 2)) % QUARTERS)
        kind = (1 - last) * (n % 2) + last * ((n + total_steps - full) // QUARTERS - total_steps // QUARTERS)
        return i, kind

    def band(i):
        return pl.ds(pl.multiple_of((i % QUARTERS) * 2 * SUB, 2 * SUB), 2 * SUB)

    own_copy = pltpu.make_async_copy(x_hbm.at[:, pl.ds(me * mine, mine)], xall.at[pl.ds(0, local)], own_sem)

    def all_of(ref, sem):
        return pltpu.make_async_copy(ref, ref, sem)

    tables = [
        pltpu.make_async_copy(source, target, table_sem.at[n])
        for n, (source, target) in enumerate((
            (flags_hbm, flags), (index_hbm, index_ref), (high_hbm, th), (low_hbm, tl),
            (pick_a_hbm.at[me], pick_a), (pick_b_hbm.at[me], pick_b), (partner_hbm, partner_ref),
            (model_hbm, model_ref),
        ))
    ]
    barrier = pltpu.get_barrier_semaphore()
    is_root = (me == 0) & (t == 0)
    others = groups * owners - 1

    def tell(sem, peer):
        pl.semaphore_signal(sem, inc=1, device_id=peer, device_id_type=MESH)

    def tell_all(sem):
        def one(n, _):
            tell(sem, {"stn": (n + 1) // owners, "tm": (n + 1) % owners})
            return 0

        lax.fori_loop(0, others, one, 0)

    for shift in range(1, groups):
        tell(barrier, {"stn": lax.rem(me + shift, groups)})

    @pl.when(is_root)
    def _():
        tell_all(barrier)

    for copy in tables:
        copy.start()

    own_copy.start()

    @pl.when(is_root)
    def _():
        pl.semaphore_wait(barrier, groups - 1)

    @pl.when(jnp.logical_not(is_root))
    def _():
        pl.semaphore_wait(barrier, groups)
        tell(up_sem, {"stn": 0, "tm": 0})


    def small_copies(shift):
        target = lax.rem(me + shift, groups)
        return [
            pltpu.make_async_remote_copy(
                src_ref=ref.at[target], dst_ref=buf.at[groups - shift], send_sem=ws_sem.at[n, shift - 1],
                recv_sem=wr_sem.at[n, shift - 1], device_id={"stn": target}, device_id_type=MESH,
            )
            for n, (ref, buf) in enumerate(((wsend, wbuf), (dsend, dbuf)))
        ]

    def arrival(i, late):
        last = i // ((mine - 1) * QUARTERS) if mine > 1 else 1
        return i + last * QUARTERS * int(late)

    def spectra_copy(n, i):
        late, shift, source, count, here = runs[n]
        target = lax.rem(me + shift, groups)
        return pltpu.make_async_remote_copy(
            src_ref=x_hbm.at[pl.ds(source, count), target * mine + i // QUARTERS, :, band(i), :],
            dst_ref=xall.at[pl.ds(here, count), i // QUARTERS, :, band(i), :],
            send_sem=xs_sem, recv_sem=xr_sem.at[arrival(i, late)],
            device_id={"stn": target}, device_id_type=MESH,
        )

    def start_spectra(n, _):
        i, kind = sub_step(n)
        for late in (False, True):

            @pl.when(kind == int(late))
            def _():
                for r in range(len(runs)):
                    if runs[r][0] == late:
                        spectra_copy(r, i).start()

        return 0

    lax.fori_loop(0, 2, start_spectra, 0)

    tables[1].wait()
    tables[7].wait()
    index = index_ref[...]

    def look_up(n, coef):
        here = index == n
        return tuple(jnp.where(here, model_ref[c, n], coef[c]) for c in range(3))

    none = jnp.zeros(index.shape, jnp.float32)
    coef = lax.fori_loop(0, model_ref.shape[1], look_up, (none, none, none), unroll=4)
    total = depth * owners
    times = (
        lax.broadcasted_iota(jnp.int32, index.shape, 2) * total + t * depth + lax.broadcasted_iota(jnp.int32, index.shape, 1)
    ).astype(jnp.float32)
    moment = times / float(periods * total)
    delay = (coef[0] + coef[1] * moment + coef[2] * moment * moment) * (0.5 / (blocks * LANES))
    dsend[...] = jnp.zeros_like(dsend)
    for g in range(groups):
        dsend[g, :, :, :mine] = delay[:, :, g * mine : (g + 1) * mine]
    tables[0].wait()
    for g in range(groups):
        pieces = [flags[:, g * mine + p].astype(jnp.float32) for p in range(mine)]
        gap = wsend.shape[-1] - mine * blocks
        if gap:
            pieces.append(jnp.ones(pieces[0].shape[:-1] + (gap,), jnp.float32))
        both = jnp.concatenate(pieces, axis=-1) if len(pieces) > 1 else pieces[0]
        wsend[g] = (1.0 - both).astype(jnp.bfloat16)
    wbuf[0] = wsend[me]
    dbuf[0] = dsend[me]
    for shift in range(1, groups):
        for copy in small_copies(shift):
            copy.start()
    lax.fori_loop(2, total_steps, start_spectra, 0)

    @pl.when(is_root)
    def _():
        pl.semaphore_wait(up_sem, others)
        tell_all(down_sem)

    for copy in tables[2:7]:
        copy.wait()
    lag = lax.broadcasted_iota(jnp.int32, (1, lags), 1) + 1
    for quarter in range(QUARTERS):
        turn = (lag * quarter) % 4
        cq = jnp.where(turn == 0, 1.0, jnp.where(turn == 2, -1.0, 0.0))
        sq = jnp.where(turn == 1, 1.0, jnp.where(turn == 3, -1.0, 0.0))

        def turn_rows(n, _, quarter=quarter, cq=cq, sq=sq):
            r = pl.ds(pl.multiple_of(n * LANES, LANES), LANES)
            for source, target in ((th, wh), (tl, wl)):
                c = source[r, :lags].astype(jnp.float32)
                s = source[r, lags:].astype(jnp.float32)
                target[quarter, r, :lags] = (c * cq - s * sq).astype(jnp.bfloat16)
                target[quarter, r, lags:] = (s * cq + c * sq).astype(jnp.bfloat16)
            return 0

        lax.fori_loop(0, th.shape[0] // LANES, turn_rows, 0)

    for shift in range(1, groups):
        for copy in small_copies(shift):
            copy.wait_recv()

    @pl.when(jnp.logical_not(is_root))
    def _():
        pl.semaphore_wait(down_sem, 1)

    def gather_copy(shift, source):
        return pltpu.make_async_remote_copy(
            src_ref=wbuf, dst_ref=wall.at[source], send_sem=gs_sem, recv_sem=gr_sem,
            device_id={"tm": lax.rem(t + shift, owners)}, device_id_type=MESH,
        )

    for shift in range(1, owners):
        gather_copy(shift, t).start()
    wall[t] = wbuf[...]

    for g in range(groups):
        for l in range(local):
            r = (g * local + (l + turn_by * min(g, 1)) % local) * depth
            wrow[r : r + depth, :] = wbuf[g, l].astype(jnp.float32)
            d = dbuf[g, l]
            for p in range(mine):
                dsplat[p, r : r + depth, :] = jnp.broadcast_to(d[:, p : p + 1], d.shape)
    c, s = cos_sin_turns(dsplat[...] * float(SUB * LANES))
    step_c[...] = c
    step_s[...] = s
    channel = (
        lax.broadcasted_iota(jnp.int32, (SUB, LANES), 0) * LANES + lax.broadcasted_iota(jnp.int32, (SUB, LANES), 1)
    ).astype(jnp.float32)
    spectra = stations * depth

    def start_phases(p):
        def one(r, _):
            c, s = cos_sin_turns(dsplat[p, pl.ds(r, 1), :] * channel)
            base_c[r] = c
            base_s[r] = s
            return 0

        lax.fori_loop(0, spectra, one, 0, unroll=8)

    w_t = wrow[...].T
    for r in range(spectra):
        wide_w[r] = jnp.broadcast_to(w_t[:, r : r + 1], (w_t.shape[0], LANES))

    acc_flat = acc.reshape(pairs * SUB, LANES)
    v_flat = v_ref.reshape(QUARTERS * rows * SUB, LANES)

    def make_scale():
        all_of(wall.at[pl.ds(0, owners - 1)], gr_sem).wait()
        for n in range(owners):
            for g in range(groups):
                turn = turn_by * min(g, 1)
                value = wall[n, g].astype(jnp.float32)
                at = slice(n * depth, (n + 1) * depth)
                wf[g * local + turn : (g + 1) * local, at, :] = value[: local - turn]
                if turn:
                    wf[g * local : g * local + turn, at, :] = value[local - turn :]
        for a in range(stations):
            for b0 in range(a // TILE * TILE, stations, TILE):
                b = max(a, b0)
                count = b0 + TILE - b
                product = wf[a][None] * wf[b : b + count]
                m = pair_order[a, b]
                acc[m : m + count] = jnp.sum(product.reshape(count, owners * depth // SUB, SUB, LANES), axis=1)
        count = acc_flat[pl.ds(0, pairs, stride=SUB), :]
        for b in range(1, SUB):
            count = count + acc_flat[pl.ds(b, pairs, stride=SUB), :]
        counts[...] = 1.0 / jnp.sqrt(jnp.maximum(count, 1.0))
        for off, same in kinds:
            pieces = []
            if off:
                x, y = off[0]
                n = len(off) * TILE * TILE
                pieces += [(real_row[x, y], pair_order[x, y], n), (imag_row[x, y], pair_order[x, y], n)]
            for x in same:
                if x == same[0]:
                    n = len(same) * TILE * (TILE + 1) // 2
                    pieces.append((real_row[x, x], pair_order[x, x], n))
                for i in range(TILE - 1):
                    pieces.append((imag_row[x + i, x + i + 1], pair_order[x + i, x + i + 1], TILE - 1 - i))
            for row, source, n in pieces:
                scale_ref[row : row + n, :] = counts[source : source + n, :]

    def station_of(target):
        return relative_here((target % wide // split + me) % groups * local + target // wide)

    def scatter_copy(p, shift, what, target, source):
        if what == "last":
            src, dst = zs_b.at[p, target], rb.at[p, source, units - 1]
        elif what == "early":
            src, dst = zs_a.at[p, target], rb.at[p, source, pl.ds(0, units - 1)]
        else:
            late = (station_of(target) + TILE) % stations * split + target % split
            src, dst = zs_c.at[p, late], rb.at[p, source, pl.ds(0, units - 1)]
        return pltpu.make_async_remote_copy(
            src_ref=src, dst_ref=dst, send_sem=rs_sem,
            recv_sem=rr_sem.at[p], device_id={"tm": lax.rem(t + shift, owners)}, device_id_type=MESH,
        )

    def is_late(target):
        return station_of(target) >= stations - TILE

    def final_copy(p, w, source, piece):
        return pltpu.make_async_remote_copy(
            src_ref=fs.at[w, p], dst_ref=fr.at[source * split + piece, p], send_sem=fs_sem,
            recv_sem=fr_sem.at[p // (mine - 1) if mine > 1 else 1], device_id={"stn": plane, "tm": home * wide + w}, device_id_type=MESH,
        )

    def reduce_period(p):
        all_of(rb.at[p, pl.ds(0, owners - 1)], rr_sem.at[p]).wait()
        late = jnp.where(is_late(t), 1.0, 0.0)
        first = zs_a[p, t].astype(jnp.float32)
        first += late * zs_c[p, (mine_a % TILE) * split + part].astype(jnp.float32)
        last = zs_b[p, t].astype(jnp.float32)
        for shift in range(1, owners):
            source = lax.rem(t + owners - shift, owners)
            first += rb[p, source, : units - 1].astype(jnp.float32)
            last += rb[p, source, units - 1].astype(jnp.float32)
        red[: units - 1] = first
        red[units - 1] = last
        for w in range(wide):
            for n in range(own_rows):
                b = relative_here(partner_ref[w * own_rows + n])
                if split > 1:
                    keep = jnp.where(b // span == part, 1.0, 0.0)
                    b = b % span
                for ri in range(2):
                    row = red[b // TILE, pl.ds(ri * TILE + b % TILE, 1), :]
                    fs[w, p, ri, n : n + 1, :] = row * keep if split > 1 else row
        for w in range(wide):
            @pl.when((plane == me) & (w == place))
            def _():
                fr[me * split + part, p] = fs[w, p]

    def start_final(p):
        for w in range(wide):
            @pl.when(jnp.logical_not((plane == me) & (w == place)))
            def _():
                final_copy(p, w, me, part).start()

    half = TILE // 2

    def products(i, late):
        p = i // QUARTERS
        quarter = i % QUARTERS
        at = pl.ds(pl.multiple_of(p * blocks + quarter * SUB, SUB), SUB)
        first_station = stations - TILE if late else 0
        off, same = kinds[late]

        def wait_spectra(low, high):
            piece = xall.at[pl.ds(low, high - low), p, :, band(i), :]
            all_of(piece, xr_sem.at[arrival(i, late)]).wait()

        if late:
            @pl.when(i >= steps - QUARTERS)
            def _():
                wait_spectra(stations - TILE, stations)
        else:
            @pl.when(i < steps - QUARTERS)
            def _():
                wait_spectra(local, stations)

            @pl.when(i >= steps - QUARTERS)
            def _():
                wait_spectra(local, stations - TILE)

            @pl.when(quarter == 0)
            def _():
                start_phases(p)

        def rotate(n, _):
            for j in range(2):
                s = first_station + n * 2 + j
                for k in range(depth):
                    r = s * depth + k
                    tmp[j * depth + k] = xall[s, p, k, band(i), :].astype(jnp.float32)
                    real = tmp[j * depth + k, pl.ds(0, SUB, stride=2), :]
                    imag = tmp[j * depth + k, pl.ds(1, SUB, stride=2), :]
                    c = base_c[r]
                    sn = base_s[r]
                    w = wide_w[r, at, :]
                    new_real = (w * (real * c + imag * sn)).astype(jnp.bfloat16).astype(jnp.float32)
                    new_imag = (w * (imag * c - real * sn)).astype(jnp.bfloat16).astype(jnp.float32)
                    yr[quarter, k, s] = new_real
                    yi[quarter, k, s] = new_imag
                    ys[quarter, k, s] = new_real + new_imag
                    yd[quarter, k, s] = new_real - new_imag
                    pc = step_c[p, pl.ds(r, 1), :]
                    ps = step_s[p, pl.ds(r, 1), :]
                    base_c[r] = c * pc - sn * ps
                    base_s[r] = sn * pc + c * ps
            return 0

        lax.fori_loop(0, (TILE if late else stations - TILE) // 2, rotate, 0)

        for x, y0 in off:
            for y in (y0, y0 + half):
                for k in range(depth):
                    ar, ai, asum = (ref[quarter, k, x : x + TILE][:, None] for ref in (yr, yi, ys))
                    br, bi, bdiff = (ref[quarter, k, y : y + half][None] for ref in (yr, yi, yd))
                    first = ar * br if k == 0 else first + ar * br
                    second = ai * bi if k == 0 else second + ai * bi
                    third = asum * bdiff if k == 0 else third + asum * bdiff
                real = first + second
                imag = third - (first - second)
                for n in range(TILE):
                    m = real_row[x + n, y]
                    q = imag_row[x + n, y]
                    v_ref[quarter, m : m + half] = real[n]
                    v_ref[quarter, q : q + half] = imag[n]
        for x in same:
            for a in range(x, x + TILE):
                n = x + TILE - a
                for k in range(depth):
                    ar, ai = yr[quarter, k, a], yi[quarter, k, a]
                    term = ar * ar + ai * ai
                    auto = term if k == 0 else auto + term
                    if n > 1:
                        br, bi, bdiff = (ref[quarter, k, a + 1 : a + n] for ref in (yr, yi, yd))
                        asum = ys[quarter, k, a]
                        first = ar * br if k == 0 else first + ar * br
                        second = ai * bi if k == 0 else second + ai * bi
                        third = asum * bdiff if k == 0 else third + asum * bdiff
                m = real_row[a, a]
                v_ref[quarter, m] = auto
                if n > 1:
                    q = imag_row[a, a + 1]
                    v_ref[quarter, m + 1 : m + n] = first + second
                    v_ref[quarter, q : q + n - 1] = third - (first - second)

    def lag_sums(i, which):
        p = i // QUARTERS
        quarter = i % QUARTERS
        top, size = {"all": (0, rows), "early": (0, early), "late": (early, rows - early)}[which]
        here = slice(top, top + size)
        turned[here] = pltpu.roll(scale_ref[here], LANES - (p * blocks + quarter * SUB), 1)
        for b in range(SUB):
            v = v_flat[pl.ds(quarter * (rows * SUB) + top * SUB + b, size, stride=SUB), :] * turned[here, b : b + 1]
            vh[here, b * LANES : (b + 1) * LANES] = v.astype(jnp.bfloat16)
        values = dot(vh[here], wh[quarter]) + dot(vh[here], wl[quarter])

        @pl.when(quarter == 0)
        def _():
            z_ref[here] = values

        @pl.when(quarter > 0)
        def _():
            z_ref[here] += values

        @pl.when(quarter == QUARTERS - 1)
        def _():
            if which != "early":
                picked = dot(pick_b[...], z_ref[...].astype(jnp.bfloat16)).reshape(-1, 2 * TILE, LAGS)
                zs_b[p] = picked[:owners].astype(jnp.bfloat16)
                zs_c[p] = picked[owners:].reshape(zs_c.shape[1:]).astype(jnp.bfloat16)
            if which != "late":
                picked = dot(pick_a[...], z_ref[:early].astype(jnp.bfloat16))
                zs_a[p] = picked.reshape(zs_a.shape[1:]).astype(jnp.bfloat16)
            for shift in range(1, owners):
                target = lax.rem(t + shift, owners)
                if which != "early":
                    scatter_copy(p, shift, "last", target, t).start()

                    @pl.when(is_late(target))
                    def _():
                        scatter_copy(p, shift, "late", target, t).start()

                if which != "late":
                    @pl.when(jnp.logical_not(is_late(target)))
                    def _():
                        scatter_copy(p, shift, "early", target, t).start()

        if which != "early" and mine > 1:
            @pl.when((quarter == QUARTERS - 1) & (p > 0))
            def _():
                reduce_period(p - 1)

    normal = steps - QUARTERS
    ahead = 3 if normal else 0

    def step(m, _):
        stages = (normal + ahead) // ahead
        i = m - ahead * ((m // ahead + stages - 1) // stages)

        @pl.when((m < ahead) | (m >= 2 * ahead))
        def _():
            products(i, False)
            products(i, True)

        pl.when(m == ahead)(make_scale)

        @pl.when(m >= ahead)
        def _():
            lag_sums(i, "all")

        return 0

    def last_step(n, _):
        i = normal + n % QUARTERS
        for late in (False, True):

            @pl.when(n // QUARTERS == int(late))
            def _():
                products(i, late)
                lag_sums(i, "late" if late else "early")

        return 0

    own_copy.wait()
    if normal:
        lax.fori_loop(0, normal + ahead, step, 0)
    else:
        make_scale()
    lax.fori_loop(0, 2 * QUARTERS, last_step, 0)
    for p in range(mine - 1):
        start_final(p)
    for shift in range(1, groups):
        for copy in small_copies(shift):
            copy.wait_send()
    all_of(wall.at[pl.ds(0, owners - 1)], gs_sem).wait()
    reduce_period(mine - 1)
    start_final(mine - 1)
    all_of(xall.at[pl.ds(local, stations - local)], xs_sem).wait()
    all_of(rb.at[:, pl.ds(0, owners - 1)], rs_sem).wait()

    flip = (
        lax.broadcasted_iota(jnp.int32, (lags, lags), 0) + lax.broadcasted_iota(jnp.int32, (lags, lags), 1) == lags - 1
    ).astype(jnp.bfloat16)
    factor = 1.0 / math.sqrt(periods * blocks * LANES)

    def wait_final(which, count):
        @pl.when(plane == me)
        def _():
            all_of(fr.at[pl.ds(0, wide - 1), pl.ds(0, count)], fr_sem.at[which]).wait()

        @pl.when(plane != me)
        def _():
            all_of(fr.at[:, pl.ds(0, count)], fr_sem.at[which]).wait()

    def transform(first, last):
        values, low = [], []
        for g in range(groups):
            for p in range(first, last):
                value = fr[g * split, p]
                for h in range(1, split):
                    value = value + fr[g * split + h, p]
                rc, rs = value[0, :, :lags], value[0, :, lags:]
                ic, im_s = value[1, :, :lags], value[1, :, lags:]
                values.append((g * mine + p, rc + im_s, ic - rs))
                low += [rc - im_s, ic + rs]
        low = jnp.concatenate(low, axis=0) if len(low) > 1 else low[0]
        high = low.astype(jnp.bfloat16)
        rest = low - high.astype(jnp.float32)
        middle = rest.astype(jnp.bfloat16)
        rest = (rest - middle.astype(jnp.float32)).astype(jnp.bfloat16)
        low = dot(high, flip) + dot(middle, flip) + dot(rest, flip)
        sums = []
        for r in range(periods):
            parts = []
            for side in range(2):
                real = imag = None
                for n, (p, re, im) in enumerate(values):
                    if side == 0:
                        re = low[2 * n * own_rows : (2 * n + 1) * own_rows]
                        im = low[(2 * n + 1) * own_rows : (2 * n + 2) * own_rows]
                    c = math.cos(2.0 * math.pi * (p * r % periods) / periods) * factor
                    s = math.sin(2.0 * math.pi * (p * r % periods) / periods) * factor
                    if abs(c) < 1e-9 * factor:
                        new_re, new_im = s * im, -s * re
                    elif abs(s) < 1e-9 * factor:
                        new_re, new_im = c * re, c * im
                    else:
                        new_re, new_im = c * re + s * im, c * im - s * re
                    real = new_re if real is None else real + new_re
                    imag = new_im if imag is None else imag + new_im
                parts.append((real, imag))
            sums.append(parts)
        return sums

    if mine > 1:
        wait_final(0, mine - 1)
        for r, parts in enumerate(transform(0, mine - 1)):
            for side, (real, imag) in enumerate(parts):
                cols = slice(side * lags, (side + 1) * lags)
                gf[0, r, :, cols] = real
                gf[1, r, :, cols] = imag
    wait_final(1, 1)
    for r, parts in enumerate(transform(mine - 1, mine)):
        for side, pair in enumerate(parts):
            cols = slice(side * lags, (side + 1) * lags)
            for n, value in enumerate(pair):
                if mine > 1:
                    value = value + gf[n, r, :, cols]
                out_ref[n, pl.ds(side * periods + r, own_rows, stride=2 * periods), :] = value

    @pl.when(plane == me)
    def _():
        all_of(fs.at[pl.ds(0, wide - 1)], fs_sem).wait()

    @pl.when(plane != me)
    def _():
        all_of(fs, fs_sem).wait()


def per_device(spectra, flags, poly_index, delay_model, partner_order):
    local, periods, depth, _, channels = spectra.shape
    groups = lax.axis_size("stn")
    owners = lax.axis_size("tm")
    stations = local * groups
    mine = periods // groups
    blocks = flags.shape[-1]
    split = owners // stations
    wide = groups * split
    own_rows = stations // wide
    span = stations // split
    rows = stations * stations
    pairs = stations * (stations + 1) // 2
    steps = mine * QUARTERS
    width = channels // QUARTERS
    lanes = LANES
    assert channels == blocks * LANES and width == SUB * LANES and stations % TILE == 0 and mine * blocks <= lanes

    x = spectra.reshape(local, periods, depth, 2, blocks, LANES).transpose(0, 1, 2, 4, 3, 5)
    x = x.reshape(local, periods, depth, 2 * blocks, LANES)
    high, low = lag_tables(channels)
    pick_a, pick_b = pick_matrices(stations, groups, owners)
    units = span // TILE
    runs = arrivals(stations, groups)
    hbm = pl.BlockSpec(memory_space=pltpu.HBM)
    f32, bf16, i32 = jnp.float32, jnp.bfloat16, jnp.int32
    spectra_rows = stations * depth
    dma = pltpu.SemaphoreType.DMA
    out = pl.pallas_call(
        functools.partial(kernel, (groups, owners, stations, periods, depth, blocks)),
        out_shape=jax.ShapeDtypeStruct((2, own_rows * 2 * periods, LAGS // 2), f32),
        in_specs=[hbm] * 9,
        out_specs=pl.BlockSpec(memory_space=pltpu.VMEM),
        scratch_shapes=[
            pltpu.VMEM((stations, mine, depth, 2 * blocks, LANES), bf16),
            pltpu.VMEM(flags.shape, i32),
            pltpu.VMEM((local, depth, periods), i32),
            pltpu.SMEM(delay_model.shape[::-1], f32),
            pltpu.SMEM(partner_order.shape, i32),
            pltpu.VMEM((groups, local, depth, lanes), bf16),
            pltpu.VMEM((groups, local, depth, LANES), f32),
            pltpu.VMEM((groups, local, depth, lanes), bf16),
            pltpu.VMEM((groups, local, depth, LANES), f32),
            pltpu.VMEM((owners, groups, local, depth, lanes), bf16),
            pltpu.VMEM((stations, owners * depth, lanes), f32),
            pltpu.VMEM((spectra_rows, lanes), f32),
            pltpu.VMEM((pairs, SUB, lanes), f32),
            pltpu.VMEM((pairs, lanes), f32),
            pltpu.VMEM((rows, lanes), f32),
            pltpu.VMEM((rows, lanes), f32),
            pltpu.VMEM((spectra_rows, lanes, LANES), f32),
            pltpu.VMEM((mine, spectra_rows, LANES), f32),
            pltpu.VMEM((mine, spectra_rows, LANES), f32),
            pltpu.VMEM((mine, spectra_rows, LANES), f32),
            pltpu.VMEM((spectra_rows, SUB, LANES), f32),
            pltpu.VMEM((spectra_rows, SUB, LANES), f32),
            pltpu.VMEM(high.shape, bf16),
            pltpu.VMEM(low.shape, bf16),
            pltpu.VMEM(pick_a.shape[1:], bf16),
            pltpu.VMEM(pick_b.shape[1:], bf16),
            pltpu.VMEM((QUARTERS,) + high.shape, bf16),
            pltpu.VMEM((QUARTERS,) + low.shape, bf16),
            pltpu.VMEM((2 * depth, 2 * SUB, LANES), f32),
            pltpu.VMEM((QUARTERS, depth, stations, SUB, LANES), f32),
            pltpu.VMEM((QUARTERS, depth, stations, SUB, LANES), f32),
            pltpu.VMEM((QUARTERS, depth, stations, SUB, LANES), f32),
            pltpu.VMEM((QUARTERS, depth, stations, SUB, LANES), f32),
            pltpu.VMEM((QUARTERS, rows, SUB, LANES), f32),
            pltpu.VMEM((rows, width), bf16),
            pltpu.VMEM((rows, LAGS), f32),
            pltpu.VMEM((mine, owners, units - 1, 2 * TILE, LAGS), bf16),
            pltpu.VMEM((mine, owners, 2 * TILE, LAGS), bf16),
            pltpu.VMEM((mine, TILE * split, units - 1, 2 * TILE, LAGS), bf16),
            pltpu.VMEM((mine, owners, units, 2 * TILE, LAGS), bf16),
            pltpu.VMEM((units, 2 * TILE, LAGS), f32),
            pltpu.VMEM((wide, mine, 2, own_rows, LAGS), f32),
            pltpu.VMEM((wide, mine, 2, own_rows, LAGS), f32),
            pltpu.VMEM((2, periods, own_rows, LAGS), f32),
            dma((8,)),
            dma,
            dma,
            dma((steps + QUARTERS,)),
            dma((2, groups - 1)),
            dma((2, groups - 1)),
            dma,
            dma,
            dma,
            dma((mine,)),
            dma,
            dma((2,)),
            pltpu.SemaphoreType.REGULAR,
            pltpu.SemaphoreType.REGULAR,
        ],
        compiler_params=pltpu.CompilerParams(collective_id=0, has_side_effects=True, vmem_limit_bytes=40 << 20),
        name="correlate",
    )(*(
        pltpu.with_memory_space_constraint(value, pltpu.HBM)
        for value in (
            x, flags, poly_index.transpose(0, 2, 1), delay_model.T, partner_order,
            jnp.asarray(high), jnp.asarray(low), jnp.asarray(pick_a), jnp.asarray(pick_b),
        )
    ))
    out = out.reshape(2, own_rows, 2, periods, LAGS // 2).transpose(0, 1, 3, 2, 4)
    return out.reshape(2, own_rows, periods, LAGS)


def solution(mesh):
    return jax.shard_map(
        per_device,
        mesh=mesh,
        in_specs=(
            P("stn", None, "tm", None, None),
            P("stn", None, "tm", None),
            P("stn", None, "tm"),
            P(),
            P(),
        ),
        out_specs=P(None, ("stn", "tm"), None, None),
        check_vma=False,
    )
```

```python
import functools
import math

import jax
import jax.numpy as jnp
import numpy as np
from jax import lax
from jax.experimental import pallas as pl
from jax.experimental.pallas import tpu as pltpu
from jax.sharding import PartitionSpec as P

LAGS = 256
QUARTERS = 4
LANES = 128
SUB = 8
TILE = 4
MESH = pl.DeviceIdType.MESH


def lag_tables(channels):
    lags = np.arange(1, LAGS // 2 + 1)
    j = np.arange(channels // QUARTERS)
    angle = (j[:, None] * lags[None, :] % channels) * (2.0 * np.pi / channels)
    table = np.concatenate([np.cos(angle), np.sin(angle)], axis=1).astype(np.float32)
    high = table.astype(jnp.bfloat16)
    low = (table - high.astype(np.float32)).astype(jnp.bfloat16)
    return high, low


def pair_rows(stations):
    last = stations - TILE
    kinds = []
    real, imag, order = {}, {}, {}
    row = 0
    for late in (False, True):
        off = [(x, y) for x in range(0, stations, TILE) for y in range(x + TILE, stations, TILE) if (y == last) == late]
        same = [last] if late else list(range(0, last, TILE))
        for part in (real, imag):
            skip = 0 if part is real else 1
            start = row
            keys = [(x + i, y + j) for x, y in off for i in range(TILE) for j in range(TILE)]
            keys += [(x + i, x + j) for x in same for i in range(TILE) for j in range(i + skip, TILE)]
            for key in keys:
                part[key] = row
                row += 1
                if part is real:
                    order[key] = len(order)
        kinds.append((off, same))
    return kinds, real, imag, order


def late_first(local):
    return local // 4 if local >= 2 * TILE else 0


def relative(station, plane, groups, local):
    slot = (station // local - plane) % groups
    place = station % local
    return slot * local + (place if slot == 0 else (place + late_first(local)) % local)


def pick_matrices(stations, groups, owners):
    _, real, imag, _ = pair_rows(stations)
    split = owners // stations
    wide = groups * split
    local = stations // groups
    units = stations // split // TILE
    rows = stations * stations
    early = (stations - TILE) ** 2
    pick_a = np.zeros((groups, owners, units - 1, 2, TILE, rows), np.float32)
    pick_b = np.zeros((groups, owners, 2, TILE, rows), np.float32)
    pick_c = np.zeros((groups, TILE * split, units - 1, 2, TILE, rows), np.float32)
    for g in range(groups):
        for t in range(owners):
            a = relative((t % wide // split + g) % groups * local + t // wide, g, groups, local)
            late = a >= stations - TILE
            for u in range(units):
                for n in range(TILE):
                    b = (t % split * units + u) * TILE + n
                    key = (min(a, b), max(a, b))
                    if u == units - 1:
                        target = pick_b[g, t]
                    elif late:
                        target = pick_c[g, (a - stations + TILE) * split + t % split, u]
                    else:
                        target = pick_a[g, t, u]
                    target[0, n, real[key]] = 1.0
                    if a != b:
                        target[1, n, imag[key]] = 1.0 if a < b else -1.0
    pick_a = pick_a.reshape(groups, -1, rows)
    assert not pick_a[:, :, early:].any()
    pick_b = np.concatenate([pick_b.reshape(groups, -1, rows), pick_c.reshape(groups, -1, rows)], axis=1)
    return pick_a[:, :, :early].astype(jnp.bfloat16), pick_b.astype(jnp.bfloat16)


def arrivals(stations, groups):
    local = stations // groups
    runs = []
    for shift in range(1, groups):
        slot = groups - shift
        turn = late_first(local)
        places = [((i - turn) % local, slot * local + i) for i in range(local)]
        for source, here in places:
            late = here >= stations - TILE
            if runs and runs[-1][:2] == (late, shift) and source == runs[-1][2] + runs[-1][3]:
                runs[-1] = (late, shift, runs[-1][2], runs[-1][3] + 1, runs[-1][4])
            else:
                runs.append((late, shift, source, 1, here))
    return runs


def dot(a, b):
    return jnp.dot(a, b, preferred_element_type=jnp.float32)


SIN = [(-1) ** n * math.pi ** (2 * n + 1) / math.factorial(2 * n + 1) for n in range(6)]
COS = [(-1) ** n * math.pi ** (2 * n) / math.factorial(2 * n) for n in range(7)]


def cos_sin_turns(turns):
    frac = turns - jnp.floor(turns + 0.5)
    square = frac * frac
    s = jnp.full_like(square, SIN[-1])
    for coef in SIN[-2::-1]:
        s = s * square + coef
    s = s * frac
    c = jnp.full_like(square, COS[-1])
    for coef in COS[-2::-1]:
        c = c * square + coef
    return 1.0 - 2.0 * (s * s), 2.0 * (s * c)


def kernel(
    sizes,
    x_hbm, flags_hbm, index_hbm, model_hbm, partner_hbm, high_hbm, low_hbm, pick_a_hbm, pick_b_hbm,
    out_ref,
    xall, flags, index_ref, model_ref, partner_ref, wsend, dsend, wbuf, dbuf, wall, wf, wrow, acc, counts, scale_ref, turned,
    wide_w, dsplat, step_c, step_s, base_c, base_s, th, tl, pick_a, pick_b, wh, wl, tmp, yr, yi, ys, yd, v_ref, vh, z_ref,
    zs_a, zs_b, zs_c, rb, red, fs, fr, gf,
    table_sem, own_sem, xs_sem, xr_sem, ws_sem, wr_sem, gs_sem, gr_sem, rs_sem, rr_sem, fs_sem, fr_sem, up_sem, down_sem,
):
    groups, owners, stations, periods, depth, blocks = sizes
    local = stations // groups
    mine = periods // groups
    split = owners // stations
    wide = groups * split
    span = stations // split
    own_rows = stations // wide
    rows = stations * stations
    steps = mine * QUARTERS
    lags = LAGS // 2
    me = lax.axis_index("stn")
    t = lax.axis_index("tm")
    home = t // wide
    place = t % wide
    plane = (place // split + me) % groups
    part = t % split
    units = span // TILE
    early = (stations - TILE) ** 2
    turn_by = late_first(local)
    runs = arrivals(stations, groups)
    kinds, real_row, imag_row, pair_order = pair_rows(stations)
    pairs = len(real_row)

    def relative_here(station):
        slot = (station // local - me + groups) % groups
        return slot * local + (station % local + (slot + groups - 1) // groups * turn_by) % local

    mine_a = relative_here(plane * local + home)
    total_steps = 2 * steps
    full = 2 * (mine - 1) * QUARTERS

    def sub_step(n):
        last = n // full if full else 1
        i = (1 - last) * (n // 2) + last * ((mine - 1) * QUARTERS + (n + QUARTERS * 2 - full % (QUARTERS * 2)) % QUARTERS)
        kind = (1 - last) * (n % 2) + last * ((n + total_steps - full) // QUARTERS - total_steps // QUARTERS)
        return i, kind

    def band(i):
        return pl.ds(pl.multiple_of((i % QUARTERS) * 2 * SUB, 2 * SUB), 2 * SUB)

    own_copy = pltpu.make_async_copy(x_hbm.at[:, pl.ds(me * mine, mine)], xall.at[pl.ds(0, local)], own_sem)

    def all_of(ref, sem):
        return pltpu.make_async_copy(ref, ref, sem)

    tables = [
        pltpu.make_async_copy(source, target, table_sem.at[n])
        for n, (source, target) in enumerate((
            (flags_hbm, flags), (index_hbm, index_ref), (high_hbm, th), (low_hbm, tl),
            (pick_a_hbm.at[me], pick_a), (pick_b_hbm.at[me], pick_b), (partner_hbm, partner_ref),
            (model_hbm, model_ref),
        ))
    ]
    barrier = pltpu.get_barrier_semaphore()
    is_root = (me == 0) & (t == 0)
    others = groups * owners - 1

    def tell(sem, peer):
        pl.semaphore_signal(sem, inc=1, device_id=peer, device_id_type=MESH)

    def tell_all(sem):
        def one(n, _):
            tell(sem, {"stn": (n + 1) // owners, "tm": (n + 1) % owners})
            return 0

        lax.fori_loop(0, others, one, 0)

    for shift in range(1, groups):
        tell(barrier, {"stn": lax.rem(me + shift, groups)})

    @pl.when(is_root)
    def _():
        tell_all(barrier)

    for copy in tables:
        copy.start()

    own_copy.start()

    @pl.when(is_root)
    def _():
        pl.semaphore_wait(barrier, groups - 1)

    @pl.when(jnp.logical_not(is_root))
    def _():
        pl.semaphore_wait(barrier, groups)
        tell(up_sem, {"stn": 0, "tm": 0})


    def small_copies(shift):
        target = lax.rem(me + shift, groups)
        return [
            pltpu.make_async_remote_copy(
                src_ref=ref.at[target], dst_ref=buf.at[groups - shift], send_sem=ws_sem.at[n, shift - 1],
                recv_sem=wr_sem.at[n, shift - 1], device_id={"stn": target}, device_id_type=MESH,
            )
            for n, (ref, buf) in enumerate(((wsend, wbuf), (dsend, dbuf)))
        ]

    def arrival(i, late):
        last = i // ((mine - 1) * QUARTERS) if mine > 1 else 1
        return i + last * QUARTERS * int(late)

    def spectra_copy(n, i):
        late, shift, source, count, here = runs[n]
        target = lax.rem(me + shift, groups)
        return pltpu.make_async_remote_copy(
            src_ref=x_hbm.at[pl.ds(source, count), target * mine + i // QUARTERS, :, band(i), :],
            dst_ref=xall.at[pl.ds(here, count), i // QUARTERS, :, band(i), :],
            send_sem=xs_sem, recv_sem=xr_sem.at[arrival(i, late)],
            device_id={"stn": target}, device_id_type=MESH,
        )

    def start_spectra(n, _):
        i, kind = sub_step(n)
        for late in (False, True):

            @pl.when(kind == int(late))
            def _():
                for r in range(len(runs)):
                    if runs[r][0] == late:
                        spectra_copy(r, i).start()

        return 0

    lax.fori_loop(0, 2, start_spectra, 0)

    tables[1].wait()
    tables[7].wait()
    index = index_ref[...]

    def look_up(n, coef):
        here = index == n
        return tuple(jnp.where(here, model_ref[c, n], coef[c]) for c in range(3))

    none = jnp.zeros(index.shape, jnp.float32)
    coef = lax.fori_loop(0, model_ref.shape[1], look_up, (none, none, none), unroll=4)
    total = depth * owners
    times = (
        lax.broadcasted_iota(jnp.int32, index.shape, 2) * total + t * depth + lax.broadcasted_iota(jnp.int32, index.shape, 1)
    ).astype(jnp.float32)
    moment = times / float(periods * total)
    delay = (coef[0] + coef[1] * moment + coef[2] * moment * moment) * (0.5 / (blocks * LANES))
    dsend[...] = jnp.zeros_like(dsend)
    for g in range(groups):
        dsend[g, :, :, :mine] = delay[:, :, g * mine : (g + 1) * mine]
    tables[0].wait()
    for g in range(groups):
        pieces = [flags[:, g * mine + p].astype(jnp.float32) for p in range(mine)]
        gap = wsend.shape[-1] - mine * blocks
        if gap:
            pieces.append(jnp.ones(pieces[0].shape[:-1] + (gap,), jnp.float32))
        both = jnp.concatenate(pieces, axis=-1) if len(pieces) > 1 else pieces[0]
        wsend[g] = (1.0 - both).astype(jnp.bfloat16)
    wbuf[0] = wsend[me]
    dbuf[0] = dsend[me]
    for shift in range(1, groups):
        for copy in small_copies(shift):
            copy.start()
    lax.fori_loop(2, total_steps, start_spectra, 0)

    @pl.when(is_root)
    def _():
        pl.semaphore_wait(up_sem, others)
        tell_all(down_sem)

    for copy in tables[2:7]:
        copy.wait()
    lag = lax.broadcasted_iota(jnp.int32, (1, lags), 1) + 1
    for quarter in range(QUARTERS):
        turn = (lag * quarter) % 4
        cq = jnp.where(turn == 0, 1.0, jnp.where(turn == 2, -1.0, 0.0))
        sq = jnp.where(turn == 1, 1.0, jnp.where(turn == 3, -1.0, 0.0))

        def turn_rows(n, _, quarter=quarter, cq=cq, sq=sq):
            r = pl.ds(pl.multiple_of(n * LANES, LANES), LANES)
            for source, target in ((th, wh), (tl, wl)):
                c = source[r, :lags].astype(jnp.float32)
                s = source[r, lags:].astype(jnp.float32)
                target[quarter, r, :lags] = (c * cq - s * sq).astype(jnp.bfloat16)
                target[quarter, r, lags:] = (s * cq + c * sq).astype(jnp.bfloat16)
            return 0

        lax.fori_loop(0, th.shape[0] // LANES, turn_rows, 0)

    for shift in range(1, groups):
        for copy in small_copies(shift):
            copy.wait_recv()

    @pl.when(jnp.logical_not(is_root))
    def _():
        pl.semaphore_wait(down_sem, 1)

    def gather_copy(shift, source):
        return pltpu.make_async_remote_copy(
            src_ref=wbuf, dst_ref=wall.at[source], send_sem=gs_sem, recv_sem=gr_sem,
            device_id={"tm": lax.rem(t + shift, owners)}, device_id_type=MESH,
        )

    for shift in range(1, owners):
        gather_copy(shift, t).start()
    wall[t] = wbuf[...]

    for g in range(groups):
        for l in range(local):
            r = (g * local + (l + turn_by * min(g, 1)) % local) * depth
            wrow[r : r + depth, :] = wbuf[g, l].astype(jnp.float32)
            d = dbuf[g, l]
            for p in range(mine):
                dsplat[p, r : r + depth, :] = jnp.broadcast_to(d[:, p : p + 1], d.shape)
    c, s = cos_sin_turns(dsplat[...] * float(SUB * LANES))
    step_c[...] = c
    step_s[...] = s
    channel = (
        lax.broadcasted_iota(jnp.int32, (SUB, LANES), 0) * LANES + lax.broadcasted_iota(jnp.int32, (SUB, LANES), 1)
    ).astype(jnp.float32)
    spectra = stations * depth

    def start_phases(p):
        def one(r, _):
            c, s = cos_sin_turns(dsplat[p, pl.ds(r, 1), :] * channel)
            base_c[p % 2, r] = c
            base_s[p % 2, r] = s
            return 0

        lax.fori_loop(0, spectra, one, 0, unroll=8)

    w_t = wrow[...].T
    for r in range(spectra):
        wide_w[r] = jnp.broadcast_to(w_t[:, r : r + 1], (w_t.shape[0], LANES))

    acc_flat = acc.reshape(pairs * SUB, LANES)
    v_flat = v_ref.reshape(QUARTERS * rows * SUB, LANES)

    def make_scale():
        all_of(wall.at[pl.ds(0, owners - 1)], gr_sem).wait()
        for n in range(owners):
            for g in range(groups):
                turn = turn_by * min(g, 1)
                value = wall[n, g].astype(jnp.float32)
                at = slice(n * depth, (n + 1) * depth)
                wf[g * local + turn : (g + 1) * local, at, :] = value[: local - turn]
                if turn:
                    wf[g * local : g * local + turn, at, :] = value[local - turn :]
        for a in range(stations):
            for b0 in range(a // TILE * TILE, stations, TILE):
                b = max(a, b0)
                count = b0 + TILE - b
                product = wf[a][None] * wf[b : b + count]
                m = pair_order[a, b]
                acc[m : m + count] = jnp.sum(product.reshape(count, owners * depth // SUB, SUB, LANES), axis=1)
        count = acc_flat[pl.ds(0, pairs, stride=SUB), :]
        for b in range(1, SUB):
            count = count + acc_flat[pl.ds(b, pairs, stride=SUB), :]
        counts[...] = 1.0 / jnp.sqrt(jnp.maximum(count, 1.0))
        for off, same in kinds:
            pieces = []
            if off:
                x, y = off[0]
                n = len(off) * TILE * TILE
                pieces += [(real_row[x, y], pair_order[x, y], n), (imag_row[x, y], pair_order[x, y], n)]
            for x in same:
                if x == same[0]:
                    n = len(same) * TILE * (TILE + 1) // 2
                    pieces.append((real_row[x, x], pair_order[x, x], n))
                for i in range(TILE - 1):
                    pieces.append((imag_row[x + i, x + i + 1], pair_order[x + i, x + i + 1], TILE - 1 - i))
            for row, source, n in pieces:
                scale_ref[row : row + n, :] = counts[source : source + n, :]

    def station_of(target):
        return relative_here((target % wide // split + me) % groups * local + target // wide)

    def scatter_copy(p, shift, what, target, source):
        if what == "last":
            src, dst = zs_b.at[p, target], rb.at[p, source, units - 1]
        elif what == "early":
            src, dst = zs_a.at[p, target], rb.at[p, source, pl.ds(0, units - 1)]
        else:
            late = (station_of(target) + TILE) % stations * split + target % split
            src, dst = zs_c.at[p, late], rb.at[p, source, pl.ds(0, units - 1)]
        return pltpu.make_async_remote_copy(
            src_ref=src, dst_ref=dst, send_sem=rs_sem,
            recv_sem=rr_sem.at[p], device_id={"tm": lax.rem(t + shift, owners)}, device_id_type=MESH,
        )

    def is_late(target):
        return station_of(target) >= stations - TILE

    def final_copy(p, w, source, piece):
        return pltpu.make_async_remote_copy(
            src_ref=fs.at[w, p], dst_ref=fr.at[source * split + piece, p], send_sem=fs_sem,
            recv_sem=fr_sem.at[p // (mine - 1) if mine > 1 else 1], device_id={"stn": plane, "tm": home * wide + w}, device_id_type=MESH,
        )

    def reduce_period(p):
        all_of(rb.at[p, pl.ds(0, owners - 1)], rr_sem.at[p]).wait()
        late = jnp.where(is_late(t), 1.0, 0.0)
        first = zs_a[p, t].astype(jnp.float32)
        first += late * zs_c[p, (mine_a % TILE) * split + part].astype(jnp.float32)
        last = zs_b[p, t].astype(jnp.float32)
        for shift in range(1, owners):
            source = lax.rem(t + owners - shift, owners)
            first += rb[p, source, : units - 1].astype(jnp.float32)
            last += rb[p, source, units - 1].astype(jnp.float32)
        red[: units - 1] = first
        red[units - 1] = last
        for w in range(wide):
            for n in range(own_rows):
                b = relative_here(partner_ref[w * own_rows + n])
                if split > 1:
                    keep = jnp.where(b // span == part, 1.0, 0.0)
                    b = b % span
                for ri in range(2):
                    row = red[b // TILE, pl.ds(ri * TILE + b % TILE, 1), :]
                    fs[w, p, ri, n : n + 1, :] = row * keep if split > 1 else row
        for w in range(wide):
            @pl.when((plane == me) & (w == place))
            def _():
                fr[me * split + part, p] = fs[w, p]

    def start_final(p):
        for w in range(wide):
            @pl.when(jnp.logical_not((plane == me) & (w == place)))
            def _():
                final_copy(p, w, me, part).start()

    half = TILE // 2

    def products(i, late):
        p = i // QUARTERS
        quarter = i % QUARTERS
        at = pl.ds(pl.multiple_of(p * blocks + quarter * SUB, SUB), SUB)
        first_station = stations - TILE if late else 0
        off, same = kinds[late]

        def wait_spectra(low, high):
            piece = xall.at[pl.ds(low, high - low), p, :, band(i), :]
            all_of(piece, xr_sem.at[arrival(i, late)]).wait()

        if late:
            @pl.when(i >= steps - QUARTERS)
            def _():
                wait_spectra(stations - TILE, stations)
        else:
            @pl.when(i < steps - QUARTERS)
            def _():
                wait_spectra(local, stations)

            @pl.when(i >= steps - QUARTERS)
            def _():
                wait_spectra(local, stations - TILE)

            @pl.when((quarter == 1) & (p < mine - 1))
            def _():
                start_phases(p + 1)

        def rotate(n, _):
            for j in range(2):
                s = first_station + n * 2 + j
                for k in range(depth):
                    r = s * depth + k
                    tmp[j * depth + k] = xall[s, p, k, band(i), :].astype(jnp.float32)
                    real = tmp[j * depth + k, pl.ds(0, SUB, stride=2), :]
                    imag = tmp[j * depth + k, pl.ds(1, SUB, stride=2), :]
                    c = base_c[p % 2, r]
                    sn = base_s[p % 2, r]
                    w = wide_w[r, at, :]
                    new_real = (w * (real * c + imag * sn)).astype(jnp.bfloat16).astype(jnp.float32)
                    new_imag = (w * (imag * c - real * sn)).astype(jnp.bfloat16).astype(jnp.float32)
                    yr[quarter, k, s] = new_real
                    yi[quarter, k, s] = new_imag
                    ys[quarter, k, s] = new_real + new_imag
                    yd[quarter, k, s] = new_real - new_imag
                    pc = step_c[p, pl.ds(r, 1), :]
                    ps = step_s[p, pl.ds(r, 1), :]
                    base_c[p % 2, r] = c * pc - sn * ps
                    base_s[p % 2, r] = sn * pc + c * ps
            return 0

        lax.fori_loop(0, (TILE if late else stations - TILE) // 2, rotate, 0)

        for x, y0 in off:
            for y in (y0, y0 + half):
                for k in range(depth):
                    ar, ai, asum = (ref[quarter, k, x : x + TILE][:, None] for ref in (yr, yi, ys))
                    br, bi, bdiff = (ref[quarter, k, y : y + half][None] for ref in (yr, yi, yd))
                    first = ar * br if k == 0 else first + ar * br
                    second = ai * bi if k == 0 else second + ai * bi
                    third = asum * bdiff if k == 0 else third + asum * bdiff
                real = first + second
                imag = third - (first - second)
                for n in range(TILE):
                    m = real_row[x + n, y]
                    q = imag_row[x + n, y]
                    v_ref[quarter, m : m + half] = real[n]
                    v_ref[quarter, q : q + half] = imag[n]
        for x in same:
            for a in range(x, x + TILE):
                n = x + TILE - a
                for k in range(depth):
                    ar, ai = yr[quarter, k, a], yi[quarter, k, a]
                    term = ar * ar + ai * ai
                    auto = term if k == 0 else auto + term
                    if n > 1:
                        br, bi, bdiff = (ref[quarter, k, a + 1 : a + n] for ref in (yr, yi, yd))
                        asum = ys[quarter, k, a]
                        first = ar * br if k == 0 else first + ar * br
                        second = ai * bi if k == 0 else second + ai * bi
                        third = asum * bdiff if k == 0 else third + asum * bdiff
                m = real_row[a, a]
                v_ref[quarter, m] = auto
                if n > 1:
                    q = imag_row[a, a + 1]
                    v_ref[quarter, m + 1 : m + n] = first + second
                    v_ref[quarter, q : q + n - 1] = third - (first - second)

    def lag_sums(i, which):
        p = i // QUARTERS
        quarter = i % QUARTERS
        top, size = {"all": (0, rows), "early": (0, early), "late": (early, rows - early)}[which]
        here = slice(top, top + size)
        turned[here] = pltpu.roll(scale_ref[here], LANES - (p * blocks + quarter * SUB), 1)
        for b in range(SUB):
            v = v_flat[pl.ds(quarter * (rows * SUB) + top * SUB + b, size, stride=SUB), :] * turned[here, b : b + 1]
            vh[here, b * LANES : (b + 1) * LANES] = v.astype(jnp.bfloat16)
        values = dot(vh[here], wh[quarter]) + dot(vh[here], wl[quarter])

        @pl.when(quarter == 0)
        def _():
            z_ref[here] = values

        @pl.when(quarter > 0)
        def _():
            z_ref[here] += values

        @pl.when(quarter == QUARTERS - 1)
        def _():
            if which != "early":
                picked = dot(pick_b[...], z_ref[...].astype(jnp.bfloat16)).reshape(-1, 2 * TILE, LAGS)
                zs_b[p] = picked[:owners].astype(jnp.bfloat16)
                zs_c[p] = picked[owners:].reshape(zs_c.shape[1:]).astype(jnp.bfloat16)
            if which != "late":
                picked = dot(pick_a[...], z_ref[:early].astype(jnp.bfloat16))
                zs_a[p] = picked.reshape(zs_a.shape[1:]).astype(jnp.bfloat16)
            for shift in range(1, owners):
                target = lax.rem(t + shift, owners)
                if which != "early":
                    scatter_copy(p, shift, "last", target, t).start()

                    @pl.when(is_late(target))
                    def _():
                        scatter_copy(p, shift, "late", target, t).start()

                if which != "late":
                    @pl.when(jnp.logical_not(is_late(target)))
                    def _():
                        scatter_copy(p, shift, "early", target, t).start()

        if which == "all" and mine > 2:
            @pl.when(((quarter == 1) & (p >= 2)) | ((quarter == 2) & (p == mine - 2)))
            def _():
                reduce_period(p - 3 + quarter)

        if which == "late" and mine > 1:
            @pl.when(quarter == QUARTERS - 1)
            def _():
                reduce_period(p - 1)

    normal = steps - QUARTERS
    ahead = 3 if normal else 0

    def step(m, _):
        stages = (normal + ahead) // ahead
        i = m - ahead * ((m // ahead + stages - 1) // stages)

        @pl.when((m < ahead) | (m >= 2 * ahead))
        def _():
            products(i, False)
            products(i, True)

        pl.when(m == ahead)(make_scale)

        @pl.when(m >= ahead)
        def _():
            lag_sums(i, "all")

        return 0

    def last_step(n, _):
        i = normal + n % QUARTERS
        for late in (False, True):

            @pl.when(n // QUARTERS == int(late))
            def _():
                products(i, late)
                lag_sums(i, "late" if late else "early")

        return 0

    start_phases(0)
    own_copy.wait()
    if normal:
        lax.fori_loop(0, normal + ahead, step, 0)
    else:
        make_scale()
    lax.fori_loop(0, 2 * QUARTERS, last_step, 0)
    for p in range(mine - 1):
        start_final(p)
    for shift in range(1, groups):
        for copy in small_copies(shift):
            copy.wait_send()
    all_of(wall.at[pl.ds(0, owners - 1)], gs_sem).wait()
    reduce_period(mine - 1)
    start_final(mine - 1)
    all_of(xall.at[pl.ds(local, stations - local)], xs_sem).wait()
    all_of(rb.at[:, pl.ds(0, owners - 1)], rs_sem).wait()

    flip = (
        lax.broadcasted_iota(jnp.int32, (lags, lags), 0) + lax.broadcasted_iota(jnp.int32, (lags, lags), 1) == lags - 1
    ).astype(jnp.bfloat16)
    factor = 1.0 / math.sqrt(periods * blocks * LANES)

    def wait_final(which, count):
        @pl.when(plane == me)
        def _():
            all_of(fr.at[pl.ds(0, wide - 1), pl.ds(0, count)], fr_sem.at[which]).wait()

        @pl.when(plane != me)
        def _():
            all_of(fr.at[:, pl.ds(0, count)], fr_sem.at[which]).wait()

    def transform(first, last):
        values, low = [], []
        for g in range(groups):
            for p in range(first, last):
                value = fr[g * split, p]
                for h in range(1, split):
                    value = value + fr[g * split + h, p]
                rc, rs = value[0, :, :lags], value[0, :, lags:]
                ic, im_s = value[1, :, :lags], value[1, :, lags:]
                values.append((g * mine + p, rc + im_s, ic - rs))
                low += [rc - im_s, ic + rs]
        low = jnp.concatenate(low, axis=0) if len(low) > 1 else low[0]
        high = low.astype(jnp.bfloat16)
        rest = low - high.astype(jnp.float32)
        middle = rest.astype(jnp.bfloat16)
        rest = (rest - middle.astype(jnp.float32)).astype(jnp.bfloat16)
        low = dot(high, flip) + dot(middle, flip) + dot(rest, flip)
        sums = []
        for r in range(periods):
            parts = []
            for side in range(2):
                real = imag = None
                for n, (p, re, im) in enumerate(values):
                    if side == 0:
                        re = low[2 * n * own_rows : (2 * n + 1) * own_rows]
                        im = low[(2 * n + 1) * own_rows : (2 * n + 2) * own_rows]
                    c = math.cos(2.0 * math.pi * (p * r % periods) / periods) * factor
                    s = math.sin(2.0 * math.pi * (p * r % periods) / periods) * factor
                    if abs(c) < 1e-9 * factor:
                        new_re, new_im = s * im, -s * re
                    elif abs(s) < 1e-9 * factor:
                        new_re, new_im = c * re, c * im
                    else:
                        new_re, new_im = c * re + s * im, c * im - s * re
                    real = new_re if real is None else real + new_re
                    imag = new_im if imag is None else imag + new_im
                parts.append((real, imag))
            sums.append(parts)
        return sums

    if mine > 1:
        wait_final(0, mine - 1)
        for r, parts in enumerate(transform(0, mine - 1)):
            for side, (real, imag) in enumerate(parts):
                cols = slice(side * lags, (side + 1) * lags)
                gf[0, r, :, cols] = real
                gf[1, r, :, cols] = imag
    wait_final(1, 1)
    for r, parts in enumerate(transform(mine - 1, mine)):
        for side, pair in enumerate(parts):
            cols = slice(side * lags, (side + 1) * lags)
            for n, value in enumerate(pair):
                if mine > 1:
                    value = value + gf[n, r, :, cols]
                out_ref[n, pl.ds(side * periods + r, own_rows, stride=2 * periods), :] = value

    @pl.when(plane == me)
    def _():
        all_of(fs.at[pl.ds(0, wide - 1)], fs_sem).wait()

    @pl.when(plane != me)
    def _():
        all_of(fs, fs_sem).wait()


def per_device(spectra, flags, poly_index, delay_model, partner_order):
    local, periods, depth, _, channels = spectra.shape
    groups = lax.axis_size("stn")
    owners = lax.axis_size("tm")
    stations = local * groups
    mine = periods // groups
    blocks = flags.shape[-1]
    split = owners // stations
    wide = groups * split
    own_rows = stations // wide
    span = stations // split
    rows = stations * stations
    pairs = stations * (stations + 1) // 2
    steps = mine * QUARTERS
    width = channels // QUARTERS
    lanes = LANES
    assert channels == blocks * LANES and width == SUB * LANES and stations % TILE == 0 and mine * blocks <= lanes

    x = spectra.reshape(local, periods, depth, 2, blocks, LANES).transpose(0, 1, 2, 4, 3, 5)
    x = x.reshape(local, periods, depth, 2 * blocks, LANES)
    high, low = lag_tables(channels)
    pick_a, pick_b = pick_matrices(stations, groups, owners)
    units = span // TILE
    runs = arrivals(stations, groups)
    hbm = pl.BlockSpec(memory_space=pltpu.HBM)
    f32, bf16, i32 = jnp.float32, jnp.bfloat16, jnp.int32
    spectra_rows = stations * depth
    dma = pltpu.SemaphoreType.DMA
    out = pl.pallas_call(
        functools.partial(kernel, (groups, owners, stations, periods, depth, blocks)),
        out_shape=jax.ShapeDtypeStruct((2, own_rows * 2 * periods, LAGS // 2), f32),
        in_specs=[hbm] * 9,
        out_specs=pl.BlockSpec(memory_space=pltpu.VMEM),
        scratch_shapes=[
            pltpu.VMEM((stations, mine, depth, 2 * blocks, LANES), bf16),
            pltpu.VMEM(flags.shape, i32),
            pltpu.VMEM((local, depth, periods), i32),
            pltpu.SMEM(delay_model.shape[::-1], f32),
            pltpu.SMEM(partner_order.shape, i32),
            pltpu.VMEM((groups, local, depth, lanes), bf16),
            pltpu.VMEM((groups, local, depth, LANES), f32),
            pltpu.VMEM((groups, local, depth, lanes), bf16),
            pltpu.VMEM((groups, local, depth, LANES), f32),
            pltpu.VMEM((owners, groups, local, depth, lanes), bf16),
            pltpu.VMEM((stations, owners * depth, lanes), f32),
            pltpu.VMEM((spectra_rows, lanes), f32),
            pltpu.VMEM((pairs, SUB, lanes), f32),
            pltpu.VMEM((pairs, lanes), f32),
            pltpu.VMEM((rows, lanes), f32),
            pltpu.VMEM((rows, lanes), f32),
            pltpu.VMEM((spectra_rows, lanes, LANES), f32),
            pltpu.VMEM((mine, spectra_rows, LANES), f32),
            pltpu.VMEM((mine, spectra_rows, LANES), f32),
            pltpu.VMEM((mine, spectra_rows, LANES), f32),
            pltpu.VMEM((2, spectra_rows, SUB, LANES), f32),
            pltpu.VMEM((2, spectra_rows, SUB, LANES), f32),
            pltpu.VMEM(high.shape, bf16),
            pltpu.VMEM(low.shape, bf16),
            pltpu.VMEM(pick_a.shape[1:], bf16),
            pltpu.VMEM(pick_b.shape[1:], bf16),
            pltpu.VMEM((QUARTERS,) + high.shape, bf16),
            pltpu.VMEM((QUARTERS,) + low.shape, bf16),
            pltpu.VMEM((2 * depth, 2 * SUB, LANES), f32),
            pltpu.VMEM((QUARTERS, depth, stations, SUB, LANES), f32),
            pltpu.VMEM((QUARTERS, depth, stations, SUB, LANES), f32),
            pltpu.VMEM((QUARTERS, depth, stations, SUB, LANES), f32),
            pltpu.VMEM((QUARTERS, depth, stations, SUB, LANES), f32),
            pltpu.VMEM((QUARTERS, rows, SUB, LANES), f32),
            pltpu.VMEM((rows, width), bf16),
            pltpu.VMEM((rows, LAGS), f32),
            pltpu.VMEM((mine, owners, units - 1, 2 * TILE, LAGS), bf16),
            pltpu.VMEM((mine, owners, 2 * TILE, LAGS), bf16),
            pltpu.VMEM((mine, TILE * split, units - 1, 2 * TILE, LAGS), bf16),
            pltpu.VMEM((mine, owners, units, 2 * TILE, LAGS), bf16),
            pltpu.VMEM((units, 2 * TILE, LAGS), f32),
            pltpu.VMEM((wide, mine, 2, own_rows, LAGS), f32),
            pltpu.VMEM((wide, mine, 2, own_rows, LAGS), f32),
            pltpu.VMEM((2, periods, own_rows, LAGS), f32),
            dma((8,)),
            dma,
            dma,
            dma((steps + QUARTERS,)),
            dma((2, groups - 1)),
            dma((2, groups - 1)),
            dma,
            dma,
            dma,
            dma((mine,)),
            dma,
            dma((2,)),
            pltpu.SemaphoreType.REGULAR,
            pltpu.SemaphoreType.REGULAR,
        ],
        compiler_params=pltpu.CompilerParams(collective_id=0, has_side_effects=True, vmem_limit_bytes=40 << 20),
        name="correlate",
    )(*(
        pltpu.with_memory_space_constraint(value, pltpu.HBM)
        for value in (
            x, flags, poly_index.transpose(0, 2, 1), delay_model.T, partner_order,
            jnp.asarray(high), jnp.asarray(low), jnp.asarray(pick_a), jnp.asarray(pick_b),
        )
    ))
    out = out.reshape(2, own_rows, 2, periods, LAGS // 2).transpose(0, 1, 3, 2, 4)
    return out.reshape(2, own_rows, periods, LAGS)


def solution(mesh):
    return jax.shard_map(
        per_device,
        mesh=mesh,
        in_specs=(
            P("stn", None, "tm", None, None),
            P("stn", None, "tm", None),
            P("stn", None, "tm"),
            P(),
            P(),
        ),
        out_specs=P(None, ("stn", "tm"), None, None),
        check_vma=False,
    )
```

```python
import functools
import math

import jax
import jax.numpy as jnp
import numpy as np
from jax import lax
from jax.experimental import pallas as pl
from jax.experimental.pallas import tpu as pltpu
from jax.sharding import PartitionSpec as P

LAGS = 256
QUARTERS = 4
LANES = 128
SUB = 8
TILE = 4
MESH = pl.DeviceIdType.MESH


def lag_tables(channels):
    lags = np.arange(1, LAGS // 2 + 1)
    j = np.arange(channels // QUARTERS)
    angle = (j[:, None] * lags[None, :] % channels) * (2.0 * np.pi / channels)
    table = np.concatenate([np.cos(angle), np.sin(angle)], axis=1).astype(np.float32)
    high = table.astype(jnp.bfloat16)
    low = (table - high.astype(np.float32)).astype(jnp.bfloat16)
    return high, low


def pair_rows(stations):
    last = stations - TILE
    kinds = []
    real, imag, order = {}, {}, {}
    row = 0
    for late in (False, True):
        off = [(x, y) for x in range(0, stations, TILE) for y in range(x + TILE, stations, TILE) if (y == last) == late]
        same = [last] if late else list(range(0, last, TILE))
        for part in (real, imag):
            skip = 0 if part is real else 1
            start = row
            keys = [(x + i, y + j) for x, y in off for i in range(TILE) for j in range(TILE)]
            keys += [(x + i, x + j) for x in same for i in range(TILE) for j in range(i + skip, TILE)]
            for key in keys:
                part[key] = row
                row += 1
                if part is real:
                    order[key] = len(order)
        kinds.append((off, same))
    return kinds, real, imag, order


def late_first(local):
    return local // 4 if local >= 2 * TILE else 0


def relative(station, plane, groups, local):
    slot = (station // local - plane) % groups
    place = station % local
    return slot * local + (place if slot == 0 else (place + late_first(local)) % local)


def pick_matrices(stations, groups, owners):
    _, real, imag, _ = pair_rows(stations)
    split = owners // stations
    wide = groups * split
    local = stations // groups
    units = stations // split // TILE
    rows = stations * stations
    early = (stations - TILE) ** 2
    pick_a = np.zeros((groups, owners, units - 1, 2, TILE, rows), np.float32)
    pick_b = np.zeros((groups, owners, 2, TILE, rows), np.float32)
    pick_c = np.zeros((groups, TILE * split, units - 1, 2, TILE, rows), np.float32)
    for g in range(groups):
        for t in range(owners):
            a = relative((t % wide // split + g) % groups * local + t // wide, g, groups, local)
            late = a >= stations - TILE
            for u in range(units):
                for n in range(TILE):
                    b = (t % split * units + u) * TILE + n
                    key = (min(a, b), max(a, b))
                    if u == units - 1:
                        target = pick_b[g, t]
                    elif late:
                        target = pick_c[g, (a - stations + TILE) * split + t % split, u]
                    else:
                        target = pick_a[g, t, u]
                    target[0, n, real[key]] = 1.0
                    if a != b:
                        target[1, n, imag[key]] = 1.0 if a < b else -1.0
    pick_a = pick_a.reshape(groups, -1, rows)
    assert not pick_a[:, :, early:].any()
    pick_b = np.concatenate([pick_b.reshape(groups, -1, rows), pick_c.reshape(groups, -1, rows)], axis=1)
    return pick_a[:, :, :early].astype(jnp.bfloat16), pick_b.astype(jnp.bfloat16)


def arrivals(stations, groups):
    local = stations // groups
    runs = []
    for shift in range(1, groups):
        slot = groups - shift
        turn = late_first(local)
        places = [((i - turn) % local, slot * local + i) for i in range(local)]
        for source, here in places:
            late = here >= stations - TILE
            if runs and runs[-1][:2] == (late, shift) and source == runs[-1][2] + runs[-1][3]:
                runs[-1] = (late, shift, runs[-1][2], runs[-1][3] + 1, runs[-1][4])
            else:
                runs.append((late, shift, source, 1, here))
    return runs


def dot(a, b):
    return jnp.dot(a, b, preferred_element_type=jnp.float32)


SIN = [(-1) ** n * math.pi ** (2 * n + 1) / math.factorial(2 * n + 1) for n in range(6)]
COS = [(-1) ** n * math.pi ** (2 * n) / math.factorial(2 * n) for n in range(7)]


def cos_sin_turns(turns):
    frac = turns - jnp.floor(turns + 0.5)
    square = frac * frac
    s = jnp.full_like(square, SIN[-1])
    for coef in SIN[-2::-1]:
        s = s * square + coef
    s = s * frac
    c = jnp.full_like(square, COS[-1])
    for coef in COS[-2::-1]:
        c = c * square + coef
    return 1.0 - 2.0 * (s * s), 2.0 * (s * c)


def kernel(
    sizes,
    x_hbm, flags_hbm, index_hbm, model_hbm, partner_hbm, high_hbm, low_hbm, pick_a_hbm, pick_b_hbm,
    out_ref,
    xall, flags, index_ref, model_ref, partner_ref, wsend, dsend, wbuf, dbuf, wall, wf, wrow, acc, counts, scale_ref, turned,
    wide_w, dsplat, step_c, step_s, base_c, base_s, th, tl, pick_a, pick_b, wh, wl, tmp, yr, yi, ys, yd, v_ref, vh, z_ref,
    zs_a, zs_b, zs_c, rb, red, fs, fr, gf,
    table_sem, own_sem, xs_sem, xr_sem, ws_sem, wr_sem, gs_sem, gr_sem, rs_sem, rr_sem, fs_sem, fr_sem, up_sem, down_sem,
):
    groups, owners, stations, periods, depth, blocks = sizes
    local = stations // groups
    mine = periods // groups
    split = owners // stations
    wide = groups * split
    span = stations // split
    own_rows = stations // wide
    rows = stations * stations
    steps = mine * QUARTERS
    lags = LAGS // 2
    me = lax.axis_index("stn")
    t = lax.axis_index("tm")
    home = t // wide
    place = t % wide
    plane = (place // split + me) % groups
    part = t % split
    units = span // TILE
    early = (stations - TILE) ** 2
    turn_by = late_first(local)
    runs = arrivals(stations, groups)
    kinds, real_row, imag_row, pair_order = pair_rows(stations)
    pairs = len(real_row)

    def relative_here(station):
        slot = (station // local - me + groups) % groups
        return slot * local + (station % local + (slot + groups - 1) // groups * turn_by) % local

    mine_a = relative_here(plane * local + home)
    total_steps = 2 * steps
    full = 2 * (mine - 1) * QUARTERS

    def sub_step(n):
        last = n // full if full else 1
        i = (1 - last) * (n // 2) + last * ((mine - 1) * QUARTERS + (n + QUARTERS * 2 - full % (QUARTERS * 2)) % QUARTERS)
        kind = (1 - last) * (n % 2) + last * ((n + total_steps - full) // QUARTERS - total_steps // QUARTERS)
        return i, kind

    def band(i):
        return pl.ds(pl.multiple_of((i % QUARTERS) * 2 * SUB, 2 * SUB), 2 * SUB)

    own_copy = pltpu.make_async_copy(x_hbm.at[:, pl.ds(me * mine, mine)], xall.at[pl.ds(0, local)], own_sem)

    def all_of(ref, sem):
        return pltpu.make_async_copy(ref, ref, sem)

    tables = [
        pltpu.make_async_copy(source, target, table_sem.at[n])
        for n, (source, target) in enumerate((
            (flags_hbm, flags), (index_hbm, index_ref), (high_hbm, th), (low_hbm, tl),
            (pick_a_hbm.at[me], pick_a), (pick_b_hbm.at[me], pick_b), (partner_hbm, partner_ref),
            (model_hbm, model_ref),
        ))
    ]
    barrier = pltpu.get_barrier_semaphore()
    is_root = (me == 0) & (t == 0)
    others = groups * owners - 1

    def tell(sem, peer):
        pl.semaphore_signal(sem, inc=1, device_id=peer, device_id_type=MESH)

    def tell_all(sem):
        def one(n, _):
            tell(sem, {"stn": (n + 1) // owners, "tm": (n + 1) % owners})
            return 0

        lax.fori_loop(0, others, one, 0)

    for shift in range(1, groups):
        tell(barrier, {"stn": lax.rem(me + shift, groups)})

    @pl.when(is_root)
    def _():
        tell_all(barrier)

    for copy in tables:
        copy.start()

    own_copy.start()

    @pl.when(is_root)
    def _():
        pl.semaphore_wait(barrier, groups - 1)

    @pl.when(jnp.logical_not(is_root))
    def _():
        pl.semaphore_wait(barrier, groups)
        tell(up_sem, {"stn": 0, "tm": 0})


    def small_copies(shift):
        target = lax.rem(me + shift, groups)
        return [
            pltpu.make_async_remote_copy(
                src_ref=ref.at[target], dst_ref=buf.at[groups - shift], send_sem=ws_sem.at[n, shift - 1],
                recv_sem=wr_sem.at[n, shift - 1], device_id={"stn": target}, device_id_type=MESH,
            )
            for n, (ref, buf) in enumerate(((wsend, wbuf), (dsend, dbuf)))
        ]

    def arrival(i, late):
        last = i // ((mine - 1) * QUARTERS) if mine > 1 else 1
        return i + last * QUARTERS * int(late)

    def spectra_copy(n, i):
        late, shift, source, count, here = runs[n]
        target = lax.rem(me + shift, groups)
        return pltpu.make_async_remote_copy(
            src_ref=x_hbm.at[pl.ds(source, count), target * mine + i // QUARTERS, :, band(i), :],
            dst_ref=xall.at[pl.ds(here, count), i // QUARTERS, :, band(i), :],
            send_sem=xs_sem, recv_sem=xr_sem.at[arrival(i, late)],
            device_id={"stn": target}, device_id_type=MESH,
        )

    def start_spectra(n, _):
        i, kind = sub_step(n)
        for late in (False, True):

            @pl.when(kind == int(late))
            def _():
                for r in range(len(runs)):
                    if runs[r][0] == late:
                        spectra_copy(r, i).start()

        return 0

    lax.fori_loop(0, 2, start_spectra, 0)

    tables[1].wait()
    tables[7].wait()
    index = index_ref[...]

    def look_up(n, coef):
        here = index == n
        return tuple(jnp.where(here, model_ref[c, n], coef[c]) for c in range(3))

    none = jnp.zeros(index.shape, jnp.float32)
    coef = lax.fori_loop(0, model_ref.shape[1], look_up, (none, none, none), unroll=4)
    total = depth * owners
    times = (
        lax.broadcasted_iota(jnp.int32, index.shape, 2) * total + t * depth + lax.broadcasted_iota(jnp.int32, index.shape, 1)
    ).astype(jnp.float32)
    moment = times / float(periods * total)
    delay = (coef[0] + coef[1] * moment + coef[2] * moment * moment) * (0.5 / (blocks * LANES))
    dsend[...] = jnp.zeros_like(dsend)
    for g in range(groups):
        pieces = [delay[l][:, g * mine : (g + 1) * mine] for l in range(local)]
        dsend[g, :, : local * mine] = jnp.concatenate(pieces, axis=-1)
    tables[0].wait()
    for g in range(groups):
        pieces = [flags[:, g * mine + p].astype(jnp.float32) for p in range(mine)]
        gap = wsend.shape[-1] - mine * blocks
        if gap:
            pieces.append(jnp.ones(pieces[0].shape[:-1] + (gap,), jnp.float32))
        both = jnp.concatenate(pieces, axis=-1) if len(pieces) > 1 else pieces[0]
        wsend[g] = (1.0 - both).astype(jnp.bfloat16)
    wbuf[0] = wsend[me]
    dbuf[0] = dsend[me]
    for shift in range(1, groups):
        for copy in small_copies(shift):
            copy.start()
    lax.fori_loop(2, total_steps, start_spectra, 0)

    @pl.when(is_root)
    def _():
        pl.semaphore_wait(up_sem, others)
        tell_all(down_sem)

    for copy in tables[2:7]:
        copy.wait()
    lag = lax.broadcasted_iota(jnp.int32, (1, lags), 1) + 1
    for quarter in range(QUARTERS):
        turn = (lag * quarter) % 4
        cq = jnp.where(turn == 0, 1.0, jnp.where(turn == 2, -1.0, 0.0))
        sq = jnp.where(turn == 1, 1.0, jnp.where(turn == 3, -1.0, 0.0))

        def turn_rows(n, _, quarter=quarter, cq=cq, sq=sq):
            r = pl.ds(pl.multiple_of(n * LANES, LANES), LANES)
            for source, target in ((th, wh), (tl, wl)):
                c = source[r, :lags].astype(jnp.float32)
                s = source[r, lags:].astype(jnp.float32)
                target[quarter, r, :lags] = (c * cq - s * sq).astype(jnp.bfloat16)
                target[quarter, r, lags:] = (s * cq + c * sq).astype(jnp.bfloat16)
            return 0

        lax.fori_loop(0, th.shape[0] // LANES, turn_rows, 0)

    for shift in range(1, groups):
        for copy in small_copies(shift):
            copy.wait_recv()

    @pl.when(jnp.logical_not(is_root))
    def _():
        pl.semaphore_wait(down_sem, 1)

    def gather_copy(shift, source):
        return pltpu.make_async_remote_copy(
            src_ref=wbuf, dst_ref=wall.at[source], send_sem=gs_sem, recv_sem=gr_sem,
            device_id={"tm": lax.rem(t + shift, owners)}, device_id_type=MESH,
        )

    for shift in range(1, owners):
        gather_copy(shift, t).start()
    wall[t] = wbuf[...]

    for g in range(groups):
        for l in range(local):
            r = (g * local + (l + turn_by * min(g, 1)) % local) * depth
            wrow[r : r + depth, :] = wbuf[g, l].astype(jnp.float32)
            d = dbuf[g]
            for p in range(mine):
                n = l * mine + p
                dsplat[p, r : r + depth, :] = jnp.broadcast_to(d[:, n : n + 1], d.shape)
    c, s = cos_sin_turns(dsplat[...] * float(SUB * LANES))
    step_c[...] = c
    step_s[...] = s
    channel = (
        lax.broadcasted_iota(jnp.int32, (SUB, LANES), 0) * LANES + lax.broadcasted_iota(jnp.int32, (SUB, LANES), 1)
    ).astype(jnp.float32)
    spectra = stations * depth

    def start_phases(p):
        def one(r, _):
            c, s = cos_sin_turns(dsplat[p, pl.ds(r, 1), :] * channel)
            base_c[p % 2, r] = c
            base_s[p % 2, r] = s
            return 0

        lax.fori_loop(0, spectra, one, 0, unroll=8)

    w_t = wrow[...].T
    for r in range(spectra):
        wide_w[r] = jnp.broadcast_to(w_t[:, r : r + 1], (w_t.shape[0], LANES))

    acc_flat = acc.reshape(pairs * SUB, LANES)
    v_flat = v_ref.reshape(QUARTERS * rows * SUB, LANES)

    def make_scale():
        all_of(wall.at[pl.ds(0, owners - 1)], gr_sem).wait()
        for n in range(owners):
            for g in range(groups):
                turn = turn_by * min(g, 1)
                value = wall[n, g].astype(jnp.float32)
                at = slice(n * depth, (n + 1) * depth)
                wf[g * local + turn : (g + 1) * local, at, :] = value[: local - turn]
                if turn:
                    wf[g * local : g * local + turn, at, :] = value[local - turn :]
        for a in range(stations):
            for b0 in range(a // TILE * TILE, stations, TILE):
                b = max(a, b0)
                count = b0 + TILE - b
                product = wf[a][None] * wf[b : b + count]
                m = pair_order[a, b]
                acc[m : m + count] = jnp.sum(product.reshape(count, owners * depth // SUB, SUB, LANES), axis=1)
        count = acc_flat[pl.ds(0, pairs, stride=SUB), :]
        for b in range(1, SUB):
            count = count + acc_flat[pl.ds(b, pairs, stride=SUB), :]
        counts[...] = 1.0 / jnp.sqrt(jnp.maximum(count, 1.0))
        for off, same in kinds:
            pieces = []
            if off:
                x, y = off[0]
                n = len(off) * TILE * TILE
                pieces += [(real_row[x, y], pair_order[x, y], n), (imag_row[x, y], pair_order[x, y], n)]
            for x in same:
                if x == same[0]:
                    n = len(same) * TILE * (TILE + 1) // 2
                    pieces.append((real_row[x, x], pair_order[x, x], n))
                for i in range(TILE - 1):
                    pieces.append((imag_row[x + i, x + i + 1], pair_order[x + i, x + i + 1], TILE - 1 - i))
            for row, source, n in pieces:
                scale_ref[row : row + n, :] = counts[source : source + n, :]

    def station_of(target):
        return relative_here((target % wide // split + me) % groups * local + target // wide)

    def scatter_copy(p, shift, what, target, source):
        if what == "last":
            src, dst = zs_b.at[p, target], rb.at[p, source, units - 1]
        elif what == "early":
            src, dst = zs_a.at[p, target], rb.at[p, source, pl.ds(0, units - 1)]
        else:
            late = (station_of(target) + TILE) % stations * split + target % split
            src, dst = zs_c.at[p, late], rb.at[p, source, pl.ds(0, units - 1)]
        return pltpu.make_async_remote_copy(
            src_ref=src, dst_ref=dst, send_sem=rs_sem,
            recv_sem=rr_sem.at[p], device_id={"tm": lax.rem(t + shift, owners)}, device_id_type=MESH,
        )

    def is_late(target):
        return station_of(target) >= stations - TILE

    def final_copy(p, w, source, piece):
        return pltpu.make_async_remote_copy(
            src_ref=fs.at[w, p], dst_ref=fr.at[source * split + piece, p], send_sem=fs_sem,
            recv_sem=fr_sem.at[p // (mine - 1) if mine > 1 else 1], device_id={"stn": plane, "tm": home * wide + w}, device_id_type=MESH,
        )

    def reduce_period(p):
        all_of(rb.at[p, pl.ds(0, owners - 1)], rr_sem.at[p]).wait()
        late = jnp.where(is_late(t), 1.0, 0.0)
        first = zs_a[p, t].astype(jnp.float32)
        first += late * zs_c[p, (mine_a % TILE) * split + part].astype(jnp.float32)
        last = zs_b[p, t].astype(jnp.float32)
        for shift in range(1, owners):
            source = lax.rem(t + owners - shift, owners)
            first += rb[p, source, : units - 1].astype(jnp.float32)
            last += rb[p, source, units - 1].astype(jnp.float32)
        red[: units - 1] = first
        red[units - 1] = last
        for w in range(wide):
            for n in range(own_rows):
                b = relative_here(partner_ref[w * own_rows + n])
                if split > 1:
                    keep = jnp.where(b // span == part, 1.0, 0.0)
                    b = b % span
                for ri in range(2):
                    row = red[b // TILE, pl.ds(ri * TILE + b % TILE, 1), :]
                    fs[w, p, ri, n : n + 1, :] = row * keep if split > 1 else row
        for w in range(wide):
            @pl.when((plane == me) & (w == place))
            def _():
                fr[me * split + part, p] = fs[w, p]

    def start_final(p):
        for w in range(wide):
            @pl.when(jnp.logical_not((plane == me) & (w == place)))
            def _():
                final_copy(p, w, me, part).start()

    half = TILE // 2

    def products(i, late):
        p = i // QUARTERS
        quarter = i % QUARTERS
        at = pl.ds(pl.multiple_of(p * blocks + quarter * SUB, SUB), SUB)
        first_station = stations - TILE if late else 0
        off, same = kinds[late]

        def wait_spectra(low, high):
            piece = xall.at[pl.ds(low, high - low), p, :, band(i), :]
            all_of(piece, xr_sem.at[arrival(i, late)]).wait()

        if late:
            @pl.when(i >= steps - QUARTERS)
            def _():
                wait_spectra(stations - TILE, stations)
        else:
            @pl.when(i < steps - QUARTERS)
            def _():
                wait_spectra(local, stations)

            @pl.when(i >= steps - QUARTERS)
            def _():
                wait_spectra(local, stations - TILE)

            @pl.when((quarter == 1) & (p < mine - 1))
            def _():
                start_phases(p + 1)

        def rotate(n, _):
            for j in range(2):
                s = first_station + n * 2 + j
                for k in range(depth):
                    r = s * depth + k
                    tmp[j * depth + k] = xall[s, p, k, band(i), :].astype(jnp.float32)
                    real = tmp[j * depth + k, pl.ds(0, SUB, stride=2), :]
                    imag = tmp[j * depth + k, pl.ds(1, SUB, stride=2), :]
                    c = base_c[p % 2, r]
                    sn = base_s[p % 2, r]
                    w = wide_w[r, at, :]
                    new_real = (w * (real * c + imag * sn)).astype(jnp.bfloat16).astype(jnp.float32)
                    new_imag = (w * (imag * c - real * sn)).astype(jnp.bfloat16).astype(jnp.float32)
                    yr[quarter, k, s] = new_real
                    yi[quarter, k, s] = new_imag
                    ys[quarter, k, s] = new_real + new_imag
                    yd[quarter, k, s] = new_real - new_imag
                    pc = step_c[p, pl.ds(r, 1), :]
                    ps = step_s[p, pl.ds(r, 1), :]
                    base_c[p % 2, r] = c * pc - sn * ps
                    base_s[p % 2, r] = sn * pc + c * ps
            return 0

        lax.fori_loop(0, (TILE if late else stations - TILE) // 2, rotate, 0)

        for x, y0 in off:
            for y in (y0, y0 + half):
                for k in range(depth):
                    ar, ai, asum = (ref[quarter, k, x : x + TILE][:, None] for ref in (yr, yi, ys))
                    br, bi, bdiff = (ref[quarter, k, y : y + half][None] for ref in (yr, yi, yd))
                    first = ar * br if k == 0 else first + ar * br
                    second = ai * bi if k == 0 else second + ai * bi
                    third = asum * bdiff if k == 0 else third + asum * bdiff
                real = first + second
                imag = third - (first - second)
                for n in range(TILE):
                    m = real_row[x + n, y]
                    q = imag_row[x + n, y]
                    v_ref[quarter, m : m + half] = real[n]
                    v_ref[quarter, q : q + half] = imag[n]
        for x in same:
            for a in range(x, x + TILE):
                n = x + TILE - a
                for k in range(depth):
                    ar, ai = yr[quarter, k, a], yi[quarter, k, a]
                    term = ar * ar + ai * ai
                    auto = term if k == 0 else auto + term
                    if n > 1:
                        br, bi, bdiff = (ref[quarter, k, a + 1 : a + n] for ref in (yr, yi, yd))
                        asum = ys[quarter, k, a]
                        first = ar * br if k == 0 else first + ar * br
                        second = ai * bi if k == 0 else second + ai * bi
                        third = asum * bdiff if k == 0 else third + asum * bdiff
                m = real_row[a, a]
                v_ref[quarter, m] = auto
                if n > 1:
                    q = imag_row[a, a + 1]
                    v_ref[quarter, m + 1 : m + n] = first + second
                    v_ref[quarter, q : q + n - 1] = third - (first - second)

    def lag_sums(i, which):
        p = i // QUARTERS
        quarter = i % QUARTERS
        top, size = {"all": (0, rows), "early": (0, early), "late": (early, rows - early)}[which]
        here = slice(top, top + size)
        turned[here] = pltpu.roll(scale_ref[here], LANES - (p * blocks + quarter * SUB), 1)
        for b in range(SUB):
            v = v_flat[pl.ds(quarter * (rows * SUB) + top * SUB + b, size, stride=SUB), :] * turned[here, b : b + 1]
            vh[here, b * LANES : (b + 1) * LANES] = v.astype(jnp.bfloat16)
        values = dot(vh[here], wh[quarter]) + dot(vh[here], wl[quarter])

        @pl.when(quarter == 0)
        def _():
            z_ref[here] = values

        @pl.when(quarter > 0)
        def _():
            z_ref[here] += values

        @pl.when(quarter == QUARTERS - 1)
        def _():
            if which != "early":
                picked = dot(pick_b[...], z_ref[...].astype(jnp.bfloat16)).reshape(-1, 2 * TILE, LAGS)
                zs_b[p] = picked[:owners].astype(jnp.bfloat16)
                zs_c[p] = picked[owners:].reshape(zs_c.shape[1:]).astype(jnp.bfloat16)
            if which != "late":
                picked = dot(pick_a[...], z_ref[:early].astype(jnp.bfloat16))
                zs_a[p] = picked.reshape(zs_a.shape[1:]).astype(jnp.bfloat16)
            for shift in range(1, owners):
                target = lax.rem(t + shift, owners)
                if which != "early":
                    scatter_copy(p, shift, "last", target, t).start()

                    @pl.when(is_late(target))
                    def _():
                        scatter_copy(p, shift, "late", target, t).start()

                if which != "late":
                    @pl.when(jnp.logical_not(is_late(target)))
                    def _():
                        scatter_copy(p, shift, "early", target, t).start()

        if which == "all" and mine > 2:
            @pl.when(((quarter == 1) & (p >= 2)) | ((quarter == 2) & (p == mine - 2)))
            def _():
                reduce_period(p - 3 + quarter)

        if which == "late" and mine > 1:
            @pl.when(quarter == QUARTERS - 1)
            def _():
                reduce_period(p - 1)

    normal = steps - QUARTERS
    ahead = 2 if normal else 0

    def step(m, _):
        stages = (normal + ahead) // ahead
        i = m - ahead * ((m // ahead + stages - 1) // stages)

        @pl.when((m < ahead) | (m >= 2 * ahead))
        def _():
            products(i, False)
            products(i, True)

        pl.when(m == ahead)(make_scale)

        @pl.when(m >= ahead)
        def _():
            lag_sums(i, "all")

        return 0

    def last_step(n, _):
        i = normal + n % QUARTERS
        for late in (False, True):

            @pl.when(n // QUARTERS == int(late))
            def _():
                products(i, late)
                lag_sums(i, "late" if late else "early")

        return 0

    start_phases(0)
    own_copy.wait()
    if normal:
        lax.fori_loop(0, normal + ahead, step, 0)
    else:
        make_scale()
    lax.fori_loop(0, 2 * QUARTERS, last_step, 0)
    for p in range(mine - 1):
        start_final(p)
    for shift in range(1, groups):
        for copy in small_copies(shift):
            copy.wait_send()
    all_of(wall.at[pl.ds(0, owners - 1)], gs_sem).wait()
    reduce_period(mine - 1)
    start_final(mine - 1)
    all_of(xall.at[pl.ds(local, stations - local)], xs_sem).wait()
    all_of(rb.at[:, pl.ds(0, owners - 1)], rs_sem).wait()

    flip = (
        lax.broadcasted_iota(jnp.int32, (lags, lags), 0) + lax.broadcasted_iota(jnp.int32, (lags, lags), 1) == lags - 1
    ).astype(jnp.bfloat16)
    factor = 1.0 / math.sqrt(periods * blocks * LANES)

    def wait_final(which, count):
        @pl.when(plane == me)
        def _():
            all_of(fr.at[pl.ds(0, wide - 1), pl.ds(0, count)], fr_sem.at[which]).wait()

        @pl.when(plane != me)
        def _():
            all_of(fr.at[:, pl.ds(0, count)], fr_sem.at[which]).wait()

    def transform(first, last):
        values, low = [], []
        for g in range(groups):
            for p in range(first, last):
                value = fr[g * split, p]
                for h in range(1, split):
                    value = value + fr[g * split + h, p]
                rc, rs = value[0, :, :lags], value[0, :, lags:]
                ic, im_s = value[1, :, :lags], value[1, :, lags:]
                values.append((g * mine + p, rc + im_s, ic - rs))
                low += [rc - im_s, ic + rs]
        low = jnp.concatenate(low, axis=0) if len(low) > 1 else low[0]
        high = low.astype(jnp.bfloat16)
        rest = low - high.astype(jnp.float32)
        middle = rest.astype(jnp.bfloat16)
        rest = (rest - middle.astype(jnp.float32)).astype(jnp.bfloat16)
        low = dot(high, flip) + dot(middle, flip) + dot(rest, flip)
        sums = []
        for r in range(periods):
            parts = []
            for side in range(2):
                real = imag = None
                for n, (p, re, im) in enumerate(values):
                    if side == 0:
                        re = low[2 * n * own_rows : (2 * n + 1) * own_rows]
                        im = low[(2 * n + 1) * own_rows : (2 * n + 2) * own_rows]
                    c = math.cos(2.0 * math.pi * (p * r % periods) / periods) * factor
                    s = math.sin(2.0 * math.pi * (p * r % periods) / periods) * factor
                    if abs(c) < 1e-9 * factor:
                        new_re, new_im = s * im, -s * re
                    elif abs(s) < 1e-9 * factor:
                        new_re, new_im = c * re, c * im
                    else:
                        new_re, new_im = c * re + s * im, c * im - s * re
                    real = new_re if real is None else real + new_re
                    imag = new_im if imag is None else imag + new_im
                parts.append((real, imag))
            sums.append(parts)
        return sums

    if mine > 1:
        wait_final(0, mine - 1)
        for r, parts in enumerate(transform(0, mine - 1)):
            for side, (real, imag) in enumerate(parts):
                cols = slice(side * lags, (side + 1) * lags)
                gf[0, r, :, cols] = real
                gf[1, r, :, cols] = imag
    wait_final(1, 1)
    for r, parts in enumerate(transform(mine - 1, mine)):
        for side, pair in enumerate(parts):
            cols = slice(side * lags, (side + 1) * lags)
            for n, value in enumerate(pair):
                if mine > 1:
                    value = value + gf[n, r, :, cols]
                out_ref[n, pl.ds(side * periods + r, own_rows, stride=2 * periods), :] = value

    @pl.when(plane == me)
    def _():
        all_of(fs.at[pl.ds(0, wide - 1)], fs_sem).wait()

    @pl.when(plane != me)
    def _():
        all_of(fs, fs_sem).wait()


def per_device(spectra, flags, poly_index, delay_model, partner_order):
    local, periods, depth, _, channels = spectra.shape
    groups = lax.axis_size("stn")
    owners = lax.axis_size("tm")
    stations = local * groups
    mine = periods // groups
    blocks = flags.shape[-1]
    split = owners // stations
    wide = groups * split
    own_rows = stations // wide
    span = stations // split
    rows = stations * stations
    pairs = stations * (stations + 1) // 2
    steps = mine * QUARTERS
    width = channels // QUARTERS
    lanes = LANES
    assert channels == blocks * LANES and width == SUB * LANES and stations % TILE == 0 and mine * blocks <= lanes and local * mine <= lanes

    x = spectra.reshape(local, periods, depth, 2, blocks, LANES).transpose(0, 1, 2, 4, 3, 5)
    x = x.reshape(local, periods, depth, 2 * blocks, LANES)
    high, low = lag_tables(channels)
    pick_a, pick_b = pick_matrices(stations, groups, owners)
    units = span // TILE
    runs = arrivals(stations, groups)
    hbm = pl.BlockSpec(memory_space=pltpu.HBM)
    f32, bf16, i32 = jnp.float32, jnp.bfloat16, jnp.int32
    spectra_rows = stations * depth
    dma = pltpu.SemaphoreType.DMA
    out = pl.pallas_call(
        functools.partial(kernel, (groups, owners, stations, periods, depth, blocks)),
        out_shape=jax.ShapeDtypeStruct((2, own_rows * 2 * periods, LAGS // 2), f32),
        in_specs=[hbm] * 9,
        out_specs=pl.BlockSpec(memory_space=pltpu.VMEM),
        scratch_shapes=[
            pltpu.VMEM((stations, mine, depth, 2 * blocks, LANES), bf16),
            pltpu.VMEM(flags.shape, i32),
            pltpu.VMEM((local, depth, periods), i32),
            pltpu.SMEM(delay_model.shape[::-1], f32),
            pltpu.SMEM(partner_order.shape, i32),
            pltpu.VMEM((groups, local, depth, lanes), bf16),
            pltpu.VMEM((groups, depth, LANES), f32),
            pltpu.VMEM((groups, local, depth, lanes), bf16),
            pltpu.VMEM((groups, depth, LANES), f32),
            pltpu.VMEM((owners, groups, local, depth, lanes), bf16),
            pltpu.VMEM((stations, owners * depth, lanes), f32),
            pltpu.VMEM((spectra_rows, lanes), f32),
            pltpu.VMEM((pairs, SUB, lanes), f32),
            pltpu.VMEM((pairs, lanes), f32),
            pltpu.VMEM((rows, lanes), f32),
            pltpu.VMEM((rows, lanes), f32),
            pltpu.VMEM((spectra_rows, lanes, LANES), f32),
            pltpu.VMEM((mine, spectra_rows, LANES), f32),
            pltpu.VMEM((mine, spectra_rows, LANES), f32),
            pltpu.VMEM((mine, spectra_rows, LANES), f32),
            pltpu.VMEM((2, spectra_rows, SUB, LANES), f32),
            pltpu.VMEM((2, spectra_rows, SUB, LANES), f32),
            pltpu.VMEM(high.shape, bf16),
            pltpu.VMEM(low.shape, bf16),
            pltpu.VMEM(pick_a.shape[1:], bf16),
            pltpu.VMEM(pick_b.shape[1:], bf16),
            pltpu.VMEM((QUARTERS,) + high.shape, bf16),
            pltpu.VMEM((QUARTERS,) + low.shape, bf16),
            pltpu.VMEM((2 * depth, 2 * SUB, LANES), f32),
            pltpu.VMEM((QUARTERS, depth, stations, SUB, LANES), f32),
            pltpu.VMEM((QUARTERS, depth, stations, SUB, LANES), f32),
            pltpu.VMEM((QUARTERS, depth, stations, SUB, LANES), f32),
            pltpu.VMEM((QUARTERS, depth, stations, SUB, LANES), f32),
            pltpu.VMEM((QUARTERS, rows, SUB, LANES), f32),
            pltpu.VMEM((rows, width), bf16),
            pltpu.VMEM((rows, LAGS), f32),
            pltpu.VMEM((mine, owners, units - 1, 2 * TILE, LAGS), bf16),
            pltpu.VMEM((mine, owners, 2 * TILE, LAGS), bf16),
            pltpu.VMEM((mine, TILE * split, units - 1, 2 * TILE, LAGS), bf16),
            pltpu.VMEM((mine, owners, units, 2 * TILE, LAGS), bf16),
            pltpu.VMEM((units, 2 * TILE, LAGS), f32),
            pltpu.VMEM((wide, mine, 2, own_rows, LAGS), f32),
            pltpu.VMEM((wide, mine, 2, own_rows, LAGS), f32),
            pltpu.VMEM((2, periods, own_rows, LAGS), f32),
            dma((8,)),
            dma,
            dma,
            dma((steps + QUARTERS,)),
            dma((2, groups - 1)),
            dma((2, groups - 1)),
            dma,
            dma,
            dma,
            dma((mine,)),
            dma,
            dma((2,)),
            pltpu.SemaphoreType.REGULAR,
            pltpu.SemaphoreType.REGULAR,
        ],
        compiler_params=pltpu.CompilerParams(collective_id=0, has_side_effects=True, vmem_limit_bytes=40 << 20),
        name="correlate",
    )(*(
        pltpu.with_memory_space_constraint(value, pltpu.HBM)
        for value in (
            x, flags, poly_index.transpose(0, 2, 1), delay_model.T, partner_order,
            jnp.asarray(high), jnp.asarray(low), jnp.asarray(pick_a), jnp.asarray(pick_b),
        )
    ))
    out = out.reshape(2, own_rows, 2, periods, LAGS // 2).transpose(0, 1, 3, 2, 4)
    return out.reshape(2, own_rows, periods, LAGS)


def solution(mesh):
    return jax.shard_map(
        per_device,
        mesh=mesh,
        in_specs=(
            P("stn", None, "tm", None, None),
            P("stn", None, "tm", None),
            P("stn", None, "tm"),
            P(),
            P(),
        ),
        out_specs=P(None, ("stn", "tm"), None, None),
        check_vma=False,
    )
```
